256 devices in a mesh: gx: 8 (over z_lo, core), gy: 4 (over x), sa: 8 (over z_hi, y).
Axes of the slice: x: 4, y: 4, z: 8 (z_hi: 2, z_lo: 4; z = z_hi * 4 + z_lo), core: 2. Of those that a mesh axis runs over, the one named last changes fastest.
Arguments:
- field_now: float32 [160, 256, 1024], P('sa', 'gy', 'gx'), may hold values from -1.5 to 1.5
- field_before: float32 [160, 256, 1024], P('sa', 'gy', 'gx'), may hold values from -1.5 to 1.5
- source: float32 [160, 256, 1024], P('sa', 'gy', 'gx'), may hold values from -0.06 to 0.06
- log_fields: float32 [9, 256, 1024], P(None, ('gy', 'sa'), 'gx'), may hold values from -0.15 to 0.15
- weights: float32 [1500], replicated, may hold values from 0.0002 to 0.002
- mean_perm: float32 [], replicated, may hold values from 0.5 to 2
- node_index: int32 [1500, 8], replicated, may hold values from 0 to 6
- mode_index: int32 [160, 8], replicated, may hold values from 0 to 3, as said below
Outputs:
- fresh: float32 [160, 256, 1024], P('sa', 'gy', 'gx')
- update: float32 [160, 256, 1024], P('sa', 'gy', 'gx')
The draws below stay inside these ranges and needn't reach their ends.
Inputs may be any that keep to these rules, and one draw needn't show every extreme that they name: `node_index`: each entry numbers a point of the list in the first step. `mode_index`: the rows are distinct multi-indices of total degree at most 3.
All inputs are finite; a program needn't handle non-finite values.
Results may differ from the reference program's by a relative error of at most 0.0003.
Values sent between devices are 32-bit elements; how exact they have to be, the bound alone decides.
No kernel may reach another device: no remote copies, remote signals or barrier semaphores. Data moves between devices by JAX's collectives and lax.ppermute only.
A program may use at most 64 MiB of HBM per device.

```python
import math
import jax
import jax.numpy as jnp
import numpy as np
from jax import lax

G = 8
P_SIZE = 160
Q = 1500
NX = 1024
NY = 256


def multi_indices(germ_count, highest):
    listed = [[]]
    for column in range(germ_count):
        listed = [record + [degree] for record in listed for degree in range(highest + 1) if sum(record) + degree <= highest]
    return np.array(listed, dtype=np.int32)


def draw_mode_index(key, part):
    table = jnp.asarray(multi_indices(G, 3))
    shuffled = jax.random.permutation(jax.random.fold_in(key, 17), table.shape[0])
    return table[shuffled[:P_SIZE]]


def plant(result, rng, least, largest):
    longest = result.shape.index(max(result.shape))
    spots = []
    for shift in (0, 1):
        where = [jax.random.randint(jax.random.fold_in(rng, axis), (), 0, length) for axis, length in enumerate(result.shape)]
        where[longest] = (where[longest] + shift) % result.shape[longest]
        spots.append(tuple(where))
    return result.at[spots[0]].set(least).at[spots[1]].set(largest)


def level_of(rng, extent, cuts, low, top_value):
    gain = 1.0
    for position, parts in cuts:
        heights = jax.random.uniform(jax.random.fold_in(jax.random.fold_in(rng, 6), position), (parts,), jnp.float32, low / len(cuts), top_value / len(cuts))
        gain = gain * jnp.repeat(jnp.exp(heights), extent[position] // parts).reshape((-1,) + (1,) * (len(extent) - 1 - position))
    return gain


def scatter_about(key, extent, spread, reach, split=(), kind=jnp.bfloat16):
    values = jax.random.normal(key, extent, jnp.float32) * spread
    if len(split) > 0:
        values = level_of(key, extent, split, -0.22, 0.18) * values
    return jnp.clip(values, min=-reach, max=reach).astype(kind)


def setup_inputs(seed: int = 0) -> dict:
    streams_of = jax.random.split(jax.random.key(seed), 9)
    field_now = scatter_about(streams_of[0], (P_SIZE, NY, NX), 0.1, 1.5, ((0, 8), (1, 4), (2, 8)), jnp.float32)
    field_before = scatter_about(streams_of[1], (P_SIZE, NY, NX), 0.1, 1.5, ((0, 8), (1, 4), (2, 8)), jnp.float32)
    source = scatter_about(streams_of[2], (P_SIZE, NY, NX), 0.01, 0.06, ((0, 8), (1, 4), (2, 8)), jnp.float32)
    log_fields = jnp.clip(jax.random.uniform(streams_of[3], (G + 1, NY, NX), jnp.float32, -0.15, 0.15) * level_of(streams_of[3], (G + 1, NY, NX), ((1, 32), (2, 8)), -0.4, 0.0), -0.15, 0.15)
    weights = jnp.clip(jnp.exp(jax.random.uniform(streams_of[4], (Q,), jnp.float32, math.log(0.0002), math.log(0.002))), 0.0002, 0.002)
    mean_perm = jnp.clip(jnp.exp(jax.random.uniform(streams_of[5], (), jnp.float32, math.log(0.5), math.log(2.0))), 0.5, 2.0)
    node_index = plant(jax.random.randint(streams_of[6], (Q, G), 0, 7), jax.random.fold_in(streams_of[6], 1), 0, 6).astype(jnp.int32)
    mode_index = draw_mode_index(jax.random.fold_in(streams_of[8], 71), 0)
    return {"field_now": field_now, "field_before": field_before, "source": source, "log_fields": log_fields, "weights": weights, "mean_perm": mean_perm, "node_index": node_index, "mode_index": mode_index}


HIGHEST = lax.Precision.HIGHEST
hermite_points = (0.0, -1.7320508075688772, 1.7320508075688772, -1.355626179974266, 1.355626179974266, -2.8569700138728056, 2.8569700138728056)
storage_rate = 0.0004
relax_weight = 1.6
step_length = 0.3

def node_germs(node_index):
    levels = jnp.arange(len(hermite_points), dtype=jnp.int32)
    picked = (node_index[:, :, None] == levels).astype(jnp.float32)
    points = jnp.asarray(hermite_points, dtype=jnp.float32)
    return lax.optimization_barrier(jnp.sum(picked * points, axis=2))

def chaos_basis(node_index, mode_index):
    germ_values = node_germs(node_index)
    square = germ_values * germ_values
    hermite = jnp.stack([jnp.ones_like(germ_values), germ_values, (square - 1.0) / math.sqrt(2.0), (square * germ_values - 3.0 * germ_values) / math.sqrt(6.0)], axis=2)
    degrees = jnp.arange(4, dtype=jnp.int32)
    values = jnp.ones((node_index.shape[0], mode_index.shape[0]), jnp.float32)
    for column in range(mode_index.shape[1]):
        select = (mode_index[:, column][:, None] == degrees).astype(jnp.float32)
        values = values * jnp.dot(hermite[:, column, :], select.T, precision=HIGHEST)
    return (germ_values, values)

def with_mean(germ_values):
    return jnp.concatenate([jnp.ones((germ_values.shape[0], 1), germ_values.dtype), germ_values], axis=1)

def harmonic(later, earlier):
    return 2.0 * later * earlier / (later + earlier)

def apply_operator(values, log_perm):
    conduct = jnp.exp(log_perm)
    across = harmonic(conduct[:, :, 1:], conduct[:, :, :-1]) * (values[:, :, 1:] - values[:, :, :-1])
    along = harmonic(conduct[:, 1:, :], conduct[:, :-1, :]) * (values[:, 1:, :] - values[:, :-1, :])
    across_div = jnp.pad(across, ((0, 0), (0, 0), (0, 1))) - jnp.pad(across, ((0, 0), (0, 0), (1, 0)))
    along_div = jnp.pad(along, ((0, 0), (0, 1), (0, 0))) - jnp.pad(along, ((0, 0), (1, 0), (0, 0)))
    return storage_rate * values - across_div - along_div

def cosine_matrix(length):
    freq = jnp.arange(length, dtype=jnp.int32)[:, None]
    cells = jnp.arange(length, dtype=jnp.int32)[None, :]
    phase = freq * (2 * cells + 1) % (4 * length)
    angle = phase.astype(jnp.float32) * (math.pi / (2 * length))
    factor = jnp.where(freq == 0, math.sqrt(1.0 / length), math.sqrt(2.0 / length))
    return factor * jnp.cos(angle)

def eigen_values(first, count, length):
    freq = (first + jnp.arange(count, dtype=jnp.int32)).astype(jnp.float32)
    return 2.0 - 2.0 * jnp.cos(freq * (math.pi / length))

def reference(field_now, field_before, source, log_fields, weights, mean_perm, node_index, mode_index):
    germ_values, basis = chaos_basis(node_index, mode_index)
    germ_full = with_mean(germ_values)
    node_block = math.gcd(Q, 50)
    blocks = Q // node_block
    node_items = (basis.reshape(blocks, node_block, P_SIZE), germ_full.reshape(blocks, node_block, G + 1), weights.reshape(blocks, node_block))

    def accumulate(running, node_item):
        basis_part, germ_part, weight_part = node_item
        values = jnp.einsum('qp,pyx->qyx', basis_part, field_now, precision=HIGHEST)
        log_perm = jnp.einsum('qg,gyx->qyx', germ_part, log_fields, precision=HIGHEST)
        applied = apply_operator(values, log_perm)
        running = running + jnp.einsum('qp,qyx->pyx', basis_part * weight_part[:, None], applied, precision=HIGHEST)
        return (running, None)
    galerkin, unused = lax.scan(accumulate, jnp.zeros(field_now.shape, jnp.float32), node_items)
    residual = source - galerkin
    rows_matrix = cosine_matrix(NY)
    cols_matrix = cosine_matrix(NX)
    spectral = jnp.einsum('jy,pyx->pjx', rows_matrix, residual, precision=HIGHEST)
    spectral = jnp.einsum('pjx,kx->pjk', spectral, cols_matrix, precision=HIGHEST)
    spectral = spectral / (storage_rate + mean_perm * (eigen_values(0, NY, NY)[:, None] + eigen_values(0, NX, NX)[None, :]))
    spectral = jnp.einsum('pjk,kx->pjx', spectral, cols_matrix, precision=HIGHEST)
    update = jnp.einsum('jy,pjx->pyx', rows_matrix, spectral, precision=HIGHEST)
    fresh = field_before + relax_weight * (field_now - field_before + step_length * update)
    return (fresh, update)
```

```python
import functools
import math

import jax
import jax.numpy as jnp
import numpy as np
from jax import lax
from jax.experimental import pallas as pl
from jax.experimental.pallas import tpu as pltpu
from jax.sharding import PartitionSpec as P

HIGHEST = lax.Precision.HIGHEST
hermite_points = (
    0.0,
    -1.7320508075688772,
    1.7320508075688772,
    -1.355626179974266,
    1.355626179974266,
    -2.8569700138728056,
    2.8569700138728056,
)
storage_rate = 0.0004
relax_weight = 1.6
step_length = 0.3
QB = 256
LANES = 128


def halves(x):
    top = lax.reduce_precision(x, 8, 7)
    return top.astype(jnp.bfloat16), (x - top).astype(jnp.bfloat16)


def split(x):
    top = x.astype(jnp.bfloat16)
    return top, (x - top.astype(jnp.float32)).astype(jnp.bfloat16)


def cosine_matrix(length):
    k = np.arange(length)[:, None]
    m = np.arange(length)[None, :]
    phase = (k * (2 * m + 1)) % (4 * length)
    factor = np.where(k == 0, math.sqrt(1.0 / length), math.sqrt(2.0 / length))
    return factor * np.cos(phase * (math.pi / (2 * length)))


def eigen_values(count, length):
    return 4.0 * np.sin(np.arange(count) * (math.pi / (2 * length))) ** 2


def node_tables(node_index, mode_index, weights):
    q = node_index.shape[0]
    pad = -q % QB
    index = jnp.pad(node_index.T, ((0, 0), (0, pad)))
    germ = jnp.zeros(index.shape, jnp.float32)
    for level, point in enumerate(hermite_points):
        germ = jnp.where(index == level, jnp.float32(point), germ)
    square = germ * germ
    h2 = (square - 1.0) / math.sqrt(2.0)
    h3 = (square * germ - 3.0 * germ) / math.sqrt(6.0)
    basis = None
    for i in range(germ.shape[0]):
        degree = mode_index[:, i][:, None]
        factor = jnp.where(
            degree == 0,
            1.0,
            jnp.where(degree == 1, germ[i][None], jnp.where(degree == 2, h2[i][None], h3[i][None])),
        )
        basis = factor if basis is None else basis * factor
    weighted = basis * jnp.pad(weights, (0, pad))[None]
    mass = lax.dot_general(
        storage_rate * weighted, basis, (((1,), (1,)), ((), ())), precision=HIGHEST
    )
    b_top, b_low = halves(basis.T)
    basis_cat = jnp.concatenate([b_top, b_top, b_low], axis=1)
    weight_cat = jnp.concatenate(halves(2.0 * weighted), axis=0)
    germ_full = jnp.concatenate([jnp.ones((1, q + pad), jnp.float32), germ], axis=0)
    g_top, g_low = halves(germ_full)
    germ_cat = jnp.concatenate([g_top, g_top, g_low], axis=0)
    germ_cat = jnp.pad(germ_cat, ((0, 32 - germ_cat.shape[0]), (0, 0))).T
    return basis_cat, weight_cat, germ_cat, mass


def log_cat(logs):
    top, low = halves(logs * jnp.float32(-math.log2(math.e)))
    cat = jnp.concatenate([top, low, top], axis=0)
    return jnp.pad(cat, ((0, 32 - cat.shape[0]), (0, 0)))


def put_cat(du_ref, lanes, diff):
    p = diff.shape[0]
    top, low = split(diff)
    du_ref[0:p, lanes] = top
    du_ref[p : 2 * p, lanes] = low
    du_ref[2 * p : 3 * p, lanes] = top


def add_flux(f_ref, lanes, w_ref, flux):
    p = f_ref.shape[0]
    top, low = split(flux)
    both = jnp.dot(w_ref[...], top, preferred_element_type=jnp.float32)
    rest = jnp.dot(w_ref[0:p, :], low, preferred_element_type=jnp.float32)
    f_ref[:, lanes] += both[0:p] + both[p : 2 * p] + rest


def inner_kernel(rows, u_ref, log_ref, basis_ref, germ_ref, w_ref, mass_ref, g_ref, du_ref, r_ref, f_ref):
    p = mass_ref.shape[0]
    cols = LANES
    step = pl.program_id(0)

    @pl.when(step == 0)
    def _():
        lane = lax.broadcasted_iota(jnp.int32, (p, cols), 1)
        above = None
        for y in range(rows):
            here = u_ref[pl.ds(y, p, stride=rows), :]
            ahead = pltpu.roll(here, cols - 1, axis=1)
            put_cat(du_ref, pl.ds(y * cols, cols), jnp.where(lane == cols - 1, 0.0, ahead - here))
            if y > 0:
                put_cat(du_ref, pl.ds((rows + y - 1) * cols, cols), here - above)
            above = here
        f_ref[...] = jnp.zeros_like(f_ref)

    r_ref[...] = jnp.exp2(
        jnp.dot(germ_ref[...], log_ref[...], preferred_element_type=jnp.float32)
    )

    def values(lanes):
        return jnp.dot(basis_ref[...], du_ref[:, lanes], preferred_element_type=jnp.float32)

    for y in range(0, rows, 2):
        lanes = pl.ds(y * cols, 2 * cols)
        sums = []
        for k in range(2):
            r = r_ref[:, pl.ds((y + k) * cols, cols)]
            sums.append(r + pltpu.roll(r, cols - 1, axis=1))
        add_flux(f_ref, lanes, w_ref, values(lanes) / jnp.concatenate(sums, axis=1))
    for y in range(0, rows - 1, 2):
        n = min(2, rows - 1 - y)
        lanes = pl.ds((rows + y) * cols, n * cols)
        total = r_ref[:, pl.ds(y * cols, n * cols)] + r_ref[:, pl.ds((y + 1) * cols, n * cols)]
        add_flux(f_ref, lanes, w_ref, values(lanes) / total)

    @pl.when(step == pl.num_programs(0) - 1)
    def _():
        lane = lax.broadcasted_iota(jnp.int32, (p, cols), 1)
        for y in range(rows):
            out = jnp.dot(
                mass_ref[...],
                u_ref[pl.ds(y, p, stride=rows), :],
                precision=HIGHEST,
                preferred_element_type=jnp.float32,
            )
            later = f_ref[:, pl.ds(y * cols, cols)]
            earlier = jnp.where(lane == 0, 0.0, pltpu.roll(later, 1, axis=1))
            later = jnp.where(lane == cols - 1, 0.0, later)
            out = out - (later - earlier)
            if y < rows - 1:
                out = out - f_ref[:, pl.ds((rows + y) * cols, cols)]
            if y > 0:
                out = out + f_ref[:, pl.ds((rows + y - 1) * cols, cols)]
            g_ref[y] = out


def whole(shape):
    return pl.BlockSpec(shape, lambda *_: (0,) * len(shape))


def inner_fluxes(field, logs, basis_cat, weight_cat, germ_cat, mass):
    p, rows, cols = field.shape
    q = basis_cat.shape[0]
    faces = (2 * rows - 1) * cols
    return pl.pallas_call(
        functools.partial(inner_kernel, rows),
        grid=(q // QB,),
        in_specs=[
            whole((p * rows, cols)),
            whole(logs.shape),
            pl.BlockSpec((QB, basis_cat.shape[1]), lambda i: (i, 0)),
            pl.BlockSpec((QB, germ_cat.shape[1]), lambda i: (i, 0)),
            pl.BlockSpec((2 * p, QB), lambda i: (0, i)),
            whole((p, p)),
        ],
        out_specs=whole((rows, p, cols)),
        out_shape=jax.ShapeDtypeStruct((rows, p, cols), jnp.float32),
        scratch_shapes=[
            pltpu.VMEM((3 * p, faces), jnp.bfloat16),
            pltpu.VMEM((QB, rows * cols), jnp.float32),
            pltpu.VMEM((p, faces), jnp.float32),
        ],
        compiler_params=pltpu.CompilerParams(vmem_limit_bytes=40 << 20),
        cost_estimate=pl.CostEstimate(
            flops=2 * q * faces * p * 6, bytes_accessed=8 << 20, transcendentals=q * rows * cols
        ),
        name="inner_fluxes",
    )(field.reshape(p * rows, cols), logs, basis_cat, germ_cat, weight_cat, mass)


def rim_kernel(
    rows, open_ref, g_ref, u_ref, up_ref, down_ref, side_ref, le_ref, ll_ref, basis_ref, germ_ref,
    w_ref, out_ref, du_ref, f_ref,
):
    p = up_ref.shape[0]
    cols = LANES
    step = pl.program_id(0)

    @pl.when(step == 0)
    def _():
        lane = lax.broadcasted_iota(jnp.int32, (p, cols), 1)
        first = u_ref[pl.ds(0, p, stride=rows), :]
        last = u_ref[pl.ds(rows - 1, p, stride=rows), :]
        put_cat(du_ref, pl.ds(0, cols), (first - up_ref[...]) * open_ref[0])
        put_cat(du_ref, pl.ds(cols, cols), (down_ref[...] - last) * open_ref[1])
        near = jnp.zeros((p, cols), jnp.float32)
        for y in range(rows):
            here = u_ref[pl.ds(y, p, stride=rows), :]
            near = jnp.where(lane == y, here[:, 0:1], near)
            near = jnp.where(lane == rows + y, here[:, cols - 1 : cols], near)
        side = side_ref[...]
        diff = jnp.where(lane < rows, (near - side) * open_ref[2], (side - near) * open_ref[3])
        put_cat(du_ref, pl.ds(2 * cols, cols), jnp.where(lane < 2 * rows, diff, 0.0))
        f_ref[...] = jnp.zeros_like(f_ref)

    earlier = jnp.exp2(jnp.dot(germ_ref[...], le_ref[...], preferred_element_type=jnp.float32))
    later = jnp.exp2(jnp.dot(germ_ref[...], ll_ref[...], preferred_element_type=jnp.float32))
    values = jnp.dot(basis_ref[...], du_ref[...], preferred_element_type=jnp.float32)
    add_flux(f_ref, pl.ds(0, 3 * cols), w_ref, values / (earlier + later))

    @pl.when(step == pl.num_programs(0) - 1)
    def _():
        lane = lax.broadcasted_iota(jnp.int32, (p, cols), 1)
        side = f_ref[:, pl.ds(2 * cols, cols)]
        for y in range(rows):
            out = g_ref[y]
            if y == 0:
                out = out + f_ref[:, pl.ds(0, cols)]
            if y == rows - 1:
                out = out - f_ref[:, pl.ds(cols, cols)]
            out = out + jnp.where(lane == 0, side[:, y : y + 1], 0.0)
            out = out - jnp.where(lane == cols - 1, side[:, rows + y : rows + y + 1], 0.0)
            out_ref[pl.ds(y, p, stride=rows), :] = out


def rim_fluxes(opened, inner, field, up, down, side, log_e, log_l, basis_cat, weight_cat, germ_cat):
    p, rows, cols = field.shape
    q = basis_cat.shape[0]
    return pl.pallas_call(
        functools.partial(rim_kernel, rows),
        grid=(q // QB,),
        in_specs=[
            pl.BlockSpec(memory_space=pltpu.SMEM),
            whole(inner.shape),
            whole((p * rows, cols)),
            whole((p, cols)),
            whole((p, cols)),
            whole((p, cols)),
            whole(log_e.shape),
            whole(log_l.shape),
            pl.BlockSpec((QB, basis_cat.shape[1]), lambda i: (i, 0)),
            pl.BlockSpec((QB, germ_cat.shape[1]), lambda i: (i, 0)),
            pl.BlockSpec((2 * p, QB), lambda i: (0, i)),
        ],
        out_specs=whole((p * rows, cols)),
        out_shape=jax.ShapeDtypeStruct((p * rows, cols), jnp.float32),
        scratch_shapes=[
            pltpu.VMEM((3 * p, 3 * cols), jnp.bfloat16),
            pltpu.VMEM((p, 3 * cols), jnp.float32),
        ],
        compiler_params=pltpu.CompilerParams(vmem_limit_bytes=40 << 20),
        cost_estimate=pl.CostEstimate(
            flops=2 * q * 3 * cols * p * 6, bytes_accessed=8 << 20, transcendentals=q * 6 * cols
        ),
        name="rim_fluxes",
    )(opened, inner, field.reshape(p * rows, cols), up, down, side, log_e, log_l, basis_cat, germ_cat, weight_cat)


def local_kernel(nsa, part_ref, src_ref, cy_ref, cx_ref, cxt_ref, ends_of_ref, recip_ref, z_ref, ends_ref):
    ngy, modes, length, cols = src_ref.shape
    rows = part_ref.shape[2]
    ends_ref[...] = jnp.zeros_like(ends_ref)
    for m in range(modes):
        tiles = []
        for g in range(ngy):
            for s in range(nsa):
                tiles.append(src_ref[g, m, s * rows : (s + 1) * rows, :] - part_ref[s * ngy + g, m])
        residual = jnp.concatenate(tiles, axis=0)
        spectral = jnp.dot(cy_ref[...], residual, precision=HIGHEST, preferred_element_type=jnp.float32)
        scaled = recip_ref[...] * jnp.dot(
            spectral, cxt_ref[...], precision=HIGHEST, preferred_element_type=jnp.float32
        )
        z_ref[m] = jnp.dot(scaled, cx_ref[...], precision=HIGHEST, preferred_element_type=jnp.float32)
        both = lax.dot_general(
            ends_of_ref[...], scaled, (((1,), (1,)), ((), ())),
            precision=HIGHEST, preferred_element_type=jnp.float32,
        )
        ends_ref[m : m + 1, :] = both[0:1]
        ends_ref[8 + m : 9 + m, :] = both[1:2]


def joined_kernel(z_ref, ends_ref, coef_ref, g_first_ref, g_last_ref, cyt_ref, out_ref):
    modes, ny, cols = z_ref.shape
    blocks = ends_ref.shape[0]
    ngy = out_ref.shape[0]
    length = ny // ngy
    jump = []
    for side in range(2):
        total = jnp.zeros((8, ny), jnp.float32)
        for i in range(blocks):
            total = total + coef_ref[side, 0, i : i + 1, :] * ends_ref[i, 0:8, :]
            total = total + coef_ref[side, 1, i : i + 1, :] * ends_ref[i, 8:16, :]
        jump.append(total)
    both = jnp.concatenate(jump + [jnp.zeros((LANES - 16, ny), jnp.float32)], axis=0).T
    for m in range(modes):
        x = (
            z_ref[m]
            + g_first_ref[...] * both[:, m : m + 1]
            - g_last_ref[...] * both[:, 8 + m : 9 + m]
        )
        out = jnp.dot(cyt_ref[...], x, precision=HIGHEST, preferred_element_type=jnp.float32)
        for g in range(ngy):
            out_ref[g, m] = out[g * length : (g + 1) * length]


def solve_tables(mean_perm, ny, cols, blocks, position):
    cx = cosine_matrix(cols)
    lam_y = jnp.asarray(eigen_values(ny, ny), jnp.float32)
    lam_x = jnp.asarray(eigen_values(cols, cols), jnp.float32)
    recip = 1.0 / (storage_rate + mean_perm * (lam_y[:, None] + lam_x[None, :]))
    first = jnp.asarray(cx[:, 0][:, None] * cx, jnp.float32)
    last = jnp.asarray(cx[:, -1][:, None] * cx, jnp.float32)
    g_first = jnp.dot(recip, first, precision=HIGHEST)
    g_last = jnp.dot(recip, last, precision=HIGHEST)
    k = np.arange(1, blocks)
    sine = math.sqrt(2.0 / blocks) * np.sin(np.pi * np.outer(np.arange(0, blocks + 1), k) / blocks)
    sine[0] = 0.0
    sine[blocks] = 0.0
    theta = jnp.asarray(2.0 * np.cos(np.pi * k / blocks), jnp.float32)
    spread = 1.0 / (
        1.0 / mean_perm + g_first[:, 0:1] + g_last[:, cols - 1 : cols] - g_first[:, cols - 1 : cols] * theta
    )
    table = jnp.asarray(sine, jnp.float32)
    coef = []
    for side in range(2):
        mine = lax.dynamic_slice_in_dim(table, position + side, 1, axis=0)
        inverse = jnp.einsum("ik,jk->ij", table, spread * mine, precision=HIGHEST)
        coef.append(jnp.stack([-inverse[:blocks], inverse[1:]]))
    return recip, g_first, g_last, jnp.stack(coef)


def shifted(last, leading, axis):
    count = lax.axis_size(axis)
    up = [(i, i + 1) for i in range(count - 1)]
    return lax.ppermute(last, axis, up), lax.ppermute(leading, axis, [(b, a) for a, b in up])


def on_device(
    field_now, field_before, source, log_fields, weights, mean_perm, node_index, mode_index
):
    nsa, ngy, ngx = (lax.axis_size(a) for a in ("sa", "gy", "gx"))
    modes, length, cols = field_now.shape
    rows = length // nsa
    p = modes * nsa
    ny = length * ngy
    sub = modes // ngy

    outgoing = field_now.reshape(modes, nsa, rows, cols).transpose(1, 0, 2, 3)
    field = lax.all_to_all(outgoing, "sa", 0, 0, tiled=True).reshape(p, rows, cols)
    src = lax.all_to_all(source.reshape(ngy, sub, length, cols), "gy", 0, 0, tiled=True)

    basis_cat, weight_cat, germ_cat, mass = node_tables(node_index, mode_index, weights)
    recip, g_first, g_last, coef = solve_tables(mean_perm, ny, cols, ngx, lax.axis_index("gx"))

    row_axis = ("gy", "sa")
    row_index = lax.axis_index(row_axis)
    col_index = lax.axis_index("gx")
    opened = jnp.stack(
        [row_index > 0, row_index < ngy * nsa - 1, col_index > 0, col_index < ngx - 1]
    ).astype(jnp.float32)
    log_up, log_down = shifted(log_fields[:, -1], log_fields[:, 0], row_axis)
    log_left, log_right = shifted(log_fields[:, :, -1], log_fields[:, :, 0], "gx")
    spare = jnp.zeros((log_fields.shape[0], LANES - 2 * rows), jnp.float32)
    log_e = log_cat(
        jnp.concatenate([log_up, log_fields[:, -1], log_left, log_fields[:, :, -1], spare], axis=1)
    )
    log_l = log_cat(
        jnp.concatenate([log_fields[:, 0], log_down, log_fields[:, :, 0], log_right, spare], axis=1)
    )
    logs = log_cat(log_fields.reshape(log_fields.shape[0], rows * cols))

    up, down = shifted(field[:, -1], field[:, 0], row_axis)
    left, right = shifted(field[:, :, -1], field[:, :, 0], "gx")
    side = jnp.concatenate([left, right, jnp.zeros((p, LANES - 2 * rows), jnp.float32)], axis=1)

    inner = inner_fluxes(field, logs, basis_cat, weight_cat, germ_cat, mass)
    galerkin = rim_fluxes(
        opened, inner, field, up, down, side, log_e, log_l, basis_cat, weight_cat, germ_cat
    )
    part = lax.all_to_all(
        galerkin.reshape(nsa * ngy, sub, rows, cols), ("sa", "gy"), 0, 0, tiled=True
    )

    cy = cosine_matrix(ny)
    cx = cosine_matrix(cols)
    ends_of = np.zeros((8, cols))
    ends_of[0], ends_of[1] = cx[:, 0], cx[:, -1]
    f32 = functools.partial(jnp.asarray, dtype=jnp.float32)
    params = pltpu.CompilerParams(vmem_limit_bytes=40 << 20)
    z, ends = pl.pallas_call(
        functools.partial(local_kernel, nsa),
        out_shape=(
            jax.ShapeDtypeStruct((sub, ny, cols), jnp.float32),
            jax.ShapeDtypeStruct((16, ny), jnp.float32),
        ),
        compiler_params=params,
        name="local_solve",
    )(part, src, f32(cy), f32(cx), f32(cx.T), f32(ends_of), recip)
    all_ends = lax.all_gather(ends, "gx", axis=0, tiled=False)
    columns = pl.pallas_call(
        joined_kernel,
        out_shape=jax.ShapeDtypeStruct((ngy, sub, length, cols), jnp.float32),
        compiler_params=params,
        name="joined_solve",
    )(z, all_ends, coef, g_first, g_last, f32(cy.T))
    update = lax.all_to_all(columns, "gy", 0, 0, tiled=True).reshape(modes, length, cols)
    fresh = field_before + relax_weight * (field_now - field_before + step_length * update)
    return (fresh, update)


def solution(mesh):
    block = P("sa", "gy", "gx")
    in_specs = (block, block, block, P(None, ("gy", "sa"), "gx"), P(), P(), P(), P())
    return jax.shard_map(
        on_device, mesh=mesh, in_specs=in_specs, out_specs=(block, block), check_vma=False
    )
```

```python
import functools
import math

import jax
import jax.numpy as jnp
import numpy as np
from jax import lax
from jax.experimental import pallas as pl
from jax.experimental.pallas import tpu as pltpu
from jax.sharding import PartitionSpec as P

HIGHEST = lax.Precision.HIGHEST
hermite_points = (
    0.0,
    -1.7320508075688772,
    1.7320508075688772,
    -1.355626179974266,
    1.355626179974266,
    -2.8569700138728056,
    2.8569700138728056,
)
storage_rate = 0.0004
relax_weight = 1.6
step_length = 0.3
QB = 256
LANES = 128


def halves(x):
    top = lax.reduce_precision(x, 8, 7)
    return top.astype(jnp.bfloat16), (x - top).astype(jnp.bfloat16)


def split(x):
    top = x.astype(jnp.bfloat16)
    return top, (x - top.astype(jnp.float32)).astype(jnp.bfloat16)


def cosine_matrix(length):
    k = np.arange(length)[:, None]
    m = np.arange(length)[None, :]
    phase = (k * (2 * m + 1)) % (4 * length)
    factor = np.where(k == 0, math.sqrt(1.0 / length), math.sqrt(2.0 / length))
    return factor * np.cos(phase * (math.pi / (2 * length)))


def eigen_values(count, length):
    return 4.0 * np.sin(np.arange(count) * (math.pi / (2 * length))) ** 2


SLOT = 16


def tables_kernel(index_ref, mode_ref, weight_ref, basis_ref, w_ref, germ_ref, mass_ref, sum_ref):
    germs, q = index_ref.shape
    p = mode_ref.shape[0]
    step = pl.program_id(0)
    index = index_ref[...]
    germ = jnp.zeros((germs, q), jnp.float32)
    for level, point in enumerate(hermite_points):
        germ = jnp.where(index == level, jnp.float32(point), germ)
    square = germ * germ
    h2 = (square - 1.0) / math.sqrt(2.0)
    h3 = (square * germ - 3.0 * germ) / math.sqrt(6.0)
    basis = jnp.ones((p, q), jnp.float32)
    for i in range(germs):
        degree = mode_ref[:, i : i + 1]
        factor = jnp.where(
            degree == 1,
            germ[i : i + 1],
            jnp.where(degree == 2, h2[i : i + 1], jnp.where(degree == 3, h3[i : i + 1], 1.0)),
        )
        basis = basis * factor
    weighted = basis * weight_ref[...]
    w_ref[0:p, :], w_ref[p : 2 * p, :] = split(2.0 * weighted)
    top, low = split(basis.T)
    basis_ref[:, 0:p] = top
    basis_ref[:, p : 2 * p] = top
    basis_ref[:, 2 * p : 3 * p] = low
    full = jnp.concatenate(
        [jnp.ones((8, q), jnp.float32), germ, jnp.zeros((LANES - 16, q), jnp.float32)], axis=0
    )
    top, low = split(full.T[:, 7 : 7 + SLOT])
    lane = lax.broadcasted_iota(jnp.int32, (q, SLOT), 1)
    keep = lane < germs + 1
    top = jnp.where(keep, top.astype(jnp.float32), 0.0).astype(jnp.bfloat16)
    low = jnp.where(keep, low.astype(jnp.float32), 0.0).astype(jnp.bfloat16)
    germ_ref[:, 0:SLOT] = top
    germ_ref[:, SLOT : 2 * SLOT] = top
    germ_ref[:, 2 * SLOT : 3 * SLOT] = low

    @pl.when(step == 0)
    def _():
        sum_ref[...] = jnp.zeros_like(sum_ref)

    sum_ref[...] += lax.dot_general(
        storage_rate * weighted, basis, (((1,), (1,)), ((), ())),
        precision=HIGHEST, preferred_element_type=jnp.float32,
    )

    @pl.when(step == pl.num_programs(0) - 1)
    def _():
        top, low = split(sum_ref[...])
        mass_ref[:, 0:p] = top
        mass_ref[:, p : 2 * p] = top
        mass_ref[:, 2 * p : 3 * p] = low


def node_tables(node_index, mode_index, weights):
    q, germs = node_index.shape
    p = mode_index.shape[0]
    pad = -q % QB
    index = jnp.pad(node_index.T, ((0, 0), (0, pad)))
    weights = jnp.pad(weights, (0, pad))[None]
    return pl.pallas_call(
        tables_kernel,
        grid=((q + pad) // QB,),
        in_specs=[
            pl.BlockSpec((germs, QB), lambda i: (0, i)),
            whole((p, germs)),
            pl.BlockSpec((1, QB), lambda i: (0, i)),
        ],
        out_specs=[
            pl.BlockSpec((QB, 3 * p), lambda i: (i, 0)),
            pl.BlockSpec((2 * p, QB), lambda i: (0, i)),
            pl.BlockSpec((QB, 3 * SLOT), lambda i: (i, 0)),
            whole((p, 3 * p)),
        ],
        out_shape=[
            jax.ShapeDtypeStruct((q + pad, 3 * p), jnp.bfloat16),
            jax.ShapeDtypeStruct((2 * p, q + pad), jnp.bfloat16),
            jax.ShapeDtypeStruct((q + pad, 3 * SLOT), jnp.bfloat16),
            jax.ShapeDtypeStruct((p, 3 * p), jnp.bfloat16),
        ],
        scratch_shapes=[pltpu.VMEM((p, p), jnp.float32)],
        compiler_params=pltpu.CompilerParams(vmem_limit_bytes=20 << 20),
        name="node_tables",
    )(index, mode_index, weights)


def whole(shape):
    return pl.BlockSpec(shape, lambda *_: (0,) * len(shape))


def rim_kernel(rows, u_ref, log_ref, first_ref, last_ref, near_ref):
    start = 0
    for ref in (u_ref, log_ref):
        n = ref.shape[0] // rows
        span = slice(start, start + n)
        lane = lax.broadcasted_iota(jnp.int32, (n, LANES), 1)
        near = jnp.zeros((n, LANES), jnp.float32)
        for y in range(rows):
            here = ref[pl.ds(y, n, stride=rows), :]
            if y == 0:
                first_ref[span] = here
            if y == rows - 1:
                last_ref[span] = here
            near = jnp.where(lane == y, here[:, 0:1], near)
            near = jnp.where(lane == rows + y, here[:, LANES - 1 : LANES], near)
        near_ref[span] = near
        start += n


def rim_of(rows, field, logs):
    n = (field.shape[0] + logs.shape[0]) // rows
    return pl.pallas_call(
        functools.partial(rim_kernel, rows),
        out_shape=[jax.ShapeDtypeStruct((n, LANES), jnp.float32)] * 3,
        compiler_params=pltpu.CompilerParams(vmem_limit_bytes=20 << 20),
        name="rim_of",
    )(field, logs)


def put_cat(ref, lanes, x):
    p = x.shape[0]
    top, low = split(x)
    ref[0:p, lanes] = top
    ref[p : 2 * p, lanes] = low
    ref[2 * p : 3 * p, lanes] = top


def projected(w_ref, parts):
    p = w_ref.shape[0] // 2
    top, low = parts
    both = jnp.dot(w_ref[...], top, preferred_element_type=jnp.float32)
    rest = jnp.dot(w_ref[0:p, :], low, preferred_element_type=jnp.float32)
    return both[0:p] + both[p : 2 * p] + rest


def resistance(germ_ref, log):
    return jnp.exp2(jnp.dot(germ_ref[...], log, preferred_element_type=jnp.float32))


def inner_kernel(rows, u_ref, log_ref, basis_ref, germ_ref, w_ref, mass_ref, g_ref, u_cat_ref, du_ref, r_ref, f_ref):
    p = mass_ref.shape[0]
    cols = LANES
    lane = lax.broadcasted_iota(jnp.int32, (p, cols), 1)
    above = None
    for y in range(rows):
        here = u_ref[pl.ds(y, p, stride=rows), :]
        put_cat(u_cat_ref, pl.ds(y * cols, cols), here)
        ahead = pltpu.roll(here, cols - 1, axis=1)
        put_cat(du_ref, pl.ds(y * cols, cols), jnp.where(lane == cols - 1, 0.0, ahead - here))
        if y > 0:
            put_cat(du_ref, pl.ds((rows + y - 1) * cols, cols), here - above)
        above = here

    chunks = [("x", y, 2) for y in range(0, rows, 2)]
    chunks += [("y", y, min(2, rows - 1 - y)) for y in range(0, rows - 1, 2)]

    def lanes(chunk):
        kind, y, n = chunk
        return pl.ds((y if kind == "x" else rows + y) * cols, n * cols)

    def values(chunk):
        return jnp.dot(basis_ref[...], du_ref[:, lanes(chunk)], preferred_element_type=jnp.float32)

    def total(chunk):
        kind, y, n = chunk
        if kind == "y":
            return r_ref[:, pl.ds(y * cols, n * cols)] + r_ref[:, pl.ds((y + 1) * cols, n * cols)]
        sums = []
        for k in range(n):
            r = r_ref[:, pl.ds((y + k) * cols, cols)]
            sums.append(r + pltpu.roll(r, cols - 1, axis=1))
        return jnp.concatenate(sums, axis=1)

    def fill(y):
        span = pl.ds(y * cols, 2 * cols)
        r_ref[:, span] = resistance(germ_ref, log_ref[:, span])

    fill(0)
    value = values(chunks[0])
    waiting = None
    for i, chunk in enumerate(chunks):
        later = values(chunks[i + 1]) if i + 1 < len(chunks) else None
        if 2 * (i + 1) < rows:
            fill(2 * (i + 1))
        parts = split(value / total(chunk))
        if waiting is not None:
            f_ref[:, lanes(waiting[0])] = projected(w_ref, waiting[1])
        waiting = (chunk, parts)
        value = later
    stored = [
        jnp.dot(mass_ref[...], u_cat_ref[:, pl.ds(y * cols, 2 * cols)], preferred_element_type=jnp.float32)
        for y in range(0, rows, 2)
    ]
    f_ref[:, lanes(waiting[0])] = projected(w_ref, waiting[1])

    for y in range(rows):
        out = stored[y // 2][:, (y % 2) * cols : (y % 2 + 1) * cols]
        later = f_ref[:, pl.ds(y * cols, cols)]
        earlier = jnp.where(lane == 0, 0.0, pltpu.roll(later, 1, axis=1))
        later = jnp.where(lane == cols - 1, 0.0, later)
        out = out - (later - earlier)
        if y < rows - 1:
            out = out - f_ref[:, pl.ds((rows + y) * cols, cols)]
        if y > 0:
            out = out + f_ref[:, pl.ds((rows + y - 1) * cols, cols)]
        g_ref[y] = out


def inner_fluxes(rows, field, logs, basis_cat, weight_cat, germ_cat, mass_cat):
    p, cols = field.shape[0] // rows, field.shape[1]
    q = basis_cat.shape[0]
    faces = (2 * rows - 1) * cols
    return pl.pallas_call(
        functools.partial(inner_kernel, rows),
        out_shape=jax.ShapeDtypeStruct((rows, p, cols), jnp.float32),
        scratch_shapes=[
            pltpu.VMEM((3 * p, rows * cols), jnp.bfloat16),
            pltpu.VMEM((3 * p, faces), jnp.bfloat16),
            pltpu.VMEM((q, rows * cols), jnp.float32),
            pltpu.VMEM((p, faces), jnp.float32),
        ],
        compiler_params=pltpu.CompilerParams(vmem_limit_bytes=50 << 20),
        cost_estimate=pl.CostEstimate(
            flops=2 * q * faces * p * 6, bytes_accessed=8 << 20, transcendentals=q * rows * cols
        ),
        name="inner_fluxes",
    )(field, logs, basis_cat, germ_cat, weight_cat, mass_cat)


def outer_kernel(
    rows, open_ref, g_ref, first_ref, last_ref, near_ref, up_ref, down_ref, left_ref, right_ref,
    basis_ref, germ_ref, w_ref, out_ref, du_ref, le_ref, ll_ref,
):
    p = w_ref.shape[0] // 2
    cols = LANES
    near = near_ref[...]
    left = pltpu.roll(left_ref[...], cols - rows, axis=1)
    right = pltpu.roll(right_ref[...], rows, axis=1)
    lane = lax.broadcasted_iota(jnp.int32, near.shape, 1)
    earlier = jnp.where(lane < rows, left, near)
    later = jnp.where(lane < rows, near, right)
    pairs = ((up_ref[...], first_ref[...]), (last_ref[...], down_ref[...]), (earlier, later))
    for k, (e, l) in enumerate(pairs):
        span = pl.ds(k * cols, cols)
        diff = l[0:p] - e[0:p]
        if k < 2:
            diff = diff * open_ref[k]
        else:
            low = lane[0:p] < rows
            diff = jnp.where(low, diff * open_ref[2], diff * open_ref[3])
            diff = jnp.where(lane[0:p] < 2 * rows, diff, 0.0)
        put_cat(du_ref, span, diff)
        put_cat(le_ref, span, e[p : p + SLOT])
        put_cat(ll_ref, span, l[p : p + SLOT])

    def values(span):
        return jnp.dot(basis_ref[...], du_ref[:, span], preferred_element_type=jnp.float32)

    def total(span):
        return resistance(germ_ref, le_ref[:, span]) + resistance(germ_ref, ll_ref[:, span])

    one, two = pl.ds(0, 2 * cols), pl.ds(2 * cols, cols)
    v1 = values(one)
    v2 = values(two)
    t1 = total(one)
    t2 = total(two)
    p1 = split(v1 / t1)
    p2 = split(v2 / t2)
    f1 = projected(w_ref, p1)
    side = projected(w_ref, p2)
    lane = lax.broadcasted_iota(jnp.int32, (p, cols), 1)
    for y in range(rows):
        out = g_ref[y]
        if y == 0:
            out = out + f1[:, 0:cols]
        if y == rows - 1:
            out = out - f1[:, cols : 2 * cols]
        out = out + jnp.where(lane == 0, side[:, y : y + 1], 0.0)
        out = out - jnp.where(lane == cols - 1, side[:, rows + y : rows + y + 1], 0.0)
        out_ref[pl.ds(y, p, stride=rows), :] = out


def outer_fluxes(rows, opened, inner, rims, halos, basis_cat, weight_cat, germ_cat):
    p, cols = inner.shape[1:]
    q = basis_cat.shape[0]
    vmem = pl.BlockSpec(memory_space=pltpu.VMEM)
    return pl.pallas_call(
        functools.partial(outer_kernel, rows),
        in_specs=[pl.BlockSpec(memory_space=pltpu.SMEM)] + [vmem] * 11,
        out_shape=jax.ShapeDtypeStruct((p * rows, cols), jnp.float32),
        scratch_shapes=[
            pltpu.VMEM((3 * p, 3 * cols), jnp.bfloat16),
            pltpu.VMEM((3 * SLOT, 3 * cols), jnp.bfloat16),
            pltpu.VMEM((3 * SLOT, 3 * cols), jnp.bfloat16),
        ],
        compiler_params=pltpu.CompilerParams(vmem_limit_bytes=50 << 20),
        cost_estimate=pl.CostEstimate(
            flops=2 * q * 3 * cols * p * 6, bytes_accessed=8 << 20, transcendentals=q * 6 * cols
        ),
        name="outer_fluxes",
    )(opened, inner, *rims, *halos, basis_cat, germ_cat, weight_cat)


def local_kernel(
    nsa, place_ref, part_ref, s0_ref, s1_ref, s2_ref, s3_ref, cy_ref, cx_ref, cxt_ref, ends_of_ref,
    recip_ref, coef_ref, z_ref, jump_ref, res_ref,
):
    modes, length, cols = s0_ref.shape
    rows = part_ref.shape[2]
    ngy = 4
    ny = ngy * length
    for d, src_ref in enumerate((s0_ref, s1_ref, s2_ref, s3_ref)):
        g = lax.rem(place_ref[0] + ngy - d, ngy)
        for s in range(nsa):
            span = pl.ds(pl.multiple_of(g * length + s * rows, 8), rows)
            for m in range(modes):
                res_ref[span, pl.ds(m * cols, cols)] = (
                    src_ref[m, pl.ds(s * rows, rows), :] - part_ref[s * ngy + g, m]
                )
    spectral = jnp.dot(cy_ref[...], res_ref[...], precision=HIGHEST, preferred_element_type=jnp.float32)
    spectral = jnp.concatenate([spectral[:, m * cols : (m + 1) * cols] for m in range(modes)], axis=0)
    spectral = jnp.dot(spectral, cxt_ref[...], precision=HIGHEST, preferred_element_type=jnp.float32)
    recip = recip_ref[...]
    scaled = jnp.concatenate(
        [recip * spectral[m * ny : (m + 1) * ny] for m in range(modes)], axis=0
    )
    both = lax.dot_general(
        ends_of_ref[...], scaled, (((1,), (1,)), ((), ())),
        precision=HIGHEST, preferred_element_type=jnp.float32,
    )
    pad = [jnp.zeros((8 - modes, ny), jnp.float32)]
    first = jnp.concatenate([both[0:1, m * ny : (m + 1) * ny] for m in range(modes)] + pad, axis=0)
    last = jnp.concatenate([both[1:2, m * ny : (m + 1) * ny] for m in range(modes)] + pad, axis=0)
    blocks = jump_ref.shape[0]
    for i in range(blocks + 1):
        term = coef_ref[0, i : i + 1, :] * first + coef_ref[1, i : i + 1, :] * last
        if i < blocks:
            jump_ref[i, 0:8, :] = term
        if i > 0:
            jump_ref[i - 1, 8:16, :] = term
    z = jnp.dot(scaled, cx_ref[...], precision=HIGHEST, preferred_element_type=jnp.float32)
    for m in range(modes):
        z_ref[m] = z[m * ny : (m + 1) * ny]


def joined_kernel(z_ref, jump_ref, g_first_ref, g_last_ref, cyt_ref, out_ref):
    modes, ny, cols = z_ref.shape
    blocks = jump_ref.shape[0]
    ngy = out_ref.shape[0]
    length = ny // ngy
    total = jump_ref[0]
    for i in range(1, blocks):
        total = total + jump_ref[i]
    both = jnp.concatenate([total, jnp.zeros((LANES - 16, ny), jnp.float32)], axis=0).T
    x = jnp.concatenate(
        [
            z_ref[m]
            + g_first_ref[...] * both[:, m : m + 1]
            - g_last_ref[...] * both[:, 8 + m : 9 + m]
            for m in range(modes)
        ],
        axis=1,
    )
    out = jnp.dot(cyt_ref[...], x, precision=HIGHEST, preferred_element_type=jnp.float32)
    for g in range(ngy):
        for m in range(modes):
            out_ref[g, m] = out[g * length : (g + 1) * length, m * cols : (m + 1) * cols]


def solve_tables(mean_perm, ny, cols, blocks, position):
    cx = cosine_matrix(cols)
    lam_y = jnp.asarray(eigen_values(ny, ny), jnp.float32)
    lam_x = jnp.asarray(eigen_values(cols, cols), jnp.float32)
    recip = 1.0 / (storage_rate + mean_perm * (lam_y[:, None] + lam_x[None, :]))
    first = jnp.asarray(cx[:, 0][:, None] * cx, jnp.float32)
    last = jnp.asarray(cx[:, -1][:, None] * cx, jnp.float32)
    g_first = jnp.dot(recip, first, precision=HIGHEST)
    g_last = jnp.dot(recip, last, precision=HIGHEST)
    k = np.arange(1, blocks)
    sine = math.sqrt(2.0 / blocks) * np.sin(np.pi * np.outer(np.arange(0, blocks + 1), k) / blocks)
    sine[0] = 0.0
    sine[blocks] = 0.0
    theta = jnp.asarray(2.0 * np.cos(np.pi * k / blocks), jnp.float32)
    spread = 1.0 / (
        1.0 / mean_perm + g_first[:, 0:1] + g_last[:, cols - 1 : cols] - g_first[:, cols - 1 : cols] * theta
    )
    table = jnp.asarray(sine, jnp.float32)
    coef = []
    for end, sign in ((0, -1.0), (1, 1.0)):
        mine = sign * lax.dynamic_slice_in_dim(table, position + end, 1, axis=0)
        coef.append(jnp.einsum("ik,jk->ij", table, spread * mine, precision=HIGHEST))
    return recip, g_first, g_last, jnp.stack(coef)


def rotated(x, axis, by):
    count = lax.axis_size(axis)
    return lax.ppermute(x, axis, [(i, (i + by) % count) for i in range(count)])


def on_device(
    field_now, field_before, source, log_fields, weights, mean_perm, node_index, mode_index
):
    nsa, ngy, ngx = (lax.axis_size(a) for a in ("sa", "gy", "gx"))
    modes, length, cols = field_now.shape
    rows = length // nsa
    p = modes * nsa
    ny = length * ngy
    sub = modes // ngy
    fields = log_fields.shape[0]

    outgoing = field_now.reshape(modes, nsa, rows, cols).transpose(1, 0, 2, 3)
    field = lax.all_to_all(outgoing, "sa", 0, 0, tiled=True).reshape(p * rows, cols)

    place = lax.axis_index("gy")
    blocks = source.reshape(ngy, sub, length, cols)
    pieces = [lax.dynamic_index_in_dim(blocks, (place + d) % ngy, 0, keepdims=False) for d in range(ngy)]
    pieces = pieces[:1] + [rotated(pieces[d], "gy", d) for d in range(1, ngy)]

    basis_cat, weight_cat, germ_cat, mass_cat = node_tables(node_index, mode_index, weights)
    recip, g_first, g_last, coef = solve_tables(mean_perm, ny, cols, ngx, lax.axis_index("gx"))

    row_axis = ("gy", "sa")
    row_index = lax.axis_index(row_axis)
    col_index = lax.axis_index("gx")
    opened = jnp.stack(
        [row_index > 0, row_index < ngy * nsa - 1, col_index > 0, col_index < ngx - 1]
    ).astype(jnp.float32)
    scaled_logs = jnp.pad(
        log_fields * jnp.float32(-math.log2(math.e)), ((0, SLOT - fields), (0, 0), (0, 0))
    )
    top, low = halves(scaled_logs.reshape(SLOT, rows * cols))
    logs = jnp.concatenate([top, low, top], axis=0)

    rims = rim_of(rows, field, scaled_logs.reshape(SLOT * rows, cols))
    first, last, near = rims
    halos = (
        rotated(last, row_axis, 1),
        rotated(first, row_axis, -1),
        rotated(near, "gx", 1),
        rotated(near, "gx", -1),
    )
    inner = inner_fluxes(rows, field, logs, basis_cat, weight_cat, germ_cat, mass_cat)
    galerkin = outer_fluxes(rows, opened, inner, rims, halos, basis_cat, weight_cat, germ_cat)
    part = lax.all_to_all(
        galerkin.reshape(nsa * ngy, sub, rows, cols), ("sa", "gy"), 0, 0, tiled=True
    )

    cy = cosine_matrix(ny)
    cx = cosine_matrix(cols)
    ends_of = np.zeros((8, cols))
    ends_of[0], ends_of[1] = cx[:, 0], cx[:, -1]
    f32 = functools.partial(jnp.asarray, dtype=jnp.float32)
    params = pltpu.CompilerParams(vmem_limit_bytes=40 << 20)
    vmem = pl.BlockSpec(memory_space=pltpu.VMEM)
    z, jumps = pl.pallas_call(
        functools.partial(local_kernel, nsa),
        in_specs=[pl.BlockSpec(memory_space=pltpu.SMEM)] + [vmem] * 11,
        out_shape=(
            jax.ShapeDtypeStruct((sub, ny, cols), jnp.float32),
            jax.ShapeDtypeStruct((ngx, 16, ny), jnp.float32),
        ),
        scratch_shapes=[pltpu.VMEM((ny, sub * cols), jnp.float32)],
        compiler_params=params,
        name="local_solve",
    )(place[None], part, *pieces, f32(cy), f32(cx), f32(cx.T), f32(ends_of), recip, coef)
    jumps = lax.all_to_all(jumps, "gx", 0, 0, tiled=True)
    columns = pl.pallas_call(
        joined_kernel,
        out_shape=jax.ShapeDtypeStruct((ngy, sub, length, cols), jnp.float32),
        compiler_params=params,
        name="joined_solve",
    )(z, jumps, g_first, g_last, f32(cy.T))
    update = lax.all_to_all(columns, "gy", 0, 0, tiled=True).reshape(modes, length, cols)
    fresh = field_before + relax_weight * (field_now - field_before + step_length * update)
    return (fresh, update)


def solution(mesh):
    block = P("sa", "gy", "gx")
    in_specs = (block, block, block, P(None, ("gy", "sa"), "gx"), P(), P(), P(), P())
    return jax.shard_map(
        on_device, mesh=mesh, in_specs=in_specs, out_specs=(block, block), check_vma=False
    )
```

```python
import functools
import math

import jax
import jax.numpy as jnp
import numpy as np
from jax import lax
from jax.experimental import pallas as pl
from jax.experimental.pallas import tpu as pltpu
from jax.sharding import PartitionSpec as P

HIGHEST = lax.Precision.HIGHEST
hermite_points = (
    0.0,
    -1.7320508075688772,
    1.7320508075688772,
    -1.355626179974266,
    1.355626179974266,
    -2.8569700138728056,
    2.8569700138728056,
)
storage_rate = 0.0004
relax_weight = 1.6
step_length = 0.3
QB = 256
LANES = 128


def halves(x):
    top = lax.reduce_precision(x, 8, 7)
    return top.astype(jnp.bfloat16), (x - top).astype(jnp.bfloat16)


def split(x):
    top = x.astype(jnp.bfloat16)
    return top, (x - top.astype(jnp.float32)).astype(jnp.bfloat16)


def cosine_matrix(length):
    k = np.arange(length)[:, None]
    m = np.arange(length)[None, :]
    phase = (k * (2 * m + 1)) % (4 * length)
    factor = np.where(k == 0, math.sqrt(1.0 / length), math.sqrt(2.0 / length))
    return factor * np.cos(phase * (math.pi / (2 * length)))


def eigen_values(count, length):
    return 4.0 * np.sin(np.arange(count) * (math.pi / (2 * length))) ** 2


SLOT = 16
PIECE = 384
VMEM_GRANT = 30 << 20


def tables_kernel(index_ref, mode_ref, weight_ref, basis_ref, w_ref, germ_ref, mass_ref, sum_ref):
    germs, q = index_ref.shape
    p = mode_ref.shape[0]
    step = pl.program_id(0)
    index = index_ref[...]
    germ = jnp.zeros((germs, q), jnp.float32)
    for level, point in enumerate(hermite_points):
        germ = jnp.where(index == level, jnp.float32(point), germ)
    square = germ * germ
    h2 = (square - 1.0) / math.sqrt(2.0)
    h3 = (square * germ - 3.0 * germ) / math.sqrt(6.0)
    basis = jnp.ones((p, q), jnp.float32)
    for i in range(germs):
        degree = mode_ref[:, i : i + 1]
        factor = jnp.where(
            degree == 1,
            germ[i : i + 1],
            jnp.where(degree == 2, h2[i : i + 1], jnp.where(degree == 3, h3[i : i + 1], 1.0)),
        )
        basis = basis * factor
    weighted = basis * weight_ref[...]
    w_ref[0:p, :], w_ref[p : 2 * p, :] = split(2.0 * weighted)
    top, low = split(basis.T)
    basis_ref[:, 0:p] = top
    basis_ref[:, p : 2 * p] = top
    basis_ref[:, 2 * p : 3 * p] = low
    full = jnp.concatenate(
        [jnp.ones((8, q), jnp.float32), germ, jnp.zeros((LANES - 16, q), jnp.float32)], axis=0
    )
    top, low = split(full.T[:, 7 : 7 + SLOT])
    lane = lax.broadcasted_iota(jnp.int32, (q, SLOT), 1)
    keep = lane < germs + 1
    top = jnp.where(keep, top.astype(jnp.float32), 0.0).astype(jnp.bfloat16)
    low = jnp.where(keep, low.astype(jnp.float32), 0.0).astype(jnp.bfloat16)
    germ_ref[:, 0:SLOT] = top
    germ_ref[:, SLOT : 2 * SLOT] = top
    germ_ref[:, 2 * SLOT : 3 * SLOT] = low

    @pl.when(step == 0)
    def _():
        sum_ref[...] = jnp.zeros_like(sum_ref)

    sum_ref[...] += lax.dot_general(
        storage_rate * weighted, basis, (((1,), (1,)), ((), ())),
        precision=HIGHEST, preferred_element_type=jnp.float32,
    )

    @pl.when(step == pl.num_programs(0) - 1)
    def _():
        top, low = split(sum_ref[...])
        mass_ref[:, 0:p] = top
        mass_ref[:, p : 2 * p] = top
        mass_ref[:, 2 * p : 3 * p] = low


def node_tables(node_index, mode_index, weights):
    q, germs = node_index.shape
    p = mode_index.shape[0]
    pad = -q % QB
    index = jnp.pad(node_index.T, ((0, 0), (0, pad)))
    weights = jnp.pad(weights, (0, pad))[None]
    return pl.pallas_call(
        tables_kernel,
        grid=((q + pad) // QB,),
        in_specs=[
            pl.BlockSpec((germs, QB), lambda i: (0, i)),
            whole((p, germs)),
            pl.BlockSpec((1, QB), lambda i: (0, i)),
        ],
        out_specs=[
            pl.BlockSpec((QB, 3 * p), lambda i: (i, 0)),
            pl.BlockSpec((2 * p, QB), lambda i: (0, i)),
            pl.BlockSpec((QB, 3 * SLOT), lambda i: (i, 0)),
            whole((p, 3 * p)),
        ],
        out_shape=[
            jax.ShapeDtypeStruct((q + pad, 3 * p), jnp.bfloat16),
            jax.ShapeDtypeStruct((2 * p, q + pad), jnp.bfloat16),
            jax.ShapeDtypeStruct((q + pad, 3 * SLOT), jnp.bfloat16),
            jax.ShapeDtypeStruct((p, 3 * p), jnp.bfloat16),
        ],
        scratch_shapes=[pltpu.VMEM((p, p), jnp.float32)],
        compiler_params=pltpu.CompilerParams(vmem_limit_bytes=20 << 20),
        name="node_tables",
    )(index, mode_index, weights)


def whole(shape):
    return pl.BlockSpec(shape, lambda *_: (0,) * len(shape))


def rim_kernel(rows, u_ref, log_ref, first_ref, last_ref, near_ref):
    start = 0
    for ref in (u_ref, log_ref):
        n = ref.shape[0] // rows
        span = slice(start, start + n)
        lane = lax.broadcasted_iota(jnp.int32, (n, LANES), 1)
        near = jnp.zeros((n, LANES), jnp.float32)
        for y in range(rows):
            here = ref[pl.ds(y, n, stride=rows), :]
            if y == 0:
                first_ref[span] = here
            if y == rows - 1:
                last_ref[span] = here
            near = jnp.where(lane == y, here[:, 0:1], near)
            near = jnp.where(lane == rows + y, here[:, LANES - 1 : LANES], near)
        near_ref[span] = near
        start += n


def rim_of(rows, field, logs):
    n = (field.shape[0] + logs.shape[0]) // rows
    return pl.pallas_call(
        functools.partial(rim_kernel, rows),
        out_shape=[jax.ShapeDtypeStruct((n, LANES), jnp.float32)] * 3,
        compiler_params=pltpu.CompilerParams(vmem_limit_bytes=20 << 20),
        name="rim_of",
    )(field, logs)


def put_cat(ref, lanes, x):
    p = x.shape[0]
    top, low = split(x)
    ref[0:p, lanes] = top
    ref[p : 2 * p, lanes] = low
    ref[2 * p : 3 * p, lanes] = top


def projected(w_ref, parts):
    p = w_ref.shape[0] // 2
    top, low = parts
    both = jnp.dot(w_ref[...], top, preferred_element_type=jnp.float32)
    rest = jnp.dot(w_ref[0:p, :], low, preferred_element_type=jnp.float32)
    return both[0:p] + both[p : 2 * p] + rest


def resistance(germ_ref, log):
    return jnp.exp2(jnp.dot(germ_ref[...], log, preferred_element_type=jnp.float32))


def inner_kernel(
    rows, x_rows, y_faces, extra, u_ref, log_ref, basis_ref, germ_ref, w_ref, mass_ref, *refs
):
    if extra:
        g_ref, over_ref, u_cat_ref, du_ref, r_ref, f_ref = refs
    else:
        g_ref, u_cat_ref, du_ref, r_ref, f_ref = refs
    p = mass_ref.shape[0]
    cols = LANES
    lane = lax.broadcasted_iota(jnp.int32, (p, cols), 1)
    n_x = len(x_rows)
    start = min(x_rows[0], y_faces[0] - 1)
    count = x_rows[-1] + 1 - start
    above = None
    for y in range(start, start + count):
        here = u_ref[pl.ds(y, p, stride=rows), :]
        if y in x_rows:
            at = pl.ds((y - x_rows[0]) * cols, cols)
            put_cat(u_cat_ref, at, here)
            ahead = pltpu.roll(here, cols - 1, axis=1)
            put_cat(du_ref, at, jnp.where(lane == cols - 1, 0.0, ahead - here))
        if y in y_faces and above is not None:
            put_cat(du_ref, pl.ds((n_x + y - y_faces[0]) * cols, cols), here - above)
        above = here

    chunks = [("x", y, min(2, x_rows[-1] + 1 - y)) for y in x_rows[::2]]
    chunks += [("y", y, min(2, y_faces[-1] + 1 - y)) for y in y_faces[::2]]

    def lanes(chunk):
        kind, y, n = chunk
        at = y - x_rows[0] if kind == "x" else n_x + y - y_faces[0]
        return pl.ds(at * cols, n * cols)

    def values(chunk):
        return jnp.dot(basis_ref[...], du_ref[:, lanes(chunk)], preferred_element_type=jnp.float32)

    def total(chunk):
        kind, y, n = chunk
        y = y - start
        if kind == "y":
            return r_ref[:, pl.ds((y - 1) * cols, n * cols)] + r_ref[:, pl.ds(y * cols, n * cols)]
        sums = []
        for k in range(n):
            r = r_ref[:, pl.ds((y + k) * cols, cols)]
            sums.append(r + pltpu.roll(r, cols - 1, axis=1))
        return jnp.concatenate(sums, axis=1)

    filled = []

    def fill(top):
        done = filled[-1] if filled else 0
        if done < count:
            n = min(2 if (count - done) % 2 == 0 else 3, count - done)
            r_ref[:, pl.ds(done * cols, n * cols)] = resistance(
                germ_ref, log_ref[:, pl.ds((start + done) * cols, n * cols)]
            )
            filled.append(done + n)

    fill(0)
    value = values(chunks[0])
    waiting = None
    for i, chunk in enumerate(chunks):
        later = values(chunks[i + 1]) if i + 1 < len(chunks) else None
        fill(i + 1)
        parts = split(value / total(chunk))
        if waiting is not None:
            f_ref[:, lanes(waiting[0])] = projected(w_ref, waiting[1])
        waiting = (chunk, parts)
        value = later
    stored = [
        jnp.dot(mass_ref[...], u_cat_ref[:, pl.ds(k * cols, 2 * cols)], preferred_element_type=jnp.float32)
        for k in range(0, n_x, 2)
    ]
    f_ref[:, lanes(waiting[0])] = projected(w_ref, waiting[1])

    for k, y in enumerate(x_rows):
        out = stored[k // 2][:, (k % 2) * cols : (k % 2 + 1) * cols]
        later = f_ref[:, pl.ds(k * cols, cols)]
        earlier = jnp.where(lane == 0, 0.0, pltpu.roll(later, 1, axis=1))
        later = jnp.where(lane == cols - 1, 0.0, later)
        out = out - (later - earlier)
        if y + 1 in y_faces:
            out = out - f_ref[:, pl.ds((n_x + y + 1 - y_faces[0]) * cols, cols)]
        if y in y_faces:
            out = out + f_ref[:, pl.ds((n_x + y - y_faces[0]) * cols, cols)]
        g_ref[k] = out
    if extra:
        over_ref[...] = f_ref[:, pl.ds(n_x * cols, cols)]


def inner_fluxes(rows, x_rows, y_faces, extra, field, logs, basis_cat, weight_cat, germ_cat, mass_cat):
    p, cols = field.shape[0] // rows, field.shape[1]
    q = basis_cat.shape[0]
    n = len(x_rows)
    faces = (n + len(y_faces)) * cols
    count = x_rows[-1] + 1 - min(x_rows[0], y_faces[0] - 1)
    shapes = [jax.ShapeDtypeStruct((n, p, cols), jnp.float32)]
    if extra:
        shapes.append(jax.ShapeDtypeStruct((p, cols), jnp.float32))
    return pl.pallas_call(
        functools.partial(inner_kernel, rows, x_rows, y_faces, extra),
        out_shape=shapes,
        scratch_shapes=[
            pltpu.VMEM((3 * p, n * cols), jnp.bfloat16),
            pltpu.VMEM((3 * p, faces), jnp.bfloat16),
            pltpu.VMEM((q, count * cols), jnp.float32),
            pltpu.VMEM((p, faces), jnp.float32),
        ],
        compiler_params=pltpu.CompilerParams(vmem_limit_bytes=VMEM_GRANT),
        cost_estimate=pl.CostEstimate(
            flops=2 * q * faces * p * 6, bytes_accessed=4 << 20, transcendentals=q * n * cols
        ),
        name="inner_fluxes",
    )(field, logs, basis_cat, germ_cat, weight_cat, mass_cat)


def outer_kernel(
    rows, open_ref, ga_ref, gb_ref, over_ref, first_ref, last_ref, near_ref, up_ref, down_ref,
    left_ref, right_ref, basis_ref, germ_ref, w_ref, out_ref, du_ref, le_ref, ll_ref,
):
    p = w_ref.shape[0] // 2
    q = basis_ref.shape[0]
    cols = LANES
    near = near_ref[...]
    left = pltpu.roll(left_ref[...], cols - rows, axis=1)
    right = pltpu.roll(right_ref[...], rows, axis=1)
    lane = lax.broadcasted_iota(jnp.int32, near.shape, 1)
    earlier = jnp.where(lane < rows, left, near)
    later = jnp.where(lane < rows, near, right)
    pairs = ((up_ref[...], first_ref[...]), (last_ref[...], down_ref[...]), (earlier, later))
    for k, (e, l) in enumerate(pairs):
        span = pl.ds(k * cols, cols)
        diff = l[0:p] - e[0:p]
        if k < 2:
            diff = diff * open_ref[k]
        else:
            low = lane[0:p] < rows
            diff = jnp.where(low, diff * open_ref[2], diff * open_ref[3])
            diff = jnp.where(lane[0:p] < 2 * rows, diff, 0.0)
        put_cat(du_ref, span, diff)
        put_cat(le_ref, span, e[p : p + SLOT])
        put_cat(ll_ref, span, l[p : p + SLOT])

    def values(i):
        return jnp.dot(
            basis_ref[pl.ds(i * PIECE, PIECE), :], du_ref[...], preferred_element_type=jnp.float32
        )

    def total(i):
        germ = germ_ref[pl.ds(i * PIECE, PIECE), :]
        e = jnp.exp2(jnp.dot(germ, le_ref[...], preferred_element_type=jnp.float32))
        return e + jnp.exp2(jnp.dot(germ, ll_ref[...], preferred_element_type=jnp.float32))

    def project(i, parts):
        top, low = parts
        at = pl.ds(i * PIECE, PIECE)
        both = jnp.dot(w_ref[:, at], top, preferred_element_type=jnp.float32)
        rest = jnp.dot(w_ref[0:p, at], low, preferred_element_type=jnp.float32)
        return both[0:p] + both[p : 2 * p] + rest

    steps = q // PIECE
    value, sums = values(0), total(0)
    flux, waiting = None, None
    for i in range(steps):
        later = (values(i + 1), total(i + 1)) if i + 1 < steps else (None, None)
        parts = split(value / sums)
        if waiting is not None:
            term = project(*waiting)
            flux = term if flux is None else flux + term
        waiting = (i, parts)
        value, sums = later
    flux = flux + project(*waiting)

    lane = lax.broadcasted_iota(jnp.int32, (p, cols), 1)
    half = ga_ref.shape[0]
    for y in range(rows):
        out = ga_ref[y] if y < half else gb_ref[y - half]
        if y == half - 1:
            out = out - over_ref[...]
        if y == 0:
            out = out + flux[:, 0:cols]
        if y == rows - 1:
            out = out - flux[:, cols : 2 * cols]
        out = out + jnp.where(lane == 0, flux[:, 2 * cols + y : 2 * cols + y + 1], 0.0)
        at = 2 * cols + rows + y
        out = out - jnp.where(lane == cols - 1, flux[:, at : at + 1], 0.0)
        out_ref[pl.ds(y, p, stride=rows), :] = out


def outer_fluxes(rows, opened, inner, rims, halos, basis_cat, weight_cat, germ_cat):
    p, cols = inner[0].shape[1:]
    q = basis_cat.shape[0]
    vmem = pl.BlockSpec(memory_space=pltpu.VMEM)
    return pl.pallas_call(
        functools.partial(outer_kernel, rows),
        in_specs=[pl.BlockSpec(memory_space=pltpu.SMEM)] + [vmem] * 13,
        out_shape=jax.ShapeDtypeStruct((p * rows, cols), jnp.float32),
        scratch_shapes=[
            pltpu.VMEM((3 * p, 3 * cols), jnp.bfloat16),
            pltpu.VMEM((3 * SLOT, 3 * cols), jnp.bfloat16),
            pltpu.VMEM((3 * SLOT, 3 * cols), jnp.bfloat16),
        ],
        compiler_params=pltpu.CompilerParams(vmem_limit_bytes=VMEM_GRANT),
        cost_estimate=pl.CostEstimate(
            flops=2 * q * 3 * cols * p * 6, bytes_accessed=8 << 20, transcendentals=q * 6 * cols
        ),
        name="outer_fluxes",
    )(opened, *inner, *rims, *halos, basis_cat, germ_cat, weight_cat)


def local_kernel(
    nsa, place_ref, part_ref, s0_ref, s1_ref, s2_ref, s3_ref, cy_ref, cx_ref, cxt_ref, ends_of_ref,
    recip_ref, coef_ref, z_ref, jump_ref, res_ref,
):
    modes, length, cols = s0_ref.shape
    rows = part_ref.shape[2]
    ngy = 4
    ny = ngy * length
    for d, src_ref in enumerate((s0_ref, s1_ref, s2_ref, s3_ref)):
        g = lax.rem(place_ref[0] + ngy - d, ngy)
        for s in range(nsa):
            span = pl.ds(pl.multiple_of(g * length + s * rows, 8), rows)
            for m in range(modes):
                res_ref[span, pl.ds(m * cols, cols)] = (
                    src_ref[m, pl.ds(s * rows, rows), :] - part_ref[s * ngy + g, m]
                )
    spectral = jnp.dot(cy_ref[...], res_ref[...], precision=HIGHEST, preferred_element_type=jnp.float32)
    spectral = jnp.concatenate([spectral[:, m * cols : (m + 1) * cols] for m in range(modes)], axis=0)
    spectral = jnp.dot(spectral, cxt_ref[...], precision=HIGHEST, preferred_element_type=jnp.float32)
    recip = recip_ref[...]
    scaled = jnp.concatenate(
        [recip * spectral[m * ny : (m + 1) * ny] for m in range(modes)], axis=0
    )
    both = lax.dot_general(
        ends_of_ref[...], scaled, (((1,), (1,)), ((), ())),
        precision=HIGHEST, preferred_element_type=jnp.float32,
    )
    pad = [jnp.zeros((8 - modes, ny), jnp.float32)]
    first = jnp.concatenate([both[0:1, m * ny : (m + 1) * ny] for m in range(modes)] + pad, axis=0)
    last = jnp.concatenate([both[1:2, m * ny : (m + 1) * ny] for m in range(modes)] + pad, axis=0)
    blocks = jump_ref.shape[0]
    for i in range(blocks + 1):
        term = coef_ref[0, i : i + 1, :] * first + coef_ref[1, i : i + 1, :] * last
        if i < blocks:
            jump_ref[i, 0:8, :] = term
        if i > 0:
            jump_ref[i - 1, 8:16, :] = term
    z = jnp.dot(scaled, cx_ref[...], precision=HIGHEST, preferred_element_type=jnp.float32)
    for m in range(modes):
        z_ref[m] = z[m * ny : (m + 1) * ny]


def joined_kernel(z_ref, jump_ref, g_first_ref, g_last_ref, cyt_ref, out_ref):
    modes, ny, cols = z_ref.shape
    blocks = jump_ref.shape[0]
    ngy = out_ref.shape[0]
    length = ny // ngy
    total = jump_ref[0]
    for i in range(1, blocks):
        total = total + jump_ref[i]
    both = jnp.concatenate([total, jnp.zeros((LANES - 16, ny), jnp.float32)], axis=0).T
    x = jnp.concatenate(
        [
            z_ref[m]
            + g_first_ref[...] * both[:, m : m + 1]
            - g_last_ref[...] * both[:, 8 + m : 9 + m]
            for m in range(modes)
        ],
        axis=1,
    )
    out = jnp.dot(cyt_ref[...], x, precision=HIGHEST, preferred_element_type=jnp.float32)
    for g in range(ngy):
        for m in range(modes):
            out_ref[g, m] = out[g * length : (g + 1) * length, m * cols : (m + 1) * cols]


def solve_tables(mean_perm, ny, cols, blocks, position):
    cx = cosine_matrix(cols)
    lam_y = jnp.asarray(eigen_values(ny, ny), jnp.float32)
    lam_x = jnp.asarray(eigen_values(cols, cols), jnp.float32)
    recip = 1.0 / (storage_rate + mean_perm * (lam_y[:, None] + lam_x[None, :]))
    first = jnp.asarray(cx[:, 0][:, None] * cx, jnp.float32)
    last = jnp.asarray(cx[:, -1][:, None] * cx, jnp.float32)
    g_first = jnp.dot(recip, first, precision=HIGHEST)
    g_last = jnp.dot(recip, last, precision=HIGHEST)
    k = np.arange(1, blocks)
    sine = math.sqrt(2.0 / blocks) * np.sin(np.pi * np.outer(np.arange(0, blocks + 1), k) / blocks)
    sine[0] = 0.0
    sine[blocks] = 0.0
    theta = jnp.asarray(2.0 * np.cos(np.pi * k / blocks), jnp.float32)
    spread = 1.0 / (
        1.0 / mean_perm + g_first[:, 0:1] + g_last[:, cols - 1 : cols] - g_first[:, cols - 1 : cols] * theta
    )
    table = jnp.asarray(sine, jnp.float32)
    coef = []
    for end, sign in ((0, -1.0), (1, 1.0)):
        mine = sign * lax.dynamic_slice_in_dim(table, position + end, 1, axis=0)
        coef.append(jnp.einsum("ik,jk->ij", table, spread * mine, precision=HIGHEST))
    return recip, g_first, g_last, jnp.stack(coef)


def rotated(x, axis, by):
    count = lax.axis_size(axis)
    return lax.ppermute(x, axis, [(i, (i + by) % count) for i in range(count)])


def on_device(
    field_now, field_before, source, log_fields, weights, mean_perm, node_index, mode_index
):
    nsa, ngy, ngx = (lax.axis_size(a) for a in ("sa", "gy", "gx"))
    modes, length, cols = field_now.shape
    rows = length // nsa
    p = modes * nsa
    ny = length * ngy
    sub = modes // ngy
    fields = log_fields.shape[0]

    outgoing = field_now.reshape(modes, nsa, rows, cols).transpose(1, 0, 2, 3)
    field = lax.all_to_all(outgoing, "sa", 0, 0, tiled=True).reshape(p * rows, cols)

    place = lax.axis_index("gy")
    blocks = source.reshape(ngy, sub, length, cols)
    pieces = [lax.dynamic_index_in_dim(blocks, (place + d) % ngy, 0, keepdims=False) for d in range(ngy)]
    pieces = pieces[:1] + [rotated(pieces[d], "gy", d) for d in range(1, ngy)]

    basis_cat, weight_cat, germ_cat, mass_cat = node_tables(node_index, mode_index, weights)
    recip, g_first, g_last, coef = solve_tables(mean_perm, ny, cols, ngx, lax.axis_index("gx"))

    row_axis = ("gy", "sa")
    row_index = lax.axis_index(row_axis)
    col_index = lax.axis_index("gx")
    opened = jnp.stack(
        [row_index > 0, row_index < ngy * nsa - 1, col_index > 0, col_index < ngx - 1]
    ).astype(jnp.float32)
    scaled_logs = jnp.pad(
        log_fields * jnp.float32(-math.log2(math.e)), ((0, SLOT - fields), (0, 0), (0, 0))
    )
    top, low = halves(scaled_logs.reshape(SLOT, rows * cols))
    logs = jnp.concatenate([top, low, top], axis=0)

    field, *pieces = lax.optimization_barrier((field, *pieces))
    half = rows // 2
    tables = (logs, basis_cat, weight_cat, germ_cat, mass_cat)
    upper = inner_fluxes(rows, range(half), range(1, half), False, field, *tables)
    field, upper = lax.optimization_barrier((field, upper))
    rims = rim_of(rows, field, scaled_logs.reshape(SLOT * rows, cols))
    first, last, near = rims
    halos = (
        rotated(last, row_axis, 1),
        rotated(first, row_axis, -1),
        rotated(near, "gx", 1),
        rotated(near, "gx", -1),
    )
    lower = inner_fluxes(rows, range(half, rows), range(half, rows), True, field, *tables)
    galerkin = outer_fluxes(rows, opened, upper + lower, rims, halos, basis_cat, weight_cat, germ_cat)
    part = lax.all_to_all(
        galerkin.reshape(nsa * ngy, sub, rows, cols), ("sa", "gy"), 0, 0, tiled=True
    )

    cy = cosine_matrix(ny)
    cx = cosine_matrix(cols)
    ends_of = np.zeros((8, cols))
    ends_of[0], ends_of[1] = cx[:, 0], cx[:, -1]
    f32 = functools.partial(jnp.asarray, dtype=jnp.float32)
    params = pltpu.CompilerParams(vmem_limit_bytes=40 << 20)
    vmem = pl.BlockSpec(memory_space=pltpu.VMEM)
    z, jumps = pl.pallas_call(
        functools.partial(local_kernel, nsa),
        in_specs=[pl.BlockSpec(memory_space=pltpu.SMEM)] + [vmem] * 11,
        out_shape=(
            jax.ShapeDtypeStruct((sub, ny, cols), jnp.float32),
            jax.ShapeDtypeStruct((ngx, 16, ny), jnp.float32),
        ),
        scratch_shapes=[pltpu.VMEM((ny, sub * cols), jnp.float32)],
        compiler_params=params,
        name="local_solve",
    )(place[None], part, *pieces, f32(cy), f32(cx), f32(cx.T), f32(ends_of), recip, coef)
    jumps = lax.all_to_all(jumps, "gx", 0, 0, tiled=True)
    columns = pl.pallas_call(
        joined_kernel,
        out_shape=jax.ShapeDtypeStruct((ngy, sub, length, cols), jnp.float32),
        compiler_params=params,
        name="joined_solve",
    )(z, jumps, g_first, g_last, f32(cy.T))
    update = lax.all_to_all(columns, "gy", 0, 0, tiled=True).reshape(modes, length, cols)
    fresh = field_before + relax_weight * (field_now - field_before + step_length * update)
    return (fresh, update)


def solution(mesh):
    block = P("sa", "gy", "gx")
    in_specs = (block, block, block, P(None, ("gy", "sa"), "gx"), P(), P(), P(), P())
    return jax.shard_map(
        on_device, mesh=mesh, in_specs=in_specs, out_specs=(block, block), check_vma=False
    )
```

```python
import functools
import math

import jax
import jax.numpy as jnp
import numpy as np
from jax import lax
from jax.experimental import pallas as pl
from jax.experimental.pallas import tpu as pltpu
from jax.sharding import PartitionSpec as P

HIGHEST = lax.Precision.HIGHEST
hermite_points = (
    0.0,
    -1.7320508075688772,
    1.7320508075688772,
    -1.355626179974266,
    1.355626179974266,
    -2.8569700138728056,
    2.8569700138728056,
)
storage_rate = 0.0004
relax_weight = 1.6
step_length = 0.3
QB = 256
LANES = 128


def halves(x):
    top = lax.reduce_precision(x, 8, 7)
    return top.astype(jnp.bfloat16), (x - top).astype(jnp.bfloat16)


def split(x):
    top = x.astype(jnp.bfloat16)
    return top, (x - top.astype(jnp.float32)).astype(jnp.bfloat16)


def cosine_matrix(length):
    k = np.arange(length)[:, None]
    m = np.arange(length)[None, :]
    phase = (k * (2 * m + 1)) % (4 * length)
    factor = np.where(k == 0, math.sqrt(1.0 / length), math.sqrt(2.0 / length))
    return factor * np.cos(phase * (math.pi / (2 * length)))


def eigen_values(count, length):
    return 4.0 * np.sin(np.arange(count) * (math.pi / (2 * length))) ** 2


SLOT = 16
PIECE = 384
VMEM_GRANT = 50 << 20


def tables_kernel(index_ref, mode_ref, weight_ref, basis_ref, w_ref, germ_ref, mass_ref, sum_ref):
    germs, q = index_ref.shape
    p = mode_ref.shape[0]
    step = pl.program_id(0)
    index = index_ref[...]
    germ = jnp.zeros((germs, q), jnp.float32)
    for level, point in enumerate(hermite_points):
        germ = jnp.where(index == level, jnp.float32(point), germ)
    square = germ * germ
    h2 = (square - 1.0) / math.sqrt(2.0)
    h3 = (square * germ - 3.0 * germ) / math.sqrt(6.0)
    basis = jnp.ones((p, q), jnp.float32)
    for i in range(germs):
        degree = mode_ref[:, i : i + 1]
        factor = jnp.where(
            degree == 1,
            germ[i : i + 1],
            jnp.where(degree == 2, h2[i : i + 1], jnp.where(degree == 3, h3[i : i + 1], 1.0)),
        )
        basis = basis * factor
    weighted = basis * weight_ref[...]
    w_ref[0:p, :], w_ref[p : 2 * p, :] = split(2.0 * weighted)
    top, low = split(basis.T)
    basis_ref[:, 0:p] = top
    basis_ref[:, p : 2 * p] = top
    basis_ref[:, 2 * p : 3 * p] = low
    full = jnp.concatenate(
        [jnp.ones((8, q), jnp.float32), germ, jnp.zeros((LANES - 16, q), jnp.float32)], axis=0
    )
    top, low = split(full.T[:, 7 : 7 + SLOT])
    lane = lax.broadcasted_iota(jnp.int32, (q, SLOT), 1)
    keep = lane < germs + 1
    top = jnp.where(keep, top.astype(jnp.float32), 0.0).astype(jnp.bfloat16)
    low = jnp.where(keep, low.astype(jnp.float32), 0.0).astype(jnp.bfloat16)
    germ_ref[:, 0:SLOT] = top
    germ_ref[:, SLOT : 2 * SLOT] = top
    germ_ref[:, 2 * SLOT : 3 * SLOT] = low

    @pl.when(step == 0)
    def _():
        sum_ref[...] = jnp.zeros_like(sum_ref)

    sum_ref[...] += lax.dot_general(
        storage_rate * weighted, basis, (((1,), (1,)), ((), ())),
        precision=HIGHEST, preferred_element_type=jnp.float32,
    )

    @pl.when(step == pl.num_programs(0) - 1)
    def _():
        top, low = split(sum_ref[...])
        mass_ref[:, 0:p] = top
        mass_ref[:, p : 2 * p] = top
        mass_ref[:, 2 * p : 3 * p] = low


def node_tables(node_index, mode_index, weights):
    q, germs = node_index.shape
    p = mode_index.shape[0]
    pad = -q % QB
    index = jnp.pad(node_index.T, ((0, 0), (0, pad)))
    weights = jnp.pad(weights, (0, pad))[None]
    return pl.pallas_call(
        tables_kernel,
        grid=((q + pad) // QB,),
        in_specs=[
            pl.BlockSpec((germs, QB), lambda i: (0, i)),
            whole((p, germs)),
            pl.BlockSpec((1, QB), lambda i: (0, i)),
        ],
        out_specs=[
            pl.BlockSpec((QB, 3 * p), lambda i: (i, 0)),
            pl.BlockSpec((2 * p, QB), lambda i: (0, i)),
            pl.BlockSpec((QB, 3 * SLOT), lambda i: (i, 0)),
            whole((p, 3 * p)),
        ],
        out_shape=[
            jax.ShapeDtypeStruct((q + pad, 3 * p), jnp.bfloat16),
            jax.ShapeDtypeStruct((2 * p, q + pad), jnp.bfloat16),
            jax.ShapeDtypeStruct((q + pad, 3 * SLOT), jnp.bfloat16),
            jax.ShapeDtypeStruct((p, 3 * p), jnp.bfloat16),
        ],
        scratch_shapes=[pltpu.VMEM((p, p), jnp.float32)],
        compiler_params=pltpu.CompilerParams(vmem_limit_bytes=20 << 20),
        name="node_tables",
    )(index, mode_index, weights)


def whole(shape):
    return pl.BlockSpec(shape, lambda *_: (0,) * len(shape))


def rim_kernel(rows, u_ref, log_ref, first_ref, last_ref, near_ref):
    start = 0
    for ref in (u_ref, log_ref):
        n = ref.shape[0] // rows
        span = slice(start, start + n)
        lane = lax.broadcasted_iota(jnp.int32, (n, LANES), 1)
        near = jnp.zeros((n, LANES), jnp.float32)
        for y in range(rows):
            here = ref[pl.ds(y, n, stride=rows), :]
            if y == 0:
                first_ref[span] = here
            if y == rows - 1:
                last_ref[span] = here
            near = jnp.where(lane == y, here[:, 0:1], near)
            near = jnp.where(lane == rows + y, here[:, LANES - 1 : LANES], near)
        near_ref[span] = near
        start += n


def rim_of(rows, field, logs):
    n = (field.shape[0] + logs.shape[0]) // rows
    return pl.pallas_call(
        functools.partial(rim_kernel, rows),
        out_shape=[jax.ShapeDtypeStruct((n, LANES), jnp.float32)] * 3,
        compiler_params=pltpu.CompilerParams(vmem_limit_bytes=20 << 20),
        name="rim_of",
    )(field, logs)


def put_cat(ref, lanes, x):
    p = x.shape[0]
    top, low = split(x)
    ref[0:p, lanes] = top
    ref[p : 2 * p, lanes] = low
    ref[2 * p : 3 * p, lanes] = top


def projected(w_ref, parts):
    p = w_ref.shape[0] // 2
    top, low = parts
    both = jnp.dot(w_ref[...], top, preferred_element_type=jnp.float32)
    rest = jnp.dot(w_ref[0:p, :], low, preferred_element_type=jnp.float32)
    return both[0:p] + both[p : 2 * p] + rest


def resistance(germ_ref, log):
    return jnp.exp2(jnp.dot(germ_ref[...], log, preferred_element_type=jnp.float32))


def inner_kernel(
    rows, u_ref, log_ref, basis_hbm, germ_ref, w_hbm, mass_ref, g_ref, u_cat_ref, du_ref, r_ref, f_ref,
    basis_ref, w_ref, sems,
):
    p = mass_ref.shape[0]
    cols = LANES
    basis_copy = pltpu.make_async_copy(basis_hbm, basis_ref, sems.at[0])
    w_copy = pltpu.make_async_copy(w_hbm, w_ref, sems.at[1])
    basis_copy.start()
    w_copy.start()
    lane = lax.broadcasted_iota(jnp.int32, (p, cols), 1)
    above = None
    for y in range(rows):
        here = u_ref[pl.ds(y, p, stride=rows), :]
        put_cat(u_cat_ref, pl.ds(y * cols, cols), here)
        ahead = pltpu.roll(here, cols - 1, axis=1)
        put_cat(du_ref, pl.ds(y * cols, cols), jnp.where(lane == cols - 1, 0.0, ahead - here))
        if y > 0:
            put_cat(du_ref, pl.ds((rows + y - 1) * cols, cols), here - above)
        above = here

    chunks = [("x", y, 2) for y in range(0, rows, 2)]
    chunks += [("y", y, min(2, rows - 1 - y)) for y in range(0, rows - 1, 2)]

    def lanes(chunk):
        kind, y, n = chunk
        return pl.ds((y if kind == "x" else rows + y) * cols, n * cols)

    def values(chunk):
        return jnp.dot(basis_ref[...], du_ref[:, lanes(chunk)], preferred_element_type=jnp.float32)

    def total(chunk):
        kind, y, n = chunk
        if kind == "y":
            return r_ref[:, pl.ds(y * cols, n * cols)] + r_ref[:, pl.ds((y + 1) * cols, n * cols)]
        sums = []
        for k in range(n):
            r = r_ref[:, pl.ds((y + k) * cols, cols)]
            sums.append(r + pltpu.roll(r, cols - 1, axis=1))
        return jnp.concatenate(sums, axis=1)

    def fill(y):
        span = pl.ds(y * cols, 2 * cols)
        r_ref[:, span] = resistance(germ_ref, log_ref[:, span])

    fill(0)
    basis_copy.wait()
    w_copy.wait()
    value = values(chunks[0])
    waiting = None
    for i, chunk in enumerate(chunks):
        later = values(chunks[i + 1]) if i + 1 < len(chunks) else None
        if 2 * (i + 1) < rows:
            fill(2 * (i + 1))
        parts = split(value / total(chunk))
        if waiting is not None:
            f_ref[:, lanes(waiting[0])] = projected(w_ref, waiting[1])
        waiting = (chunk, parts)
        value = later
    stored = [
        jnp.dot(mass_ref[...], u_cat_ref[:, pl.ds(y * cols, 2 * cols)], preferred_element_type=jnp.float32)
        for y in range(0, rows, 2)
    ]
    f_ref[:, lanes(waiting[0])] = projected(w_ref, waiting[1])

    for y in range(rows):
        out = stored[y // 2][:, (y % 2) * cols : (y % 2 + 1) * cols]
        later = f_ref[:, pl.ds(y * cols, cols)]
        earlier = jnp.where(lane == 0, 0.0, pltpu.roll(later, 1, axis=1))
        later = jnp.where(lane == cols - 1, 0.0, later)
        out = out - (later - earlier)
        if y < rows - 1:
            out = out - f_ref[:, pl.ds((rows + y) * cols, cols)]
        if y > 0:
            out = out + f_ref[:, pl.ds((rows + y - 1) * cols, cols)]
        g_ref[pl.ds(y, p, stride=rows), :] = out


def inner_fluxes(rows, field, logs, basis_cat, weight_cat, germ_cat, mass_cat):
    p, cols = field.shape[0] // rows, field.shape[1]
    q = basis_cat.shape[0]
    faces = (2 * rows - 1) * cols
    vmem, hbm = (pl.BlockSpec(memory_space=space) for space in (pltpu.VMEM, pltpu.HBM))
    return pl.pallas_call(
        functools.partial(inner_kernel, rows),
        in_specs=[vmem, vmem, hbm, vmem, hbm, vmem],
        out_shape=jax.ShapeDtypeStruct((p * rows, cols), jnp.float32),
        scratch_shapes=[
            pltpu.VMEM((3 * p, rows * cols), jnp.bfloat16),
            pltpu.VMEM((3 * p, faces), jnp.bfloat16),
            pltpu.VMEM((q, rows * cols), jnp.float32),
            pltpu.VMEM((p, faces), jnp.float32),
            pltpu.VMEM(basis_cat.shape, basis_cat.dtype),
            pltpu.VMEM(weight_cat.shape, weight_cat.dtype),
            pltpu.SemaphoreType.DMA((2,)),
        ],
        compiler_params=pltpu.CompilerParams(vmem_limit_bytes=VMEM_GRANT),
        cost_estimate=pl.CostEstimate(
            flops=2 * q * faces * p * 6, bytes_accessed=8 << 20, transcendentals=q * rows * cols
        ),
        name="inner_fluxes",
    )(field, logs, basis_cat, germ_cat, weight_cat, mass_cat)


def outer_kernel(
    rows, open_ref, first_ref, last_ref, near_ref, up_ref, down_ref,
    left_ref, right_ref, basis_hbm, germ_ref, w_hbm, out_ref, du_ref, le_ref, ll_ref, basis_ref, w_ref, sems,
):
    p = w_ref.shape[0] // 2
    basis_copy = pltpu.make_async_copy(basis_hbm, basis_ref, sems.at[0])
    w_copy = pltpu.make_async_copy(w_hbm, w_ref, sems.at[1])
    basis_copy.start()
    w_copy.start()
    q = basis_hbm.shape[0]
    cols = LANES
    near = near_ref[...]
    left = pltpu.roll(left_ref[...], cols - rows, axis=1)
    right = pltpu.roll(right_ref[...], rows, axis=1)
    lane = lax.broadcasted_iota(jnp.int32, near.shape, 1)
    earlier = jnp.where(lane < rows, left, near)
    later = jnp.where(lane < rows, near, right)
    pairs = ((up_ref[...], first_ref[...]), (last_ref[...], down_ref[...]), (earlier, later))
    for k, (e, l) in enumerate(pairs):
        span = pl.ds(k * cols, cols)
        diff = l[0:p] - e[0:p]
        if k < 2:
            diff = diff * open_ref[k]
        else:
            low = lane[0:p] < rows
            diff = jnp.where(low, diff * open_ref[2], diff * open_ref[3])
            diff = jnp.where(lane[0:p] < 2 * rows, diff, 0.0)
        put_cat(du_ref, span, diff)
        put_cat(le_ref, span, e[p : p + SLOT])
        put_cat(ll_ref, span, l[p : p + SLOT])

    def values(i):
        return jnp.dot(
            basis_ref[pl.ds(i * PIECE, PIECE), :], du_ref[...], preferred_element_type=jnp.float32
        )

    def total(i):
        germ = germ_ref[pl.ds(i * PIECE, PIECE), :]
        e = jnp.exp2(jnp.dot(germ, le_ref[...], preferred_element_type=jnp.float32))
        return e + jnp.exp2(jnp.dot(germ, ll_ref[...], preferred_element_type=jnp.float32))

    def project(i, parts):
        top, low = parts
        at = pl.ds(i * PIECE, PIECE)
        both = jnp.dot(w_ref[:, at], top, preferred_element_type=jnp.float32)
        rest = jnp.dot(w_ref[0:p, at], low, preferred_element_type=jnp.float32)
        return both[0:p] + both[p : 2 * p] + rest

    basis_copy.wait()
    w_copy.wait()
    steps = q // PIECE
    value, sums = values(0), total(0)
    flux, waiting = None, None
    for i in range(steps):
        later = (values(i + 1), total(i + 1)) if i + 1 < steps else (None, None)
        parts = split(value / sums)
        if waiting is not None:
            term = project(*waiting)
            flux = term if flux is None else flux + term
        waiting = (i, parts)
        value, sums = later
    flux = flux + project(*waiting)

    sub = p // out_ref.shape[0]
    for d in range(out_ref.shape[0]):
        span = slice(d * sub, (d + 1) * sub)
        out_ref[d, 0:sub, :] = flux[span, 0:cols]
        out_ref[d, sub : 2 * sub, :] = flux[span, cols : 2 * cols]
        out_ref[d, 2 * sub : 3 * sub, :] = flux[span, 2 * cols : 3 * cols]
        out_ref[d, 3 * sub : SLOT, :] = jnp.zeros((SLOT - 3 * sub, cols), jnp.float32)


def outer_fluxes(rows, parts, opened, rims, halos, basis_cat, weight_cat, germ_cat):
    q, cols = basis_cat.shape[0], LANES
    p = weight_cat.shape[0] // 2
    vmem, hbm = (pl.BlockSpec(memory_space=space) for space in (pltpu.VMEM, pltpu.HBM))
    return pl.pallas_call(
        functools.partial(outer_kernel, rows),
        in_specs=[pl.BlockSpec(memory_space=pltpu.SMEM)] + [vmem] * 7 + [hbm, vmem, hbm],
        out_shape=jax.ShapeDtypeStruct((parts, SLOT, cols), jnp.float32),
        scratch_shapes=[
            pltpu.VMEM((3 * p, 3 * cols), jnp.bfloat16),
            pltpu.VMEM((3 * SLOT, 3 * cols), jnp.bfloat16),
            pltpu.VMEM((3 * SLOT, 3 * cols), jnp.bfloat16),
            pltpu.VMEM(basis_cat.shape, basis_cat.dtype),
            pltpu.VMEM(weight_cat.shape, weight_cat.dtype),
            pltpu.SemaphoreType.DMA((2,)),
        ],
        compiler_params=pltpu.CompilerParams(vmem_limit_bytes=VMEM_GRANT),
        cost_estimate=pl.CostEstimate(
            flops=2 * q * 3 * cols * p * 6, bytes_accessed=4 << 20, transcendentals=q * 6 * cols
        ),
        name="outer_fluxes",
    )(opened, *rims, *halos, basis_cat, germ_cat, weight_cat)


def local_kernel(
    nsa, place_ref, part_ref, rim_ref, s0_ref, s1_ref, s2_ref, s3_ref, cy_ref, cxt_ref, side_of_ref,
    ends_of_ref, recip_ref, coef_ref, scaled_ref, jump_ref, res_ref,
):
    modes, length, cols = s0_ref.shape
    rows = part_ref.shape[2]
    ngy = 4
    ny = ngy * length
    row = lax.broadcasted_iota(jnp.int32, (rows, cols), 0)
    lane = lax.broadcasted_iota(jnp.int32, (rows, cols), 1)
    own = (lane == row) | (lane == rows + row)
    first_row, last_row = row == 0, row == rows - 1
    for g in range(ngy):
        sides = jnp.concatenate(
            [
                jnp.where(own, rim_ref[s * ngy + g, 2 * modes + m : 2 * modes + m + 1, :], 0.0)
                for s in range(nsa)
                for m in range(modes)
            ],
            axis=0,
        )
        sides = jnp.dot(sides, side_of_ref[...], precision=HIGHEST, preferred_element_type=jnp.float32)
        for s in range(nsa):
            for m in range(modes):
                block = s * ngy + g
                at = (s * modes + m) * rows
                gain = part_ref[block, m] + sides[at : at + rows]
                gain = gain + jnp.where(first_row, rim_ref[block, m : m + 1, :], 0.0)
                gain = gain - jnp.where(last_row, rim_ref[block, modes + m : modes + m + 1, :], 0.0)
                res_ref[pl.ds(g * length + s * rows, rows), pl.ds(m * cols, cols)] = gain
    for d, src_ref in enumerate((s0_ref, s1_ref, s2_ref, s3_ref)):
        g = lax.rem(place_ref[0] + ngy - d, ngy)
        span = pl.ds(pl.multiple_of(g * length, 8), length)
        for m in range(modes):
            at = pl.ds(m * cols, cols)
            res_ref[span, at] = src_ref[m] - res_ref[span, at]
    spectral = jnp.dot(cy_ref[...], res_ref[...], precision=HIGHEST, preferred_element_type=jnp.float32)
    spectral = jnp.concatenate([spectral[:, m * cols : (m + 1) * cols] for m in range(modes)], axis=0)
    spectral = jnp.dot(spectral, cxt_ref[...], precision=HIGHEST, preferred_element_type=jnp.float32)
    recip = recip_ref[...]
    scaled = jnp.concatenate(
        [recip * spectral[m * ny : (m + 1) * ny] for m in range(modes)], axis=0
    )
    both = lax.dot_general(
        ends_of_ref[...], scaled, (((1,), (1,)), ((), ())),
        precision=HIGHEST, preferred_element_type=jnp.float32,
    )
    pad = [jnp.zeros((8 - modes, ny), jnp.float32)]
    first = jnp.concatenate([both[0:1, m * ny : (m + 1) * ny] for m in range(modes)] + pad, axis=0)
    last = jnp.concatenate([both[1:2, m * ny : (m + 1) * ny] for m in range(modes)] + pad, axis=0)
    blocks = jump_ref.shape[0]
    for i in range(blocks + 1):
        term = coef_ref[0, i : i + 1, :] * first + coef_ref[1, i : i + 1, :] * last
        if i < blocks:
            jump_ref[i, 0:8, :] = term
        if i > 0:
            jump_ref[i - 1, 8:16, :] = term
    scaled_ref[...] = scaled


def back_kernel(scaled_ref, cx_ref, z_ref):
    z_ref[...] = jnp.dot(
        scaled_ref[...], cx_ref[...], precision=HIGHEST, preferred_element_type=jnp.float32
    )


def joined_kernel(z_ref, jump_ref, g_first_ref, g_last_ref, cyt_ref, out_ref):
    blocks = jump_ref.shape[0]
    ngy, modes = out_ref.shape[:2]
    ny, cols = g_first_ref.shape
    length = ny // ngy
    total = jump_ref[0]
    for i in range(1, blocks):
        total = total + jump_ref[i]
    both = jnp.concatenate([total, jnp.zeros((LANES - 16, ny), jnp.float32)], axis=0).T
    x = jnp.concatenate(
        [
            z_ref[m * ny : (m + 1) * ny]
            + g_first_ref[...] * both[:, m : m + 1]
            - g_last_ref[...] * both[:, 8 + m : 9 + m]
            for m in range(modes)
        ],
        axis=1,
    )
    out = jnp.dot(cyt_ref[...], x, precision=HIGHEST, preferred_element_type=jnp.float32)
    for g in range(ngy):
        for m in range(modes):
            out_ref[g, m] = out[g * length : (g + 1) * length, m * cols : (m + 1) * cols]


def solve_tables(mean_perm, ny, cols, blocks, position):
    cx = cosine_matrix(cols)
    lam_y = jnp.asarray(eigen_values(ny, ny), jnp.float32)
    lam_x = jnp.asarray(eigen_values(cols, cols), jnp.float32)
    recip = 1.0 / (storage_rate + mean_perm * (lam_y[:, None] + lam_x[None, :]))
    first = jnp.asarray(cx[:, 0][:, None] * cx, jnp.float32)
    last = jnp.asarray(cx[:, -1][:, None] * cx, jnp.float32)
    g_first = jnp.dot(recip, first, precision=HIGHEST)
    g_last = jnp.dot(recip, last, precision=HIGHEST)
    k = np.arange(1, blocks)
    sine = math.sqrt(2.0 / blocks) * np.sin(np.pi * np.outer(np.arange(0, blocks + 1), k) / blocks)
    sine[0] = 0.0
    sine[blocks] = 0.0
    theta = jnp.asarray(2.0 * np.cos(np.pi * k / blocks), jnp.float32)
    spread = 1.0 / (
        1.0 / mean_perm + g_first[:, 0:1] + g_last[:, cols - 1 : cols] - g_first[:, cols - 1 : cols] * theta
    )
    table = jnp.asarray(sine, jnp.float32)
    coef = []
    for end, sign in ((0, -1.0), (1, 1.0)):
        mine = sign * lax.dynamic_slice_in_dim(table, position + end, 1, axis=0)
        coef.append(jnp.einsum("ik,jk->ij", table, spread * mine, precision=HIGHEST))
    return recip, g_first, g_last, jnp.stack(coef)


def rotated(x, axis, by):
    count = lax.axis_size(axis)
    return lax.ppermute(x, axis, [(i, (i + by) % count) for i in range(count)])


def row_blocks_kernel(x_ref, out_ref, sems):
    blocks, _, rows, _ = out_ref.shape
    copies = [
        pltpu.make_async_copy(x_ref.at[:, pl.ds(k * rows, rows), :], out_ref.at[k], sems.at[k])
        for k in range(blocks)
    ]
    for copy in copies:
        copy.start()
    for copy in copies:
        copy.wait()


def row_blocks(x, blocks):
    modes, length, cols = x.shape
    anywhere = pl.BlockSpec(memory_space=pl.ANY)
    return pl.pallas_call(
        row_blocks_kernel,
        in_specs=[anywhere],
        out_specs=anywhere,
        out_shape=jax.ShapeDtypeStruct((blocks, modes, length // blocks, cols), x.dtype),
        scratch_shapes=[pltpu.SemaphoreType.DMA((blocks,))],
        name="row_blocks",
    )(x)


def relaxed_kernel(now_ref, before_ref, update_ref, fresh_ref, out_ref):
    update = update_ref[...]
    before = before_ref[...]
    fresh_ref[...] = before + relax_weight * (now_ref[...] - before + step_length * update)
    out_ref[...] = update


def relaxed(now, before, update):
    modes, length, cols = now.shape
    block = pl.BlockSpec((modes // 4, length, cols), lambda i: (i, 0, 0))
    shape = jax.ShapeDtypeStruct(now.shape, now.dtype)
    return pl.pallas_call(
        relaxed_kernel,
        grid=(4,),
        in_specs=[block] * 3,
        out_specs=[block] * 2,
        out_shape=[shape] * 2,
        name="relaxed",
    )(now, before, update)


def on_device(
    field_now, field_before, source, log_fields, weights, mean_perm, node_index, mode_index
):
    nsa, ngy, ngx = (lax.axis_size(a) for a in ("sa", "gy", "gx"))
    modes, length, cols = field_now.shape
    rows = length // nsa
    p = modes * nsa
    ny = length * ngy
    sub = modes // ngy
    fields = log_fields.shape[0]

    outgoing = row_blocks(field_now, nsa)
    field = lax.all_to_all(outgoing, "sa", 0, 0, tiled=True).reshape(p * rows, cols)

    place = lax.axis_index("gy")
    blocks = source.reshape(ngy, sub, length, cols)
    pieces = [lax.dynamic_index_in_dim(blocks, (place + d) % ngy, 0, keepdims=False) for d in range(ngy)]
    pieces = pieces[:1] + [rotated(pieces[d], "gy", d) for d in range(1, ngy)]

    basis_cat, weight_cat, germ_cat, mass_cat = node_tables(node_index, mode_index, weights)
    recip, g_first, g_last, coef = solve_tables(mean_perm, ny, cols, ngx, lax.axis_index("gx"))

    row_axis = ("gy", "sa")
    row_index = lax.axis_index(row_axis)
    col_index = lax.axis_index("gx")
    opened = jnp.stack(
        [row_index > 0, row_index < ngy * nsa - 1, col_index > 0, col_index < ngx - 1]
    ).astype(jnp.float32)
    scaled_logs = jnp.pad(
        log_fields * jnp.float32(-math.log2(math.e)), ((0, SLOT - fields), (0, 0), (0, 0))
    )
    top, low = halves(scaled_logs.reshape(SLOT, rows * cols))
    logs = jnp.concatenate([top, low, top], axis=0)

    field, *pieces = lax.optimization_barrier((field, *pieces))
    inner = inner_fluxes(rows, field, logs, basis_cat, weight_cat, germ_cat, mass_cat)
    field, inner = lax.optimization_barrier((field, inner))
    part = lax.all_to_all(inner.reshape(nsa * ngy, sub, rows, cols), ("sa", "gy"), 0, 0, tiled=True)
    rims = rim_of(rows, field, scaled_logs.reshape(SLOT * rows, cols))
    first, last, near = rims
    halos = (
        rotated(last, row_axis, 1),
        rotated(first, row_axis, -1),
        rotated(near, "gx", 1),
        rotated(near, "gx", -1),
    )
    outer = outer_fluxes(rows, nsa * ngy, opened, rims, halos, basis_cat, weight_cat, germ_cat)
    outer, part = lax.optimization_barrier((outer, part))
    rim_part = lax.all_to_all(outer, ("sa", "gy"), 0, 0, tiled=True)

    cy = cosine_matrix(ny)
    cx = cosine_matrix(cols)
    ends_of = np.zeros((8, cols))
    ends_of[0], ends_of[1] = cx[:, 0], cx[:, -1]
    side_of = np.zeros((cols, cols))
    side_of[:rows, 0] = 1.0
    side_of[rows : 2 * rows, -1] = -1.0
    f32 = functools.partial(jnp.asarray, dtype=jnp.float32)
    params = pltpu.CompilerParams(vmem_limit_bytes=VMEM_GRANT)
    vmem = pl.BlockSpec(memory_space=pltpu.VMEM)
    scaled, jumps = pl.pallas_call(
        functools.partial(local_kernel, nsa),
        in_specs=[pl.BlockSpec(memory_space=pltpu.SMEM)] + [vmem] * 12,
        out_shape=(
            jax.ShapeDtypeStruct((sub * ny, cols), jnp.float32),
            jax.ShapeDtypeStruct((ngx, 16, ny), jnp.float32),
        ),
        scratch_shapes=[pltpu.VMEM((ny, sub * cols), jnp.float32)],
        compiler_params=params,
        name="local_solve",
    )(place[None], part, rim_part, *pieces, f32(cy), f32(cx.T), f32(side_of), f32(ends_of), recip, coef)
    jumps = lax.all_to_all(jumps, "gx", 0, 0, tiled=True)
    z = pl.pallas_call(
        back_kernel,
        out_shape=jax.ShapeDtypeStruct((sub * ny, cols), jnp.float32),
        compiler_params=params,
        cost_estimate=pl.CostEstimate(
            flops=12 * sub * ny * cols * cols, bytes_accessed=2 << 20, transcendentals=0
        ),
        name="back",
    )(scaled, f32(cx))
    columns = pl.pallas_call(
        joined_kernel,
        out_shape=jax.ShapeDtypeStruct((ngy, sub, length, cols), jnp.float32),
        compiler_params=params,
        name="joined_solve",
    )(z, jumps, g_first, g_last, f32(cy.T))
    update = lax.all_to_all(columns, "gy", 0, 0, tiled=True).reshape(modes, length, cols)
    fresh, update = relaxed(field_now, field_before, update)
    return (fresh, update)


def solution(mesh):
    block = P("sa", "gy", "gx")
    in_specs = (block, block, block, P(None, ("gy", "sa"), "gx"), P(), P(), P(), P())
    return jax.shard_map(
        on_device, mesh=mesh, in_specs=in_specs, out_specs=(block, block), check_vma=False
    )
```

```python
import functools
import math

import jax
import jax.numpy as jnp
import numpy as np
from jax import lax
from jax.experimental import pallas as pl
from jax.experimental.pallas import tpu as pltpu
from jax.sharding import PartitionSpec as P

HIGHEST = lax.Precision.HIGHEST
hermite_points = (
    0.0,
    -1.7320508075688772,
    1.7320508075688772,
    -1.355626179974266,
    1.355626179974266,
    -2.8569700138728056,
    2.8569700138728056,
)
storage_rate = 0.0004
relax_weight = 1.6
step_length = 0.3
QB = 256
LANES = 128


def halves(x):
    top = lax.reduce_precision(x, 8, 7)
    return top.astype(jnp.bfloat16), (x - top).astype(jnp.bfloat16)


def split(x):
    top = x.astype(jnp.bfloat16)
    return top, (x - top.astype(jnp.float32)).astype(jnp.bfloat16)


def cosine_matrix(length):
    k = np.arange(length)[:, None]
    m = np.arange(length)[None, :]
    phase = (k * (2 * m + 1)) % (4 * length)
    factor = np.where(k == 0, math.sqrt(1.0 / length), math.sqrt(2.0 / length))
    return factor * np.cos(phase * (math.pi / (2 * length)))


def eigen_values(count, length):
    return 4.0 * np.sin(np.arange(count) * (math.pi / (2 * length))) ** 2


SLOT = 16
PIECE = 384


def tables_kernel(index_ref, mode_ref, weight_ref, basis_ref, w_ref, germ_ref, mass_ref, sum_ref):
    germs, q = index_ref.shape
    p = mode_ref.shape[0]
    step = pl.program_id(0)
    index = index_ref[...]
    germ = jnp.zeros((germs, q), jnp.float32)
    for level, point in enumerate(hermite_points):
        germ = jnp.where(index == level, jnp.float32(point), germ)
    square = germ * germ
    h2 = (square - 1.0) / math.sqrt(2.0)
    h3 = (square * germ - 3.0 * germ) / math.sqrt(6.0)
    basis = jnp.ones((p, q), jnp.float32)
    for i in range(germs):
        degree = mode_ref[:, i : i + 1]
        factor = jnp.where(
            degree == 1,
            germ[i : i + 1],
            jnp.where(degree == 2, h2[i : i + 1], jnp.where(degree == 3, h3[i : i + 1], 1.0)),
        )
        basis = basis * factor
    weighted = basis * weight_ref[...]
    w_ref[0:p, :], w_ref[p : 2 * p, :] = split(2.0 * weighted)
    top, low = split(basis.T)
    basis_ref[:, 0:p] = top
    basis_ref[:, p : 2 * p] = top
    basis_ref[:, 2 * p : 3 * p] = low
    full = jnp.concatenate(
        [jnp.ones((8, q), jnp.float32), germ, jnp.zeros((LANES - 16, q), jnp.float32)], axis=0
    )
    top, low = split(full.T[:, 7 : 7 + SLOT])
    lane = lax.broadcasted_iota(jnp.int32, (q, SLOT), 1)
    keep = lane < germs + 1
    top = jnp.where(keep, top.astype(jnp.float32), 0.0).astype(jnp.bfloat16)
    low = jnp.where(keep, low.astype(jnp.float32), 0.0).astype(jnp.bfloat16)
    germ_ref[:, 0:SLOT] = top
    germ_ref[:, SLOT : 2 * SLOT] = top
    germ_ref[:, 2 * SLOT : 3 * SLOT] = low

    @pl.when(step == 0)
    def _():
        sum_ref[...] = jnp.zeros_like(sum_ref)

    sum_ref[...] += lax.dot_general(
        storage_rate * weighted, basis, (((1,), (1,)), ((), ())),
        precision=HIGHEST, preferred_element_type=jnp.float32,
    )

    @pl.when(step == pl.num_programs(0) - 1)
    def _():
        top, low = split(sum_ref[...])
        mass_ref[:, 0:p] = top
        mass_ref[:, p : 2 * p] = top
        mass_ref[:, 2 * p : 3 * p] = low


def node_tables(node_index, mode_index, weights):
    q, germs = node_index.shape
    p = mode_index.shape[0]
    pad = -q % QB
    index = jnp.pad(node_index.T, ((0, 0), (0, pad)))
    weights = jnp.pad(weights, (0, pad))[None]
    return pl.pallas_call(
        tables_kernel,
        grid=((q + pad) // QB,),
        in_specs=[
            pl.BlockSpec((germs, QB), lambda i: (0, i)),
            whole((p, germs)),
            pl.BlockSpec((1, QB), lambda i: (0, i)),
        ],
        out_specs=[
            pl.BlockSpec((QB, 3 * p), lambda i: (i, 0)),
            pl.BlockSpec((2 * p, QB), lambda i: (0, i)),
            pl.BlockSpec((QB, 3 * SLOT), lambda i: (i, 0)),
            whole((p, 3 * p)),
        ],
        out_shape=[
            jax.ShapeDtypeStruct((q + pad, 3 * p), jnp.bfloat16),
            jax.ShapeDtypeStruct((2 * p, q + pad), jnp.bfloat16),
            jax.ShapeDtypeStruct((q + pad, 3 * SLOT), jnp.bfloat16),
            jax.ShapeDtypeStruct((p, 3 * p), jnp.bfloat16),
        ],
        scratch_shapes=[pltpu.VMEM((p, p), jnp.float32)],
        compiler_params=pltpu.CompilerParams(vmem_limit_bytes=20 << 20),
        name="node_tables",
    )(index, mode_index, weights)


def whole(shape):
    return pl.BlockSpec(shape, lambda *_: (0,) * len(shape))


def rim_kernel(rows, u_ref, log_ref, first_ref, last_ref, near_ref):
    start = 0
    for ref in (u_ref, log_ref):
        n = ref.shape[0] // rows
        span = slice(start, start + n)
        lane = lax.broadcasted_iota(jnp.int32, (n, LANES), 1)
        near = jnp.zeros((n, LANES), jnp.float32)
        for y in range(rows):
            here = ref[pl.ds(y, n, stride=rows), :]
            if y == 0:
                first_ref[span] = here
            if y == rows - 1:
                last_ref[span] = here
            near = jnp.where(lane == y, here[:, 0:1], near)
            near = jnp.where(lane == rows + y, here[:, LANES - 1 : LANES], near)
        near_ref[span] = near
        start += n


def rim_of(rows, field, logs):
    n = (field.shape[0] + logs.shape[0]) // rows
    return pl.pallas_call(
        functools.partial(rim_kernel, rows),
        out_shape=[jax.ShapeDtypeStruct((n, LANES), jnp.float32)] * 3,
        compiler_params=pltpu.CompilerParams(vmem_limit_bytes=20 << 20),
        name="rim_of",
    )(field, logs)


def put_cat(ref, lanes, x):
    p = x.shape[0]
    top, low = split(x)
    ref[0:p, lanes] = top
    ref[p : 2 * p, lanes] = low
    ref[2 * p : 3 * p, lanes] = top


def projected(w_ref, parts):
    p = w_ref.shape[0] // 2
    top, low = parts
    both = jnp.dot(w_ref[...], top, preferred_element_type=jnp.float32)
    rest = jnp.dot(w_ref[0:p, :], low, preferred_element_type=jnp.float32)
    return both[0:p] + both[p : 2 * p] + rest


def resistance(germ_ref, log):
    return jnp.exp2(jnp.dot(germ_ref[...], log, preferred_element_type=jnp.float32))


def inner_kernel(rows, u_ref, log_ref, basis_ref, germ_ref, w_ref, mass_ref, g_ref, u_cat_ref, du_ref, r_ref, f_ref):
    p = mass_ref.shape[0]
    cols = LANES
    lane = lax.broadcasted_iota(jnp.int32, (p, cols), 1)
    above = None
    for y in range(rows):
        here = u_ref[pl.ds(y, p, stride=rows), :]
        put_cat(u_cat_ref, pl.ds(y * cols, cols), here)
        ahead = pltpu.roll(here, cols - 1, axis=1)
        put_cat(du_ref, pl.ds(y * cols, cols), jnp.where(lane == cols - 1, 0.0, ahead - here))
        if y > 0:
            put_cat(du_ref, pl.ds((rows + y - 1) * cols, cols), here - above)
        above = here

    chunks = [("x", y, 2) for y in range(0, rows, 2)]
    chunks += [("y", y, min(2, rows - 1 - y)) for y in range(0, rows - 1, 2)]

    def lanes(chunk):
        kind, y, n = chunk
        return pl.ds((y if kind == "x" else rows + y) * cols, n * cols)

    def values(chunk):
        return jnp.dot(basis_ref[...], du_ref[:, lanes(chunk)], preferred_element_type=jnp.float32)

    def total(chunk):
        kind, y, n = chunk
        if kind == "y":
            return r_ref[:, pl.ds(y * cols, n * cols)] + r_ref[:, pl.ds((y + 1) * cols, n * cols)]
        sums = []
        for k in range(n):
            r = r_ref[:, pl.ds((y + k) * cols, cols)]
            sums.append(r + pltpu.roll(r, cols - 1, axis=1))
        return jnp.concatenate(sums, axis=1)

    def fill(y):
        span = pl.ds(y * cols, 2 * cols)
        r_ref[:, span] = resistance(germ_ref, log_ref[:, span])

    fill(0)
    value = values(chunks[0])
    waiting = None
    for i, chunk in enumerate(chunks):
        later = values(chunks[i + 1]) if i + 1 < len(chunks) else None
        if 2 * (i + 1) < rows:
            fill(2 * (i + 1))
        parts = split(value / total(chunk))
        if waiting is not None:
            f_ref[:, lanes(waiting[0])] = projected(w_ref, waiting[1])
        waiting = (chunk, parts)
        value = later
    stored = [
        jnp.dot(mass_ref[...], u_cat_ref[:, pl.ds(y * cols, 2 * cols)], preferred_element_type=jnp.float32)
        for y in range(0, rows, 2)
    ]
    f_ref[:, lanes(waiting[0])] = projected(w_ref, waiting[1])

    for y in range(rows):
        out = stored[y // 2][:, (y % 2) * cols : (y % 2 + 1) * cols]
        later = f_ref[:, pl.ds(y * cols, cols)]
        earlier = jnp.where(lane == 0, 0.0, pltpu.roll(later, 1, axis=1))
        later = jnp.where(lane == cols - 1, 0.0, later)
        out = out - (later - earlier)
        if y < rows - 1:
            out = out - f_ref[:, pl.ds((rows + y) * cols, cols)]
        if y > 0:
            out = out + f_ref[:, pl.ds((rows + y - 1) * cols, cols)]
        g_ref[y] = out


def inner_fluxes(rows, field, logs, basis_cat, weight_cat, germ_cat, mass_cat):
    p, cols = field.shape[0] // rows, field.shape[1]
    q = basis_cat.shape[0]
    faces = (2 * rows - 1) * cols
    return pl.pallas_call(
        functools.partial(inner_kernel, rows),
        out_shape=jax.ShapeDtypeStruct((rows, p, cols), jnp.float32),
        scratch_shapes=[
            pltpu.VMEM((3 * p, rows * cols), jnp.bfloat16),
            pltpu.VMEM((3 * p, faces), jnp.bfloat16),
            pltpu.VMEM((q, rows * cols), jnp.float32),
            pltpu.VMEM((p, faces), jnp.float32),
        ],
        compiler_params=pltpu.CompilerParams(vmem_limit_bytes=50 << 20),
        cost_estimate=pl.CostEstimate(
            flops=2 * q * faces * p * 6, bytes_accessed=8 << 20, transcendentals=q * rows * cols
        ),
        name="inner_fluxes",
    )(field, logs, basis_cat, germ_cat, weight_cat, mass_cat)


def outer_kernel(
    rows, open_ref, g_ref, first_ref, last_ref, near_ref, up_ref, down_ref,
    left_ref, right_ref, basis_ref, germ_ref, w_ref, out_ref, du_ref, le_ref, ll_ref,
):
    p = w_ref.shape[0] // 2
    q = basis_ref.shape[0]
    cols = LANES
    near = near_ref[...]
    left = pltpu.roll(left_ref[...], cols - rows, axis=1)
    right = pltpu.roll(right_ref[...], rows, axis=1)
    lane = lax.broadcasted_iota(jnp.int32, near.shape, 1)
    earlier = jnp.where(lane < rows, left, near)
    later = jnp.where(lane < rows, near, right)
    pairs = ((up_ref[...], first_ref[...]), (last_ref[...], down_ref[...]), (earlier, later))
    for k, (e, l) in enumerate(pairs):
        span = pl.ds(k * cols, cols)
        diff = l[0:p] - e[0:p]
        if k < 2:
            diff = diff * open_ref[k]
        else:
            low = lane[0:p] < rows
            diff = jnp.where(low, diff * open_ref[2], diff * open_ref[3])
            diff = jnp.where(lane[0:p] < 2 * rows, diff, 0.0)
        put_cat(du_ref, span, diff)
        put_cat(le_ref, span, e[p : p + SLOT])
        put_cat(ll_ref, span, l[p : p + SLOT])

    def values(i):
        return jnp.dot(
            basis_ref[pl.ds(i * PIECE, PIECE), :], du_ref[...], preferred_element_type=jnp.float32
        )

    def total(i):
        germ = germ_ref[pl.ds(i * PIECE, PIECE), :]
        e = jnp.exp2(jnp.dot(germ, le_ref[...], preferred_element_type=jnp.float32))
        return e + jnp.exp2(jnp.dot(germ, ll_ref[...], preferred_element_type=jnp.float32))

    def project(i, parts):
        top, low = parts
        at = pl.ds(i * PIECE, PIECE)
        both = jnp.dot(w_ref[:, at], top, preferred_element_type=jnp.float32)
        rest = jnp.dot(w_ref[0:p, at], low, preferred_element_type=jnp.float32)
        return both[0:p] + both[p : 2 * p] + rest

    steps = q // PIECE
    value, sums = values(0), total(0)
    flux, waiting = None, None
    for i in range(steps):
        later = (values(i + 1), total(i + 1)) if i + 1 < steps else (None, None)
        parts = split(value / sums)
        if waiting is not None:
            term = project(*waiting)
            flux = term if flux is None else flux + term
        waiting = (i, parts)
        value, sums = later
    flux = flux + project(*waiting)

    lane = lax.broadcasted_iota(jnp.int32, (p, cols), 1)
    for y in range(rows):
        out = g_ref[y]
        if y == 0:
            out = out + flux[:, 0:cols]
        if y == rows - 1:
            out = out - flux[:, cols : 2 * cols]
        out = out + jnp.where(lane == 0, flux[:, 2 * cols + y : 2 * cols + y + 1], 0.0)
        at = 2 * cols + rows + y
        out = out - jnp.where(lane == cols - 1, flux[:, at : at + 1], 0.0)
        out_ref[pl.ds(y, p, stride=rows), :] = out


def outer_fluxes(rows, opened, inner, rims, halos, basis_cat, weight_cat, germ_cat):
    p, cols = inner.shape[1:]
    q = basis_cat.shape[0]
    vmem = pl.BlockSpec(memory_space=pltpu.VMEM)
    return pl.pallas_call(
        functools.partial(outer_kernel, rows),
        in_specs=[pl.BlockSpec(memory_space=pltpu.SMEM)] + [vmem] * 11,
        out_shape=jax.ShapeDtypeStruct((p * rows, cols), jnp.float32),
        scratch_shapes=[
            pltpu.VMEM((3 * p, 3 * cols), jnp.bfloat16),
            pltpu.VMEM((3 * SLOT, 3 * cols), jnp.bfloat16),
            pltpu.VMEM((3 * SLOT, 3 * cols), jnp.bfloat16),
        ],
        compiler_params=pltpu.CompilerParams(vmem_limit_bytes=50 << 20),
        cost_estimate=pl.CostEstimate(
            flops=2 * q * 3 * cols * p * 6, bytes_accessed=8 << 20, transcendentals=q * 6 * cols
        ),
        name="outer_fluxes",
    )(opened, inner, *rims, *halos, basis_cat, germ_cat, weight_cat)


def local_kernel(
    nsa, place_ref, part_ref, s0_ref, s1_ref, s2_ref, s3_ref, cy_ref, cxt_ref, ends_of_ref,
    recip_ref, coef_ref, scaled_ref, jump_ref, res_ref,
):
    modes, length, cols = s0_ref.shape
    rows = part_ref.shape[2]
    ngy = 4
    ny = ngy * length
    for d, src_ref in enumerate((s0_ref, s1_ref, s2_ref, s3_ref)):
        g = lax.rem(place_ref[0] + ngy - d, ngy)
        for s in range(nsa):
            span = pl.ds(pl.multiple_of(g * length + s * rows, 8), rows)
            for m in range(modes):
                res_ref[span, pl.ds(m * cols, cols)] = (
                    src_ref[m, pl.ds(s * rows, rows), :] - part_ref[s * ngy + g, m]
                )
    spectral = jnp.dot(cy_ref[...], res_ref[...], precision=HIGHEST, preferred_element_type=jnp.float32)
    spectral = jnp.concatenate([spectral[:, m * cols : (m + 1) * cols] for m in range(modes)], axis=0)
    spectral = jnp.dot(spectral, cxt_ref[...], precision=HIGHEST, preferred_element_type=jnp.float32)
    recip = recip_ref[...]
    scaled = jnp.concatenate(
        [recip * spectral[m * ny : (m + 1) * ny] for m in range(modes)], axis=0
    )
    both = lax.dot_general(
        ends_of_ref[...], scaled, (((1,), (1,)), ((), ())),
        precision=HIGHEST, preferred_element_type=jnp.float32,
    )
    pad = [jnp.zeros((8 - modes, ny), jnp.float32)]
    first = jnp.concatenate([both[0:1, m * ny : (m + 1) * ny] for m in range(modes)] + pad, axis=0)
    last = jnp.concatenate([both[1:2, m * ny : (m + 1) * ny] for m in range(modes)] + pad, axis=0)
    blocks = jump_ref.shape[0]
    for i in range(blocks + 1):
        term = coef_ref[0, i : i + 1, :] * first + coef_ref[1, i : i + 1, :] * last
        if i < blocks:
            jump_ref[i, 0:8, :] = term
        if i > 0:
            jump_ref[i - 1, 8:16, :] = term
    scaled_ref[...] = scaled


def back_kernel(scaled_ref, cx_ref, z_ref):
    z_ref[...] = jnp.dot(
        scaled_ref[...], cx_ref[...], precision=HIGHEST, preferred_element_type=jnp.float32
    )


def joined_kernel(z_ref, jump_ref, g_first_ref, g_last_ref, cyt_ref, out_ref):
    blocks = jump_ref.shape[0]
    ngy, modes = out_ref.shape[:2]
    ny, cols = g_first_ref.shape
    length = ny // ngy
    total = jump_ref[0]
    for i in range(1, blocks):
        total = total + jump_ref[i]
    both = jnp.concatenate([total, jnp.zeros((LANES - 16, ny), jnp.float32)], axis=0).T
    x = jnp.concatenate(
        [
            z_ref[m * ny : (m + 1) * ny]
            + g_first_ref[...] * both[:, m : m + 1]
            - g_last_ref[...] * both[:, 8 + m : 9 + m]
            for m in range(modes)
        ],
        axis=1,
    )
    out = jnp.dot(cyt_ref[...], x, precision=HIGHEST, preferred_element_type=jnp.float32)
    for g in range(ngy):
        for m in range(modes):
            out_ref[g, m] = out[g * length : (g + 1) * length, m * cols : (m + 1) * cols]


def solve_tables(mean_perm, ny, cols, blocks, position):
    cx = cosine_matrix(cols)
    lam_y = jnp.asarray(eigen_values(ny, ny), jnp.float32)
    lam_x = jnp.asarray(eigen_values(cols, cols), jnp.float32)
    recip = 1.0 / (storage_rate + mean_perm * (lam_y[:, None] + lam_x[None, :]))
    first = jnp.asarray(cx[:, 0][:, None] * cx, jnp.float32)
    last = jnp.asarray(cx[:, -1][:, None] * cx, jnp.float32)
    g_first = jnp.dot(recip, first, precision=HIGHEST)
    g_last = jnp.dot(recip, last, precision=HIGHEST)
    k = np.arange(1, blocks)
    sine = math.sqrt(2.0 / blocks) * np.sin(np.pi * np.outer(np.arange(0, blocks + 1), k) / blocks)
    sine[0] = 0.0
    sine[blocks] = 0.0
    theta = jnp.asarray(2.0 * np.cos(np.pi * k / blocks), jnp.float32)
    spread = 1.0 / (
        1.0 / mean_perm + g_first[:, 0:1] + g_last[:, cols - 1 : cols] - g_first[:, cols - 1 : cols] * theta
    )
    table = jnp.asarray(sine, jnp.float32)
    coef = []
    for end, sign in ((0, -1.0), (1, 1.0)):
        mine = sign * lax.dynamic_slice_in_dim(table, position + end, 1, axis=0)
        coef.append(jnp.einsum("ik,jk->ij", table, spread * mine, precision=HIGHEST))
    return recip, g_first, g_last, jnp.stack(coef)


def rotated(x, axis, by):
    count = lax.axis_size(axis)
    return lax.ppermute(x, axis, [(i, (i + by) % count) for i in range(count)])


def on_device(
    field_now, field_before, source, log_fields, weights, mean_perm, node_index, mode_index
):
    nsa, ngy, ngx = (lax.axis_size(a) for a in ("sa", "gy", "gx"))
    modes, length, cols = field_now.shape
    rows = length // nsa
    p = modes * nsa
    ny = length * ngy
    sub = modes // ngy
    fields = log_fields.shape[0]

    outgoing = field_now.reshape(modes, nsa, rows, cols).transpose(1, 0, 2, 3)
    field = lax.all_to_all(outgoing, "sa", 0, 0, tiled=True).reshape(p * rows, cols)

    place = lax.axis_index("gy")
    blocks = source.reshape(ngy, sub, length, cols)
    pieces = [lax.dynamic_index_in_dim(blocks, (place + d) % ngy, 0, keepdims=False) for d in range(ngy)]
    pieces = pieces[:1] + [rotated(pieces[d], "gy", d) for d in range(1, ngy)]

    basis_cat, weight_cat, germ_cat, mass_cat = node_tables(node_index, mode_index, weights)
    recip, g_first, g_last, coef = solve_tables(mean_perm, ny, cols, ngx, lax.axis_index("gx"))

    row_axis = ("gy", "sa")
    row_index = lax.axis_index(row_axis)
    col_index = lax.axis_index("gx")
    opened = jnp.stack(
        [row_index > 0, row_index < ngy * nsa - 1, col_index > 0, col_index < ngx - 1]
    ).astype(jnp.float32)
    scaled_logs = jnp.pad(
        log_fields * jnp.float32(-math.log2(math.e)), ((0, SLOT - fields), (0, 0), (0, 0))
    )
    top, low = halves(scaled_logs.reshape(SLOT, rows * cols))
    logs = jnp.concatenate([top, low, top], axis=0)

    field, *pieces = lax.optimization_barrier((field, *pieces))
    rims = rim_of(rows, field, scaled_logs.reshape(SLOT * rows, cols))
    first, last, near = rims
    halos = (
        rotated(last, row_axis, 1),
        rotated(first, row_axis, -1),
        rotated(near, "gx", 1),
        rotated(near, "gx", -1),
    )
    inner = inner_fluxes(rows, field, logs, basis_cat, weight_cat, germ_cat, mass_cat)
    galerkin = outer_fluxes(rows, opened, inner, rims, halos, basis_cat, weight_cat, germ_cat)
    part = lax.all_to_all(
        galerkin.reshape(nsa * ngy, sub, rows, cols), ("sa", "gy"), 0, 0, tiled=True
    )

    cy = cosine_matrix(ny)
    cx = cosine_matrix(cols)
    ends_of = np.zeros((8, cols))
    ends_of[0], ends_of[1] = cx[:, 0], cx[:, -1]
    f32 = functools.partial(jnp.asarray, dtype=jnp.float32)
    params = pltpu.CompilerParams(vmem_limit_bytes=40 << 20)
    vmem = pl.BlockSpec(memory_space=pltpu.VMEM)
    scaled, jumps = pl.pallas_call(
        functools.partial(local_kernel, nsa),
        in_specs=[pl.BlockSpec(memory_space=pltpu.SMEM)] + [vmem] * 10,
        out_shape=(
            jax.ShapeDtypeStruct((sub * ny, cols), jnp.float32),
            jax.ShapeDtypeStruct((ngx, 16, ny), jnp.float32),
        ),
        scratch_shapes=[pltpu.VMEM((ny, sub * cols), jnp.float32)],
        compiler_params=params,
        name="local_solve",
    )(place[None], part, *pieces, f32(cy), f32(cx.T), f32(ends_of), recip, coef)
    jumps = lax.all_to_all(jumps, "gx", 0, 0, tiled=True)
    z = pl.pallas_call(
        back_kernel,
        out_shape=jax.ShapeDtypeStruct((sub * ny, cols), jnp.float32),
        compiler_params=params,
        cost_estimate=pl.CostEstimate(
            flops=12 * sub * ny * cols * cols, bytes_accessed=2 << 20, transcendentals=0
        ),
        name="back",
    )(scaled, f32(cx))
    columns = pl.pallas_call(
        joined_kernel,
        out_shape=jax.ShapeDtypeStruct((ngy, sub, length, cols), jnp.float32),
        compiler_params=params,
        name="joined_solve",
    )(z, jumps, g_first, g_last, f32(cy.T))
    update = lax.all_to_all(columns, "gy", 0, 0, tiled=True).reshape(modes, length, cols)
    fresh = field_before + relax_weight * (field_now - field_before + step_length * update)
    return (fresh, update)


def solution(mesh):
    block = P("sa", "gy", "gx")
    in_specs = (block, block, block, P(None, ("gy", "sa"), "gx"), P(), P(), P(), P())
    return jax.shard_map(
        on_device, mesh=mesh, in_specs=in_specs, out_specs=(block, block), check_vma=False
    )
```

```python
import functools
import math

import jax
import jax.numpy as jnp
import numpy as np
from jax import lax
from jax.experimental import pallas as pl
from jax.experimental.pallas import tpu as pltpu
from jax.sharding import PartitionSpec as P

HIGHEST = lax.Precision.HIGHEST
hermite_points = (
    0.0,
    -1.7320508075688772,
    1.7320508075688772,
    -1.355626179974266,
    1.355626179974266,
    -2.8569700138728056,
    2.8569700138728056,
)
storage_rate = 0.0004
relax_weight = 1.6
step_length = 0.3
QB = 256
LANES = 128


def halves(x):
    top = lax.reduce_precision(x, 8, 7)
    return top.astype(jnp.bfloat16), (x - top).astype(jnp.bfloat16)


def split(x):
    top = x.astype(jnp.bfloat16)
    return top, (x - top.astype(jnp.float32)).astype(jnp.bfloat16)


def cosine_matrix(length):
    k = np.arange(length)[:, None]
    m = np.arange(length)[None, :]
    phase = (k * (2 * m + 1)) % (4 * length)
    factor = np.where(k == 0, math.sqrt(1.0 / length), math.sqrt(2.0 / length))
    return factor * np.cos(phase * (math.pi / (2 * length)))


def eigen_values(count, length):
    return 4.0 * np.sin(np.arange(count) * (math.pi / (2 * length))) ** 2


SLOT = 16
PIECE = 384


def tables_kernel(index_ref, mode_ref, weight_ref, basis_ref, w_ref, germ_ref, mass_ref, sum_ref):
    germs, q = index_ref.shape
    p = mode_ref.shape[0]
    step = pl.program_id(0)
    index = index_ref[...]
    germ = jnp.zeros((germs, q), jnp.float32)
    for level, point in enumerate(hermite_points):
        germ = jnp.where(index == level, jnp.float32(point), germ)
    square = germ * germ
    h2 = (square - 1.0) / math.sqrt(2.0)
    h3 = (square * germ - 3.0 * germ) / math.sqrt(6.0)
    basis = jnp.ones((p, q), jnp.float32)
    for i in range(germs):
        degree = mode_ref[:, i : i + 1]
        factor = jnp.where(
            degree == 1,
            germ[i : i + 1],
            jnp.where(degree == 2, h2[i : i + 1], jnp.where(degree == 3, h3[i : i + 1], 1.0)),
        )
        basis = basis * factor
    weighted = basis * weight_ref[...]
    w_ref[0:p, :], w_ref[p : 2 * p, :] = split(2.0 * weighted)
    top, low = split(basis.T)
    basis_ref[:, 0:p] = top
    basis_ref[:, p : 2 * p] = top
    basis_ref[:, 2 * p : 3 * p] = low
    full = jnp.concatenate(
        [jnp.ones((8, q), jnp.float32), germ, jnp.zeros((LANES - 16, q), jnp.float32)], axis=0
    )
    top, low = split(full.T[:, 7 : 7 + SLOT])
    lane = lax.broadcasted_iota(jnp.int32, (q, SLOT), 1)
    keep = lane < germs + 1
    top = jnp.where(keep, top.astype(jnp.float32), 0.0).astype(jnp.bfloat16)
    low = jnp.where(keep, low.astype(jnp.float32), 0.0).astype(jnp.bfloat16)
    germ_ref[:, 0:SLOT] = top
    germ_ref[:, SLOT : 2 * SLOT] = top
    germ_ref[:, 2 * SLOT : 3 * SLOT] = low

    @pl.when(step == 0)
    def _():
        sum_ref[...] = jnp.zeros_like(sum_ref)

    sum_ref[...] += lax.dot_general(
        storage_rate * weighted, basis, (((1,), (1,)), ((), ())),
        precision=HIGHEST, preferred_element_type=jnp.float32,
    )

    @pl.when(step == pl.num_programs(0) - 1)
    def _():
        top, low = split(sum_ref[...])
        mass_ref[:, 0:p] = top
        mass_ref[:, p : 2 * p] = top
        mass_ref[:, 2 * p : 3 * p] = low


def node_tables(node_index, mode_index, weights):
    q, germs = node_index.shape
    p = mode_index.shape[0]
    pad = -q % QB
    index = jnp.pad(node_index.T, ((0, 0), (0, pad)))
    weights = jnp.pad(weights, (0, pad))[None]
    return pl.pallas_call(
        tables_kernel,
        grid=((q + pad) // QB,),
        in_specs=[
            pl.BlockSpec((germs, QB), lambda i: (0, i)),
            whole((p, germs)),
            pl.BlockSpec((1, QB), lambda i: (0, i)),
        ],
        out_specs=[
            pl.BlockSpec((QB, 3 * p), lambda i: (i, 0)),
            pl.BlockSpec((2 * p, QB), lambda i: (0, i)),
            pl.BlockSpec((QB, 3 * SLOT), lambda i: (i, 0)),
            whole((p, 3 * p)),
        ],
        out_shape=[
            jax.ShapeDtypeStruct((q + pad, 3 * p), jnp.bfloat16),
            jax.ShapeDtypeStruct((2 * p, q + pad), jnp.bfloat16),
            jax.ShapeDtypeStruct((q + pad, 3 * SLOT), jnp.bfloat16),
            jax.ShapeDtypeStruct((p, 3 * p), jnp.bfloat16),
        ],
        scratch_shapes=[pltpu.VMEM((p, p), jnp.float32)],
        compiler_params=pltpu.CompilerParams(vmem_limit_bytes=20 << 20),
        name="node_tables",
    )(index, mode_index, weights)


def whole(shape):
    return pl.BlockSpec(shape, lambda *_: (0,) * len(shape))


def rim_kernel(rows, u_ref, log_ref, first_ref, last_ref, near_ref):
    start = 0
    for ref in (u_ref, log_ref):
        n = ref.shape[0] // rows
        span = slice(start, start + n)
        lane = lax.broadcasted_iota(jnp.int32, (n, LANES), 1)
        near = jnp.zeros((n, LANES), jnp.float32)
        for y in range(rows):
            here = ref[pl.ds(y, n, stride=rows), :]
            if y == 0:
                first_ref[span] = here
            if y == rows - 1:
                last_ref[span] = here
            near = jnp.where(lane == y, here[:, 0:1], near)
            near = jnp.where(lane == rows + y, here[:, LANES - 1 : LANES], near)
        near_ref[span] = near
        start += n


def rim_of(rows, field, logs):
    n = (field.shape[0] + logs.shape[0]) // rows
    return pl.pallas_call(
        functools.partial(rim_kernel, rows),
        out_shape=[jax.ShapeDtypeStruct((n, LANES), jnp.float32)] * 3,
        compiler_params=pltpu.CompilerParams(vmem_limit_bytes=20 << 20),
        name="rim_of",
    )(field, logs)


def put_cat(ref, lanes, x):
    p = x.shape[0]
    top, low = split(x)
    ref[0:p, lanes] = top
    ref[p : 2 * p, lanes] = low
    ref[2 * p : 3 * p, lanes] = top


def projected(w_ref, parts):
    p = w_ref.shape[0] // 2
    top, low = parts
    both = jnp.dot(w_ref[...], top, preferred_element_type=jnp.float32)
    rest = jnp.dot(w_ref[0:p, :], low, preferred_element_type=jnp.float32)
    return both[0:p] + both[p : 2 * p] + rest


def resistance(germ_ref, log):
    return jnp.exp2(jnp.dot(germ_ref[...], log, preferred_element_type=jnp.float32))


def inner_kernel(rows, u_ref, log_ref, basis_ref, germ_ref, w_ref, mass_ref, g_ref, u_cat_ref, du_ref, r_ref, f_ref):
    p = mass_ref.shape[0]
    cols = LANES
    lane = lax.broadcasted_iota(jnp.int32, (p, cols), 1)
    above = None
    for y in range(rows):
        here = u_ref[pl.ds(y, p, stride=rows), :]
        put_cat(u_cat_ref, pl.ds(y * cols, cols), here)
        ahead = pltpu.roll(here, cols - 1, axis=1)
        put_cat(du_ref, pl.ds(y * cols, cols), jnp.where(lane == cols - 1, 0.0, ahead - here))
        if y > 0:
            put_cat(du_ref, pl.ds((rows + y - 1) * cols, cols), here - above)
        above = here

    chunks = [("x", y, 2) for y in range(0, rows, 2)]
    chunks += [("y", y, min(2, rows - 1 - y)) for y in range(0, rows - 1, 2)]

    def lanes(chunk):
        kind, y, n = chunk
        return pl.ds((y if kind == "x" else rows + y) * cols, n * cols)

    def values(chunk):
        return jnp.dot(basis_ref[...], du_ref[:, lanes(chunk)], preferred_element_type=jnp.float32)

    def total(chunk):
        kind, y, n = chunk
        if kind == "y":
            return r_ref[:, pl.ds(y * cols, n * cols)] + r_ref[:, pl.ds((y + 1) * cols, n * cols)]
        sums = []
        for k in range(n):
            r = r_ref[:, pl.ds((y + k) * cols, cols)]
            sums.append(r + pltpu.roll(r, cols - 1, axis=1))
        return jnp.concatenate(sums, axis=1)

    def fill(y):
        span = pl.ds(y * cols, 2 * cols)
        r_ref[:, span] = resistance(germ_ref, log_ref[:, span])

    fill(0)
    value = values(chunks[0])
    waiting = None
    for i, chunk in enumerate(chunks):
        later = values(chunks[i + 1]) if i + 1 < len(chunks) else None
        if 2 * (i + 1) < rows:
            fill(2 * (i + 1))
        parts = split(value / total(chunk))
        if waiting is not None:
            f_ref[:, lanes(waiting[0])] = projected(w_ref, waiting[1])
        waiting = (chunk, parts)
        value = later
    stored = [
        jnp.dot(mass_ref[...], u_cat_ref[:, pl.ds(y * cols, 2 * cols)], preferred_element_type=jnp.float32)
        for y in range(0, rows, 2)
    ]
    f_ref[:, lanes(waiting[0])] = projected(w_ref, waiting[1])

    for y in range(rows):
        out = stored[y // 2][:, (y % 2) * cols : (y % 2 + 1) * cols]
        later = f_ref[:, pl.ds(y * cols, cols)]
        earlier = jnp.where(lane == 0, 0.0, pltpu.roll(later, 1, axis=1))
        later = jnp.where(lane == cols - 1, 0.0, later)
        out = out - (later - earlier)
        if y < rows - 1:
            out = out - f_ref[:, pl.ds((rows + y) * cols, cols)]
        if y > 0:
            out = out + f_ref[:, pl.ds((rows + y - 1) * cols, cols)]
        g_ref[y] = out


def inner_fluxes(rows, field, logs, basis_cat, weight_cat, germ_cat, mass_cat):
    p, cols = field.shape[0] // rows, field.shape[1]
    q = basis_cat.shape[0]
    faces = (2 * rows - 1) * cols
    return pl.pallas_call(
        functools.partial(inner_kernel, rows),
        out_shape=jax.ShapeDtypeStruct((rows, p, cols), jnp.float32),
        scratch_shapes=[
            pltpu.VMEM((3 * p, rows * cols), jnp.bfloat16),
            pltpu.VMEM((3 * p, faces), jnp.bfloat16),
            pltpu.VMEM((q, rows * cols), jnp.float32),
            pltpu.VMEM((p, faces), jnp.float32),
        ],
        compiler_params=pltpu.CompilerParams(vmem_limit_bytes=50 << 20),
        cost_estimate=pl.CostEstimate(
            flops=2 * q * faces * p * 6, bytes_accessed=8 << 20, transcendentals=q * rows * cols
        ),
        name="inner_fluxes",
    )(field, logs, basis_cat, germ_cat, weight_cat, mass_cat)


def outer_kernel(
    rows, open_ref, g_ref, first_ref, last_ref, near_ref, up_ref, down_ref,
    left_ref, right_ref, basis_ref, germ_ref, w_ref, out_ref, du_ref, le_ref, ll_ref,
):
    p = w_ref.shape[0] // 2
    q = basis_ref.shape[0]
    cols = LANES
    near = near_ref[...]
    left = pltpu.roll(left_ref[...], cols - rows, axis=1)
    right = pltpu.roll(right_ref[...], rows, axis=1)
    lane = lax.broadcasted_iota(jnp.int32, near.shape, 1)
    earlier = jnp.where(lane < rows, left, near)
    later = jnp.where(lane < rows, near, right)
    pairs = ((up_ref[...], first_ref[...]), (last_ref[...], down_ref[...]), (earlier, later))
    for k, (e, l) in enumerate(pairs):
        span = pl.ds(k * cols, cols)
        diff = l[0:p] - e[0:p]
        if k < 2:
            diff = diff * open_ref[k]
        else:
            low = lane[0:p] < rows
            diff = jnp.where(low, diff * open_ref[2], diff * open_ref[3])
            diff = jnp.where(lane[0:p] < 2 * rows, diff, 0.0)
        put_cat(du_ref, span, diff)
        put_cat(le_ref, span, e[p : p + SLOT])
        put_cat(ll_ref, span, l[p : p + SLOT])

    def values(i):
        return jnp.dot(
            basis_ref[pl.ds(i * PIECE, PIECE), :], du_ref[...], preferred_element_type=jnp.float32
        )

    def total(i):
        germ = germ_ref[pl.ds(i * PIECE, PIECE), :]
        e = jnp.exp2(jnp.dot(germ, le_ref[...], preferred_element_type=jnp.float32))
        return e + jnp.exp2(jnp.dot(germ, ll_ref[...], preferred_element_type=jnp.float32))

    def project(i, parts):
        top, low = parts
        at = pl.ds(i * PIECE, PIECE)
        both = jnp.dot(w_ref[:, at], top, preferred_element_type=jnp.float32)
        rest = jnp.dot(w_ref[0:p, at], low, preferred_element_type=jnp.float32)
        return both[0:p] + both[p : 2 * p] + rest

    steps = q // PIECE
    value, sums = values(0), total(0)
    flux, waiting = None, None
    for i in range(steps):
        later = (values(i + 1), total(i + 1)) if i + 1 < steps else (None, None)
        parts = split(value / sums)
        if waiting is not None:
            term = project(*waiting)
            flux = term if flux is None else flux + term
        waiting = (i, parts)
        value, sums = later
    flux = flux + project(*waiting)

    lane = lax.broadcasted_iota(jnp.int32, (p, cols), 1)
    for y in range(rows):
        out = g_ref[y]
        if y == 0:
            out = out + flux[:, 0:cols]
        if y == rows - 1:
            out = out - flux[:, cols : 2 * cols]
        out = out + jnp.where(lane == 0, flux[:, 2 * cols + y : 2 * cols + y + 1], 0.0)
        at = 2 * cols + rows + y
        out = out - jnp.where(lane == cols - 1, flux[:, at : at + 1], 0.0)
        out_ref[pl.ds(y, p, stride=rows), :] = out


def outer_fluxes(rows, opened, inner, rims, halos, basis_cat, weight_cat, germ_cat):
    p, cols = inner.shape[1:]
    q = basis_cat.shape[0]
    vmem = pl.BlockSpec(memory_space=pltpu.VMEM)
    return pl.pallas_call(
        functools.partial(outer_kernel, rows),
        in_specs=[pl.BlockSpec(memory_space=pltpu.SMEM)] + [vmem] * 11,
        out_shape=jax.ShapeDtypeStruct((p * rows, cols), jnp.float32),
        scratch_shapes=[
            pltpu.VMEM((3 * p, 3 * cols), jnp.bfloat16),
            pltpu.VMEM((3 * SLOT, 3 * cols), jnp.bfloat16),
            pltpu.VMEM((3 * SLOT, 3 * cols), jnp.bfloat16),
        ],
        compiler_params=pltpu.CompilerParams(vmem_limit_bytes=50 << 20),
        cost_estimate=pl.CostEstimate(
            flops=2 * q * 3 * cols * p * 6, bytes_accessed=8 << 20, transcendentals=q * 6 * cols
        ),
        name="outer_fluxes",
    )(opened, inner, *rims, *halos, basis_cat, germ_cat, weight_cat)


def local_kernel(
    nsa, place_ref, part_ref, s0_ref, s1_ref, s2_ref, s3_ref, cy_ref, cxt_ref, ends_of_ref,
    recip_ref, coef_ref, scaled_ref, jump_ref, res_ref,
):
    modes, length, cols = s0_ref.shape
    rows = part_ref.shape[2]
    ngy = 4
    ny = ngy * length
    for d, src_ref in enumerate((s0_ref, s1_ref, s2_ref, s3_ref)):
        g = lax.rem(place_ref[0] + ngy - d, ngy)
        for s, block in enumerate(row_order(nsa)):
            span = pl.ds(pl.multiple_of(g * length + block * rows, 8), rows)
            for m in range(modes):
                res_ref[span, pl.ds(m * cols, cols)] = (
                    src_ref[m, pl.ds(block * rows, rows), :] - part_ref[s * ngy + g, m]
                )
    spectral = jnp.dot(cy_ref[...], res_ref[...], precision=HIGHEST, preferred_element_type=jnp.float32)
    spectral = jnp.concatenate([spectral[:, m * cols : (m + 1) * cols] for m in range(modes)], axis=0)
    spectral = jnp.dot(spectral, cxt_ref[...], precision=HIGHEST, preferred_element_type=jnp.float32)
    recip = recip_ref[...]
    scaled = jnp.concatenate(
        [recip * spectral[m * ny : (m + 1) * ny] for m in range(modes)], axis=0
    )
    both = lax.dot_general(
        ends_of_ref[...], scaled, (((1,), (1,)), ((), ())),
        precision=HIGHEST, preferred_element_type=jnp.float32,
    )
    pad = [jnp.zeros((8 - modes, ny), jnp.float32)]
    first = jnp.concatenate([both[0:1, m * ny : (m + 1) * ny] for m in range(modes)] + pad, axis=0)
    last = jnp.concatenate([both[1:2, m * ny : (m + 1) * ny] for m in range(modes)] + pad, axis=0)
    blocks = jump_ref.shape[0]
    for i in range(blocks + 1):
        term = coef_ref[0, i : i + 1, :] * first + coef_ref[1, i : i + 1, :] * last
        if i < blocks:
            jump_ref[i, 0:8, :] = term
        if i > 0:
            jump_ref[i - 1, 8:16, :] = term
    scaled_ref[...] = scaled


def back_kernel(scaled_ref, cx_ref, z_ref):
    z_ref[...] = jnp.dot(
        scaled_ref[...], cx_ref[...], precision=HIGHEST, preferred_element_type=jnp.float32
    )


def joined_kernel(z_ref, jump_ref, g_first_ref, g_last_ref, cyt_ref, out_ref):
    blocks = jump_ref.shape[0]
    ngy, modes = out_ref.shape[:2]
    ny, cols = g_first_ref.shape
    length = ny // ngy
    total = jump_ref[0]
    for i in range(1, blocks):
        total = total + jump_ref[i]
    both = jnp.concatenate([total, jnp.zeros((LANES - 16, ny), jnp.float32)], axis=0).T
    x = jnp.concatenate(
        [
            z_ref[m * ny : (m + 1) * ny]
            + g_first_ref[...] * both[:, m : m + 1]
            - g_last_ref[...] * both[:, 8 + m : 9 + m]
            for m in range(modes)
        ],
        axis=1,
    )
    out = jnp.dot(cyt_ref[...], x, precision=HIGHEST, preferred_element_type=jnp.float32)
    for g in range(ngy):
        for m in range(modes):
            out_ref[g, m] = out[g * length : (g + 1) * length, m * cols : (m + 1) * cols]


def solve_tables(mean_perm, ny, cols, blocks, position):
    cx = cosine_matrix(cols)
    lam_y = jnp.asarray(eigen_values(ny, ny), jnp.float32)
    lam_x = jnp.asarray(eigen_values(cols, cols), jnp.float32)
    recip = 1.0 / (storage_rate + mean_perm * (lam_y[:, None] + lam_x[None, :]))
    first = jnp.asarray(cx[:, 0][:, None] * cx, jnp.float32)
    last = jnp.asarray(cx[:, -1][:, None] * cx, jnp.float32)
    g_first = jnp.dot(recip, first, precision=HIGHEST)
    g_last = jnp.dot(recip, last, precision=HIGHEST)
    k = np.arange(1, blocks)
    sine = math.sqrt(2.0 / blocks) * np.sin(np.pi * np.outer(np.arange(0, blocks + 1), k) / blocks)
    sine[0] = 0.0
    sine[blocks] = 0.0
    theta = jnp.asarray(2.0 * np.cos(np.pi * k / blocks), jnp.float32)
    spread = 1.0 / (
        1.0 / mean_perm + g_first[:, 0:1] + g_last[:, cols - 1 : cols] - g_first[:, cols - 1 : cols] * theta
    )
    table = jnp.asarray(sine, jnp.float32)
    coef = []
    for end, sign in ((0, -1.0), (1, 1.0)):
        mine = sign * lax.dynamic_slice_in_dim(table, position + end, 1, axis=0)
        coef.append(jnp.einsum("ik,jk->ij", table, spread * mine, precision=HIGHEST))
    return recip, g_first, g_last, jnp.stack(coef)


def row_order(count):
    half = count // 2
    return list(range(half)) + list(range(count - 1, half - 1, -1))


def rotated(x, axis, by):
    count = lax.axis_size(axis)
    return lax.ppermute(x, axis, [(i, (i + by) % count) for i in range(count)])


def on_device(
    field_now, field_before, source, log_fields, weights, mean_perm, node_index, mode_index
):
    nsa, ngy, ngx = (lax.axis_size(a) for a in ("sa", "gy", "gx"))
    modes, length, cols = field_now.shape
    rows = length // nsa
    p = modes * nsa
    ny = length * ngy
    sub = modes // ngy
    fields = log_fields.shape[0]

    order = row_order(nsa)
    parts = field_now.reshape(modes, nsa, rows, cols)
    outgoing = jnp.stack([parts[:, block] for block in order])
    field = lax.all_to_all(outgoing, "sa", 0, 0, tiled=True).reshape(p * rows, cols)

    place = lax.axis_index("gy")
    blocks = source.reshape(ngy, sub, length, cols)
    pieces = [lax.dynamic_index_in_dim(blocks, (place + d) % ngy, 0, keepdims=False) for d in range(ngy)]
    pieces = pieces[:1] + [rotated(pieces[d], "gy", d) for d in range(1, ngy)]

    basis_cat, weight_cat, germ_cat, mass_cat = node_tables(node_index, mode_index, weights)
    recip, g_first, g_last, coef = solve_tables(mean_perm, ny, cols, ngx, lax.axis_index("gx"))

    row_axis = ("gy", "sa")
    member = lax.axis_index("sa")
    row_index = place * nsa + jnp.where(member < nsa // 2, member, nsa - 1 - (member - nsa // 2))
    log_fields = lax.ppermute(
        log_fields, row_axis, [(g * nsa + order[i], g * nsa + i) for g in range(ngy) for i in range(nsa)]
    )
    chain = [g * nsa + order.index(k) for g in range(ngy) for k in range(nsa)]
    ring = [(a, b) for a, b in zip(chain, chain[1:] + chain[:1])]
    col_index = lax.axis_index("gx")
    opened = jnp.stack(
        [row_index > 0, row_index < ngy * nsa - 1, col_index > 0, col_index < ngx - 1]
    ).astype(jnp.float32)
    scaled_logs = jnp.pad(
        log_fields * jnp.float32(-math.log2(math.e)), ((0, SLOT - fields), (0, 0), (0, 0))
    )
    top, low = halves(scaled_logs.reshape(SLOT, rows * cols))
    logs = jnp.concatenate([top, low, top], axis=0)

    field, *pieces = lax.optimization_barrier((field, *pieces))
    rims = rim_of(rows, field, scaled_logs.reshape(SLOT * rows, cols))
    first, last, near = rims
    halos = (
        lax.ppermute(last, row_axis, ring),
        lax.ppermute(first, row_axis, [(b, a) for a, b in ring]),
        rotated(near, "gx", 1),
        rotated(near, "gx", -1),
    )
    inner = inner_fluxes(rows, field, logs, basis_cat, weight_cat, germ_cat, mass_cat)
    galerkin = outer_fluxes(rows, opened, inner, rims, halos, basis_cat, weight_cat, germ_cat)
    part = lax.all_to_all(
        galerkin.reshape(nsa * ngy, sub, rows, cols), ("sa", "gy"), 0, 0, tiled=True
    )

    cy = cosine_matrix(ny)
    cx = cosine_matrix(cols)
    ends_of = np.zeros((8, cols))
    ends_of[0], ends_of[1] = cx[:, 0], cx[:, -1]
    f32 = functools.partial(jnp.asarray, dtype=jnp.float32)
    params = pltpu.CompilerParams(vmem_limit_bytes=40 << 20)
    vmem = pl.BlockSpec(memory_space=pltpu.VMEM)
    scaled, jumps = pl.pallas_call(
        functools.partial(local_kernel, nsa),
        in_specs=[pl.BlockSpec(memory_space=pltpu.SMEM)] + [vmem] * 10,
        out_shape=(
            jax.ShapeDtypeStruct((sub * ny, cols), jnp.float32),
            jax.ShapeDtypeStruct((ngx, 16, ny), jnp.float32),
        ),
        scratch_shapes=[pltpu.VMEM((ny, sub * cols), jnp.float32)],
        compiler_params=params,
        name="local_solve",
    )(place[None], part, *pieces, f32(cy), f32(cx.T), f32(ends_of), recip, coef)
    jumps = lax.all_to_all(jumps, "gx", 0, 0, tiled=True)
    z = pl.pallas_call(
        back_kernel,
        out_shape=jax.ShapeDtypeStruct((sub * ny, cols), jnp.float32),
        compiler_params=params,
        cost_estimate=pl.CostEstimate(
            flops=12 * sub * ny * cols * cols, bytes_accessed=2 << 20, transcendentals=0
        ),
        name="back",
    )(scaled, f32(cx))
    columns = pl.pallas_call(
        joined_kernel,
        out_shape=jax.ShapeDtypeStruct((ngy, sub, length, cols), jnp.float32),
        compiler_params=params,
        name="joined_solve",
    )(z, jumps, g_first, g_last, f32(cy.T))
    update = lax.all_to_all(columns, "gy", 0, 0, tiled=True).reshape(modes, length, cols)
    fresh = field_before + relax_weight * (field_now - field_before + step_length * update)
    return (fresh, update)


def solution(mesh):
    block = P("sa", "gy", "gx")
    in_specs = (block, block, block, P(None, ("gy", "sa"), "gx"), P(), P(), P(), P())
    return jax.shard_map(
        on_device, mesh=mesh, in_specs=in_specs, out_specs=(block, block), check_vma=False
    )
```

```python
import functools
import math

import jax
import jax.numpy as jnp
import numpy as np
from jax import lax
from jax.experimental import pallas as pl
from jax.experimental.pallas import tpu as pltpu
from jax.sharding import PartitionSpec as P

HIGHEST = lax.Precision.HIGHEST
hermite_points = (
    0.0,
    -1.7320508075688772,
    1.7320508075688772,
    -1.355626179974266,
    1.355626179974266,
    -2.8569700138728056,
    2.8569700138728056,
)
storage_rate = 0.0004
relax_weight = 1.6
step_length = 0.3
QB = 256
LANES = 128


def halves(x):
    top = lax.reduce_precision(x, 8, 7)
    return top.astype(jnp.bfloat16), (x - top).astype(jnp.bfloat16)


def split(x):
    top = x.astype(jnp.bfloat16)
    return top, (x - top.astype(jnp.float32)).astype(jnp.bfloat16)


def cosine_matrix(length):
    k = np.arange(length)[:, None]
    m = np.arange(length)[None, :]
    phase = (k * (2 * m + 1)) % (4 * length)
    factor = np.where(k == 0, math.sqrt(1.0 / length), math.sqrt(2.0 / length))
    return factor * np.cos(phase * (math.pi / (2 * length)))


def eigen_values(count, length):
    return 4.0 * np.sin(np.arange(count) * (math.pi / (2 * length))) ** 2


SLOT = 16
PIECE = 384


def tables_kernel(index_ref, mode_ref, weight_ref, basis_ref, w_ref, germ_ref, mass_ref, sum_ref):
    germs, q = index_ref.shape
    p = mode_ref.shape[0]
    step = pl.program_id(0)
    index = index_ref[...]
    germ = jnp.zeros((germs, q), jnp.float32)
    for level, point in enumerate(hermite_points):
        germ = jnp.where(index == level, jnp.float32(point), germ)
    square = germ * germ
    h2 = (square - 1.0) / math.sqrt(2.0)
    h3 = (square * germ - 3.0 * germ) / math.sqrt(6.0)
    basis = jnp.ones((p, q), jnp.float32)
    for i in range(germs):
        degree = mode_ref[:, i : i + 1]
        factor = jnp.where(
            degree == 1,
            germ[i : i + 1],
            jnp.where(degree == 2, h2[i : i + 1], jnp.where(degree == 3, h3[i : i + 1], 1.0)),
        )
        basis = basis * factor
    weighted = basis * weight_ref[...]
    w_ref[0:p, :], w_ref[p : 2 * p, :] = split(2.0 * weighted)
    top, low = split(basis.T)
    basis_ref[:, 0:p] = top
    basis_ref[:, p : 2 * p] = top
    basis_ref[:, 2 * p : 3 * p] = low
    full = jnp.concatenate(
        [jnp.ones((8, q), jnp.float32), germ, jnp.zeros((LANES - 16, q), jnp.float32)], axis=0
    )
    top, low = split(full.T[:, 7 : 7 + SLOT])
    lane = lax.broadcasted_iota(jnp.int32, (q, SLOT), 1)
    keep = lane < germs + 1
    top = jnp.where(keep, top.astype(jnp.float32), 0.0).astype(jnp.bfloat16)
    low = jnp.where(keep, low.astype(jnp.float32), 0.0).astype(jnp.bfloat16)
    germ_ref[:, 0:SLOT] = top
    germ_ref[:, SLOT : 2 * SLOT] = top
    germ_ref[:, 2 * SLOT : 3 * SLOT] = low

    @pl.when(step == 0)
    def _():
        sum_ref[...] = jnp.zeros_like(sum_ref)

    sum_ref[...] += lax.dot_general(
        storage_rate * weighted, basis, (((1,), (1,)), ((), ())),
        precision=HIGHEST, preferred_element_type=jnp.float32,
    )

    @pl.when(step == pl.num_programs(0) - 1)
    def _():
        top, low = split(sum_ref[...])
        mass_ref[:, 0:p] = top
        mass_ref[:, p : 2 * p] = top
        mass_ref[:, 2 * p : 3 * p] = low


def node_tables(node_index, mode_index, weights):
    q, germs = node_index.shape
    p = mode_index.shape[0]
    pad = -q % QB
    index = jnp.pad(node_index.T, ((0, 0), (0, pad)))
    weights = jnp.pad(weights, (0, pad))[None]
    return pl.pallas_call(
        tables_kernel,
        grid=((q + pad) // QB,),
        in_specs=[
            pl.BlockSpec((germs, QB), lambda i: (0, i)),
            whole((p, germs)),
            pl.BlockSpec((1, QB), lambda i: (0, i)),
        ],
        out_specs=[
            pl.BlockSpec((QB, 3 * p), lambda i: (i, 0)),
            pl.BlockSpec((2 * p, QB), lambda i: (0, i)),
            pl.BlockSpec((QB, 3 * SLOT), lambda i: (i, 0)),
            whole((p, 3 * p)),
        ],
        out_shape=[
            jax.ShapeDtypeStruct((q + pad, 3 * p), jnp.bfloat16),
            jax.ShapeDtypeStruct((2 * p, q + pad), jnp.bfloat16),
            jax.ShapeDtypeStruct((q + pad, 3 * SLOT), jnp.bfloat16),
            jax.ShapeDtypeStruct((p, 3 * p), jnp.bfloat16),
        ],
        scratch_shapes=[pltpu.VMEM((p, p), jnp.float32)],
        compiler_params=pltpu.CompilerParams(vmem_limit_bytes=20 << 20),
        name="node_tables",
    )(index, mode_index, weights)


def whole(shape):
    return pl.BlockSpec(shape, lambda *_: (0,) * len(shape))


def rim_kernel(rows, u_ref, log_ref, first_ref, last_ref, near_ref):
    start = 0
    for ref in (u_ref, log_ref):
        n = ref.shape[0] // rows
        span = slice(start, start + n)
        lane = lax.broadcasted_iota(jnp.int32, (n, LANES), 1)
        near = jnp.zeros((n, LANES), jnp.float32)
        for y in range(rows):
            here = ref[pl.ds(y, n, stride=rows), :]
            if y == 0:
                first_ref[span] = here
            if y == rows - 1:
                last_ref[span] = here
            near = jnp.where(lane == y, here[:, 0:1], near)
            near = jnp.where(lane == rows + y, here[:, LANES - 1 : LANES], near)
        near_ref[span] = near
        start += n


def rim_of(rows, field, logs):
    n = (field.shape[0] + logs.shape[0]) // rows
    return pl.pallas_call(
        functools.partial(rim_kernel, rows),
        out_shape=[jax.ShapeDtypeStruct((n, LANES), jnp.float32)] * 3,
        compiler_params=pltpu.CompilerParams(vmem_limit_bytes=20 << 20),
        name="rim_of",
    )(field, logs)


def put_cat(ref, lanes, x):
    p = x.shape[0]
    top, low = split(x)
    ref[0:p, lanes] = top
    ref[p : 2 * p, lanes] = low
    ref[2 * p : 3 * p, lanes] = top


def projected(w_ref, parts):
    p = w_ref.shape[0] // 2
    top, low = parts
    both = jnp.dot(w_ref[...], top, preferred_element_type=jnp.float32)
    rest = jnp.dot(w_ref[0:p, :], low, preferred_element_type=jnp.float32)
    return both[0:p] + both[p : 2 * p] + rest


def resistance(germ_ref, log):
    return jnp.exp2(jnp.dot(germ_ref[...], log, preferred_element_type=jnp.float32))


def inner_kernel(rows, u_ref, log_ref, basis_ref, germ_ref, w_ref, mass_ref, g_ref, u_cat_ref, du_ref, r_ref, f_ref):
    p = mass_ref.shape[0]
    cols = LANES
    lane = lax.broadcasted_iota(jnp.int32, (p, cols), 1)
    above = None
    for y in range(rows):
        here = u_ref[pl.ds(y, p, stride=rows), :]
        put_cat(u_cat_ref, pl.ds(y * cols, cols), here)
        ahead = pltpu.roll(here, cols - 1, axis=1)
        put_cat(du_ref, pl.ds(y * cols, cols), jnp.where(lane == cols - 1, 0.0, ahead - here))
        if y > 0:
            put_cat(du_ref, pl.ds((rows + y - 1) * cols, cols), here - above)
        above = here

    chunks = [("x", y, 2) for y in range(0, rows, 2)]
    chunks += [("y", y, min(2, rows - 1 - y)) for y in range(0, rows - 1, 2)]

    def lanes(chunk):
        kind, y, n = chunk
        return pl.ds((y if kind == "x" else rows + y) * cols, n * cols)

    def values(chunk):
        return jnp.dot(basis_ref[...], du_ref[:, lanes(chunk)], preferred_element_type=jnp.float32)

    def total(chunk):
        kind, y, n = chunk
        if kind == "y":
            return r_ref[:, pl.ds(y * cols, n * cols)] + r_ref[:, pl.ds((y + 1) * cols, n * cols)]
        sums = []
        for k in range(n):
            r = r_ref[:, pl.ds((y + k) * cols, cols)]
            sums.append(r + pltpu.roll(r, cols - 1, axis=1))
        return jnp.concatenate(sums, axis=1)

    def fill(y):
        span = pl.ds(y * cols, 2 * cols)
        r_ref[:, span] = resistance(germ_ref, log_ref[:, span])

    fill(0)
    value = values(chunks[0])
    waiting = None
    for i, chunk in enumerate(chunks):
        later = values(chunks[i + 1]) if i + 1 < len(chunks) else None
        if 2 * (i + 1) < rows:
            fill(2 * (i + 1))
        parts = split(value / total(chunk))
        if waiting is not None:
            f_ref[:, lanes(waiting[0])] = projected(w_ref, waiting[1])
        waiting = (chunk, parts)
        value = later
    stored = [
        jnp.dot(mass_ref[...], u_cat_ref[:, pl.ds(y * cols, 2 * cols)], preferred_element_type=jnp.float32)
        for y in range(0, rows, 2)
    ]
    f_ref[:, lanes(waiting[0])] = projected(w_ref, waiting[1])

    for y in range(rows):
        out = stored[y // 2][:, (y % 2) * cols : (y % 2 + 1) * cols]
        later = f_ref[:, pl.ds(y * cols, cols)]
        earlier = jnp.where(lane == 0, 0.0, pltpu.roll(later, 1, axis=1))
        later = jnp.where(lane == cols - 1, 0.0, later)
        out = out - (later - earlier)
        if y < rows - 1:
            out = out - f_ref[:, pl.ds((rows + y) * cols, cols)]
        if y > 0:
            out = out + f_ref[:, pl.ds((rows + y - 1) * cols, cols)]
        g_ref[y] = out


def inner_fluxes(rows, field, logs, basis_cat, weight_cat, germ_cat, mass_cat):
    p, cols = field.shape[0] // rows, field.shape[1]
    q = basis_cat.shape[0]
    faces = (2 * rows - 1) * cols
    return pl.pallas_call(
        functools.partial(inner_kernel, rows),
        out_shape=jax.ShapeDtypeStruct((rows, p, cols), jnp.float32),
        scratch_shapes=[
            pltpu.VMEM((3 * p, rows * cols), jnp.bfloat16),
            pltpu.VMEM((3 * p, faces), jnp.bfloat16),
            pltpu.VMEM((q, rows * cols), jnp.float32),
            pltpu.VMEM((p, faces), jnp.float32),
        ],
        compiler_params=pltpu.CompilerParams(vmem_limit_bytes=50 << 20),
        cost_estimate=pl.CostEstimate(
            flops=2 * q * faces * p * 6, bytes_accessed=8 << 20, transcendentals=q * rows * cols
        ),
        name="inner_fluxes",
    )(field, logs, basis_cat, germ_cat, weight_cat, mass_cat)


def outer_kernel(
    rows, open_ref, g_ref, first_ref, last_ref, near_ref, up_ref, down_ref,
    left_ref, right_ref, basis_ref, germ_ref, w_ref, out_ref, du_ref, le_ref, ll_ref,
):
    p = w_ref.shape[0] // 2
    q = basis_ref.shape[0]
    cols = LANES
    near = near_ref[...]
    left = pltpu.roll(left_ref[...], cols - rows, axis=1)
    right = pltpu.roll(right_ref[...], rows, axis=1)
    lane = lax.broadcasted_iota(jnp.int32, near.shape, 1)
    earlier = jnp.where(lane < rows, left, near)
    later = jnp.where(lane < rows, near, right)
    pairs = ((up_ref[...], first_ref[...]), (last_ref[...], down_ref[...]), (earlier, later))
    for k, (e, l) in enumerate(pairs):
        span = pl.ds(k * cols, cols)
        diff = l[0:p] - e[0:p]
        if k < 2:
            diff = diff * open_ref[k]
        else:
            low = lane[0:p] < rows
            diff = jnp.where(low, diff * open_ref[2], diff * open_ref[3])
            diff = jnp.where(lane[0:p] < 2 * rows, diff, 0.0)
        put_cat(du_ref, span, diff)
        put_cat(le_ref, span, e[p : p + SLOT])
        put_cat(ll_ref, span, l[p : p + SLOT])

    def values(i):
        return jnp.dot(
            basis_ref[pl.ds(i * PIECE, PIECE), :], du_ref[...], preferred_element_type=jnp.float32
        )

    def total(i):
        germ = germ_ref[pl.ds(i * PIECE, PIECE), :]
        e = jnp.exp2(jnp.dot(germ, le_ref[...], preferred_element_type=jnp.float32))
        return e + jnp.exp2(jnp.dot(germ, ll_ref[...], preferred_element_type=jnp.float32))

    def project(i, parts):
        top, low = parts
        at = pl.ds(i * PIECE, PIECE)
        both = jnp.dot(w_ref[:, at], top, preferred_element_type=jnp.float32)
        rest = jnp.dot(w_ref[0:p, at], low, preferred_element_type=jnp.float32)
        return both[0:p] + both[p : 2 * p] + rest

    steps = q // PIECE
    value, sums = values(0), total(0)
    flux, waiting = None, None
    for i in range(steps):
        later = (values(i + 1), total(i + 1)) if i + 1 < steps else (None, None)
        parts = split(value / sums)
        if waiting is not None:
            term = project(*waiting)
            flux = term if flux is None else flux + term
        waiting = (i, parts)
        value, sums = later
    flux = flux + project(*waiting)

    lane = lax.broadcasted_iota(jnp.int32, (p, cols), 1)
    for y in range(rows):
        out = g_ref[y]
        if y == 0:
            out = out + flux[:, 0:cols]
        if y == rows - 1:
            out = out - flux[:, cols : 2 * cols]
        out = out + jnp.where(lane == 0, flux[:, 2 * cols + y : 2 * cols + y + 1], 0.0)
        at = 2 * cols + rows + y
        out = out - jnp.where(lane == cols - 1, flux[:, at : at + 1], 0.0)
        out_ref[pl.ds(y, p, stride=rows), :] = out


def outer_fluxes(rows, opened, inner, rims, halos, basis_cat, weight_cat, germ_cat):
    p, cols = inner.shape[1:]
    q = basis_cat.shape[0]
    vmem = pl.BlockSpec(memory_space=pltpu.VMEM)
    return pl.pallas_call(
        functools.partial(outer_kernel, rows),
        in_specs=[pl.BlockSpec(memory_space=pltpu.SMEM)] + [vmem] * 11,
        out_shape=jax.ShapeDtypeStruct((p * rows, cols), jnp.float32),
        scratch_shapes=[
            pltpu.VMEM((3 * p, 3 * cols), jnp.bfloat16),
            pltpu.VMEM((3 * SLOT, 3 * cols), jnp.bfloat16),
            pltpu.VMEM((3 * SLOT, 3 * cols), jnp.bfloat16),
        ],
        compiler_params=pltpu.CompilerParams(vmem_limit_bytes=50 << 20),
        cost_estimate=pl.CostEstimate(
            flops=2 * q * 3 * cols * p * 6, bytes_accessed=8 << 20, transcendentals=q * 6 * cols
        ),
        name="outer_fluxes",
    )(opened, inner, *rims, *halos, basis_cat, germ_cat, weight_cat)


def local_kernel(
    nsa, place_ref, part_ref, s0_ref, s1_ref, s2_ref, s3_ref, cy_ref, cxt_ref, ends_of_ref,
    recip_ref, coef_ref, scaled_ref, jump_ref, res_ref,
):
    modes, length, cols = s0_ref.shape
    rows = part_ref.shape[2]
    ngy = 4
    ny = ngy * length
    for d, src_ref in enumerate((s0_ref, s1_ref, s2_ref, s3_ref)):
        g = lax.rem(place_ref[0] + ngy - d, ngy)
        for s, block in enumerate(row_order(nsa)):
            span = pl.ds(pl.multiple_of(g * length + block * rows, 8), rows)
            for m in range(modes):
                res_ref[span, pl.ds(m * cols, cols)] = (
                    src_ref[m, pl.ds(block * rows, rows), :] - part_ref[s * ngy + g, m]
                )
    spectral = jnp.dot(cy_ref[...], res_ref[...], precision=HIGHEST, preferred_element_type=jnp.float32)
    spectral = jnp.concatenate([spectral[:, m * cols : (m + 1) * cols] for m in range(modes)], axis=0)
    spectral = jnp.dot(spectral, cxt_ref[...], precision=HIGHEST, preferred_element_type=jnp.float32)
    recip = recip_ref[...]
    scaled = jnp.concatenate(
        [recip * spectral[m * ny : (m + 1) * ny] for m in range(modes)], axis=0
    )
    both = lax.dot_general(
        ends_of_ref[...], scaled, (((1,), (1,)), ((), ())),
        precision=HIGHEST, preferred_element_type=jnp.float32,
    )
    pad = [jnp.zeros((8 - modes, ny), jnp.float32)]
    first = jnp.concatenate([both[0:1, m * ny : (m + 1) * ny] for m in range(modes)] + pad, axis=0)
    last = jnp.concatenate([both[1:2, m * ny : (m + 1) * ny] for m in range(modes)] + pad, axis=0)
    blocks = jump_ref.shape[0]
    for i in range(blocks + 1):
        term = coef_ref[0, i : i + 1, :] * first + coef_ref[1, i : i + 1, :] * last
        if i < blocks:
            jump_ref[i, 0:8, :] = term
        if i > 0:
            jump_ref[i - 1, 8:16, :] = term
    scaled_ref[...] = scaled


def back_kernel(scaled_ref, cx_ref, z_ref):
    z_ref[...] = jnp.dot(
        scaled_ref[...], cx_ref[...], precision=HIGHEST, preferred_element_type=jnp.float32
    )


def joined_kernel(z_ref, jump_ref, g_first_ref, g_last_ref, cyt_ref, out_ref):
    blocks = jump_ref.shape[0]
    ngy, modes = out_ref.shape[:2]
    ny, cols = g_first_ref.shape
    length = ny // ngy
    total = jump_ref[0]
    for i in range(1, blocks):
        total = total + jump_ref[i]
    both = jnp.concatenate([total, jnp.zeros((LANES - 16, ny), jnp.float32)], axis=0).T
    x = jnp.concatenate(
        [
            z_ref[m * ny : (m + 1) * ny]
            + g_first_ref[...] * both[:, m : m + 1]
            - g_last_ref[...] * both[:, 8 + m : 9 + m]
            for m in range(modes)
        ],
        axis=1,
    )
    out = jnp.dot(cyt_ref[...], x, precision=HIGHEST, preferred_element_type=jnp.float32)
    for g in range(ngy):
        for m in range(modes):
            out_ref[g, m] = out[g * length : (g + 1) * length, m * cols : (m + 1) * cols]


def solve_tables(mean_perm, ny, cols, blocks, position):
    cx = cosine_matrix(cols)
    lam_y = jnp.asarray(eigen_values(ny, ny), jnp.float32)
    lam_x = jnp.asarray(eigen_values(cols, cols), jnp.float32)
    recip = 1.0 / (storage_rate + mean_perm * (lam_y[:, None] + lam_x[None, :]))
    first = jnp.asarray(cx[:, 0][:, None] * cx, jnp.float32)
    last = jnp.asarray(cx[:, -1][:, None] * cx, jnp.float32)
    g_first = jnp.dot(recip, first, precision=HIGHEST)
    g_last = jnp.dot(recip, last, precision=HIGHEST)
    k = np.arange(1, blocks)
    sine = math.sqrt(2.0 / blocks) * np.sin(np.pi * np.outer(np.arange(0, blocks + 1), k) / blocks)
    sine[0] = 0.0
    sine[blocks] = 0.0
    theta = jnp.asarray(2.0 * np.cos(np.pi * k / blocks), jnp.float32)
    spread = 1.0 / (
        1.0 / mean_perm + g_first[:, 0:1] + g_last[:, cols - 1 : cols] - g_first[:, cols - 1 : cols] * theta
    )
    table = jnp.asarray(sine, jnp.float32)
    coef = []
    for end, sign in ((0, -1.0), (1, 1.0)):
        mine = sign * lax.dynamic_slice_in_dim(table, position + end, 1, axis=0)
        coef.append(jnp.einsum("ik,jk->ij", table, spread * mine, precision=HIGHEST))
    return recip, g_first, g_last, jnp.stack(coef)


def row_order(count):
    half = count // 2
    return list(range(half)) + list(range(count - 1, half - 1, -1))


def rotated(x, axis, by):
    count = lax.axis_size(axis)
    return lax.ppermute(x, axis, [(i, (i + by) % count) for i in range(count)])


def dealt_kernel(order, x_ref, out_ref):
    rows = out_ref.shape[2]
    for k, block in enumerate(order):
        out_ref[k] = x_ref[:, block * rows : (block + 1) * rows, :]


def dealt(x, order):
    modes, length, cols = x.shape
    return pl.pallas_call(
        functools.partial(dealt_kernel, order),
        out_shape=jax.ShapeDtypeStruct((len(order), modes, length // len(order), cols), x.dtype),
        name="dealt",
    )(x)


def on_device(
    field_now, field_before, source, log_fields, weights, mean_perm, node_index, mode_index
):
    nsa, ngy, ngx = (lax.axis_size(a) for a in ("sa", "gy", "gx"))
    modes, length, cols = field_now.shape
    rows = length // nsa
    p = modes * nsa
    ny = length * ngy
    sub = modes // ngy
    fields = log_fields.shape[0]

    order = row_order(nsa)
    outgoing = dealt(field_now, order)
    field = lax.all_to_all(outgoing, "sa", 0, 0, tiled=True).reshape(p * rows, cols)

    place = lax.axis_index("gy")
    blocks = source.reshape(ngy, sub, length, cols)
    pieces = [lax.dynamic_index_in_dim(blocks, (place + d) % ngy, 0, keepdims=False) for d in range(ngy)]
    pieces = pieces[:1] + [rotated(pieces[d], "gy", d) for d in range(1, ngy)]

    basis_cat, weight_cat, germ_cat, mass_cat = node_tables(node_index, mode_index, weights)
    recip, g_first, g_last, coef = solve_tables(mean_perm, ny, cols, ngx, lax.axis_index("gx"))

    row_axis = ("gy", "sa")
    member = lax.axis_index("sa")
    row_index = place * nsa + jnp.where(member < nsa // 2, member, nsa - 1 - (member - nsa // 2))
    log_fields = lax.ppermute(
        log_fields, row_axis, [(g * nsa + order[i], g * nsa + i) for g in range(ngy) for i in range(nsa)]
    )
    chain = [g * nsa + order.index(k) for g in range(ngy) for k in range(nsa)]
    ring = [(a, b) for a, b in zip(chain, chain[1:] + chain[:1])]
    col_index = lax.axis_index("gx")
    opened = jnp.stack(
        [row_index > 0, row_index < ngy * nsa - 1, col_index > 0, col_index < ngx - 1]
    ).astype(jnp.float32)
    scaled_logs = jnp.pad(
        log_fields * jnp.float32(-math.log2(math.e)), ((0, SLOT - fields), (0, 0), (0, 0))
    )
    top, low = halves(scaled_logs.reshape(SLOT, rows * cols))
    logs = jnp.concatenate([top, low, top], axis=0)

    field, *pieces = lax.optimization_barrier((field, *pieces))
    rims = rim_of(rows, field, scaled_logs.reshape(SLOT * rows, cols))
    first, last, near = rims
    halos = (
        lax.ppermute(last, row_axis, ring),
        lax.ppermute(first, row_axis, [(b, a) for a, b in ring]),
        rotated(near, "gx", 1),
        rotated(near, "gx", -1),
    )
    inner = inner_fluxes(rows, field, logs, basis_cat, weight_cat, germ_cat, mass_cat)
    galerkin = outer_fluxes(rows, opened, inner, rims, halos, basis_cat, weight_cat, germ_cat)
    part = lax.all_to_all(
        galerkin.reshape(nsa * ngy, sub, rows, cols), ("sa", "gy"), 0, 0, tiled=True
    )

    cy = cosine_matrix(ny)
    cx = cosine_matrix(cols)
    ends_of = np.zeros((8, cols))
    ends_of[0], ends_of[1] = cx[:, 0], cx[:, -1]
    f32 = functools.partial(jnp.asarray, dtype=jnp.float32)
    params = pltpu.CompilerParams(vmem_limit_bytes=40 << 20)
    vmem = pl.BlockSpec(memory_space=pltpu.VMEM)
    scaled, jumps = pl.pallas_call(
        functools.partial(local_kernel, nsa),
        in_specs=[pl.BlockSpec(memory_space=pltpu.SMEM)] + [vmem] * 10,
        out_shape=(
            jax.ShapeDtypeStruct((sub * ny, cols), jnp.float32),
            jax.ShapeDtypeStruct((ngx, 16, ny), jnp.float32),
        ),
        scratch_shapes=[pltpu.VMEM((ny, sub * cols), jnp.float32)],
        compiler_params=params,
        name="local_solve",
    )(place[None], part, *pieces, f32(cy), f32(cx.T), f32(ends_of), recip, coef)
    jumps = lax.all_to_all(jumps, "gx", 0, 0, tiled=True)
    z = pl.pallas_call(
        back_kernel,
        out_shape=jax.ShapeDtypeStruct((sub * ny, cols), jnp.float32),
        compiler_params=params,
        cost_estimate=pl.CostEstimate(
            flops=12 * sub * ny * cols * cols, bytes_accessed=2 << 20, transcendentals=0
        ),
        name="back",
    )(scaled, f32(cx))
    columns = pl.pallas_call(
        joined_kernel,
        out_shape=jax.ShapeDtypeStruct((ngy, sub, length, cols), jnp.float32),
        compiler_params=params,
        name="joined_solve",
    )(z, jumps, g_first, g_last, f32(cy.T))
    update = lax.all_to_all(columns, "gy", 0, 0, tiled=True).reshape(modes, length, cols)
    fresh = field_before + relax_weight * (field_now - field_before + step_length * update)
    return (fresh, update)


def solution(mesh):
    block = P("sa", "gy", "gx")
    in_specs = (block, block, block, P(None, ("gy", "sa"), "gx"), P(), P(), P(), P())
    return jax.shard_map(
        on_device, mesh=mesh, in_specs=in_specs, out_specs=(block, block), check_vma=False
    )
```

```python
import functools
import math

import jax
import jax.numpy as jnp
import numpy as np
from jax import lax
from jax.experimental import pallas as pl
from jax.experimental.pallas import tpu as pltpu
from jax.sharding import PartitionSpec as P

HIGHEST = lax.Precision.HIGHEST
hermite_points = (
    0.0,
    -1.7320508075688772,
    1.7320508075688772,
    -1.355626179974266,
    1.355626179974266,
    -2.8569700138728056,
    2.8569700138728056,
)
storage_rate = 0.0004
relax_weight = 1.6
step_length = 0.3
QB = 256
LANES = 128


def halves(x):
    top = lax.reduce_precision(x, 8, 7)
    return top.astype(jnp.bfloat16), (x - top).astype(jnp.bfloat16)


def split(x):
    top = x.astype(jnp.bfloat16)
    return top, (x - top.astype(jnp.float32)).astype(jnp.bfloat16)


def cosine_matrix(length):
    k = np.arange(length)[:, None]
    m = np.arange(length)[None, :]
    phase = (k * (2 * m + 1)) % (4 * length)
    factor = np.where(k == 0, math.sqrt(1.0 / length), math.sqrt(2.0 / length))
    return factor * np.cos(phase * (math.pi / (2 * length)))


def eigen_values(count, length):
    return 4.0 * np.sin(np.arange(count) * (math.pi / (2 * length))) ** 2


SLOT = 16
PIECE = 384


def tables_kernel(index_ref, mode_ref, weight_ref, basis_ref, w_ref, germ_ref, mass_ref, sum_ref):
    germs, q = index_ref.shape
    p = mode_ref.shape[0]
    step = pl.program_id(0)
    index = index_ref[...]
    germ = jnp.zeros((germs, q), jnp.float32)
    for level, point in enumerate(hermite_points):
        germ = jnp.where(index == level, jnp.float32(point), germ)
    square = germ * germ
    h2 = (square - 1.0) / math.sqrt(2.0)
    h3 = (square * germ - 3.0 * germ) / math.sqrt(6.0)
    basis = jnp.ones((p, q), jnp.float32)
    for i in range(germs):
        degree = mode_ref[:, i : i + 1]
        factor = jnp.where(
            degree == 1,
            germ[i : i + 1],
            jnp.where(degree == 2, h2[i : i + 1], jnp.where(degree == 3, h3[i : i + 1], 1.0)),
        )
        basis = basis * factor
    weighted = basis * weight_ref[...]
    w_ref[0:p, :], w_ref[p : 2 * p, :] = split(2.0 * weighted)
    top, low = split(basis.T)
    basis_ref[:, 0:p] = top
    basis_ref[:, p : 2 * p] = top
    basis_ref[:, 2 * p : 3 * p] = low
    full = jnp.concatenate(
        [jnp.ones((8, q), jnp.float32), germ, jnp.zeros((LANES - 16, q), jnp.float32)], axis=0
    )
    top, low = split(full.T[:, 7 : 7 + SLOT])
    lane = lax.broadcasted_iota(jnp.int32, (q, SLOT), 1)
    keep = lane < germs + 1
    top = jnp.where(keep, top.astype(jnp.float32), 0.0).astype(jnp.bfloat16)
    low = jnp.where(keep, low.astype(jnp.float32), 0.0).astype(jnp.bfloat16)
    germ_ref[:, 0:SLOT] = top
    germ_ref[:, SLOT : 2 * SLOT] = top
    germ_ref[:, 2 * SLOT : 3 * SLOT] = low

    @pl.when(step == 0)
    def _():
        sum_ref[...] = jnp.zeros_like(sum_ref)

    sum_ref[...] += lax.dot_general(
        storage_rate * weighted, basis, (((1,), (1,)), ((), ())),
        precision=HIGHEST, preferred_element_type=jnp.float32,
    )

    @pl.when(step == pl.num_programs(0) - 1)
    def _():
        top, low = split(sum_ref[...])
        mass_ref[:, 0:p] = top
        mass_ref[:, p : 2 * p] = top
        mass_ref[:, 2 * p : 3 * p] = low


def node_tables(node_index, mode_index, weights):
    q, germs = node_index.shape
    p = mode_index.shape[0]
    pad = -q % QB
    index = jnp.pad(node_index.T, ((0, 0), (0, pad)))
    weights = jnp.pad(weights, (0, pad))[None]
    return pl.pallas_call(
        tables_kernel,
        grid=((q + pad) // QB,),
        in_specs=[
            pl.BlockSpec((germs, QB), lambda i: (0, i)),
            whole((p, germs)),
            pl.BlockSpec((1, QB), lambda i: (0, i)),
        ],
        out_specs=[
            pl.BlockSpec((QB, 3 * p), lambda i: (i, 0)),
            pl.BlockSpec((2 * p, QB), lambda i: (0, i)),
            pl.BlockSpec((QB, 3 * SLOT), lambda i: (i, 0)),
            whole((p, 3 * p)),
        ],
        out_shape=[
            jax.ShapeDtypeStruct((q + pad, 3 * p), jnp.bfloat16),
            jax.ShapeDtypeStruct((2 * p, q + pad), jnp.bfloat16),
            jax.ShapeDtypeStruct((q + pad, 3 * SLOT), jnp.bfloat16),
            jax.ShapeDtypeStruct((p, 3 * p), jnp.bfloat16),
        ],
        scratch_shapes=[pltpu.VMEM((p, p), jnp.float32)],
        compiler_params=pltpu.CompilerParams(vmem_limit_bytes=20 << 20),
        name="node_tables",
    )(index, mode_index, weights)


def whole(shape):
    return pl.BlockSpec(shape, lambda *_: (0,) * len(shape))


def rim_kernel(rows, u_ref, log_ref, first_ref, last_ref, near_ref):
    start = 0
    for ref in (u_ref, log_ref):
        n = ref.shape[0] // rows
        span = slice(start, start + n)
        lane = lax.broadcasted_iota(jnp.int32, (n, LANES), 1)
        near = jnp.zeros((n, LANES), jnp.float32)
        for y in range(rows):
            here = ref[pl.ds(y, n, stride=rows), :]
            if y == 0:
                first_ref[span] = here
            if y == rows - 1:
                last_ref[span] = here
            near = jnp.where(lane == y, here[:, 0:1], near)
            near = jnp.where(lane == rows + y, here[:, LANES - 1 : LANES], near)
        near_ref[span] = near
        start += n


def rim_of(rows, field, logs):
    n = (field.shape[0] + logs.shape[0]) // rows
    return pl.pallas_call(
        functools.partial(rim_kernel, rows),
        out_shape=[jax.ShapeDtypeStruct((n, LANES), jnp.float32)] * 3,
        compiler_params=pltpu.CompilerParams(vmem_limit_bytes=20 << 20),
        name="rim_of",
    )(field, logs)


def put_cat(ref, lanes, x):
    p = x.shape[0]
    top, low = split(x)
    ref[0:p, lanes] = top
    ref[p : 2 * p, lanes] = low
    ref[2 * p : 3 * p, lanes] = top


def projected(w_ref, parts):
    p = w_ref.shape[0] // 2
    top, low = parts
    both = jnp.dot(w_ref[...], top, preferred_element_type=jnp.float32)
    rest = jnp.dot(w_ref[0:p, :], low, preferred_element_type=jnp.float32)
    return both[0:p] + both[p : 2 * p] + rest


def resistance(germ_ref, log):
    return jnp.exp2(jnp.dot(germ_ref[...], log, preferred_element_type=jnp.float32))


def inner_kernel(rows, u_ref, log_ref, basis_ref, germ_ref, w_ref, mass_ref, g_ref, u_cat_ref, du_ref, r_ref, f_ref):
    p = mass_ref.shape[0]
    cols = LANES
    lane = lax.broadcasted_iota(jnp.int32, (p, cols), 1)
    above = None
    for y in range(rows):
        here = u_ref[pl.ds(y, p, stride=rows), :]
        put_cat(u_cat_ref, pl.ds(y * cols, cols), here)
        ahead = pltpu.roll(here, cols - 1, axis=1)
        put_cat(du_ref, pl.ds(y * cols, cols), jnp.where(lane == cols - 1, 0.0, ahead - here))
        if y > 0:
            put_cat(du_ref, pl.ds((rows + y - 1) * cols, cols), here - above)
        above = here

    chunks = [("x", y, 2) for y in range(0, rows, 2)]
    chunks += [("y", y, min(2, rows - 1 - y)) for y in range(0, rows - 1, 2)]

    def lanes(chunk):
        kind, y, n = chunk
        return pl.ds((y if kind == "x" else rows + y) * cols, n * cols)

    def values(chunk):
        return jnp.dot(basis_ref[...], du_ref[:, lanes(chunk)], preferred_element_type=jnp.float32)

    def total(chunk):
        kind, y, n = chunk
        if kind == "y":
            return r_ref[:, pl.ds(y * cols, n * cols)] + r_ref[:, pl.ds((y + 1) * cols, n * cols)]
        sums = []
        for k in range(n):
            r = r_ref[:, pl.ds((y + k) * cols, cols)]
            sums.append(r + pltpu.roll(r, cols - 1, axis=1))
        return jnp.concatenate(sums, axis=1)

    def fill(y):
        span = pl.ds(y * cols, 2 * cols)
        r_ref[:, span] = resistance(germ_ref, log_ref[:, span])

    fill(0)
    value = values(chunks[0])
    waiting = None
    for i, chunk in enumerate(chunks):
        later = values(chunks[i + 1]) if i + 1 < len(chunks) else None
        if 2 * (i + 1) < rows:
            fill(2 * (i + 1))
        parts = split(value / total(chunk))
        if waiting is not None:
            f_ref[:, lanes(waiting[0])] = projected(w_ref, waiting[1])
        waiting = (chunk, parts)
        value = later
    stored = [
        jnp.dot(mass_ref[...], u_cat_ref[:, pl.ds(y * cols, 2 * cols)], preferred_element_type=jnp.float32)
        for y in range(0, rows, 2)
    ]
    f_ref[:, lanes(waiting[0])] = projected(w_ref, waiting[1])

    for y in range(rows):
        out = stored[y // 2][:, (y % 2) * cols : (y % 2 + 1) * cols]
        later = f_ref[:, pl.ds(y * cols, cols)]
        earlier = jnp.where(lane == 0, 0.0, pltpu.roll(later, 1, axis=1))
        later = jnp.where(lane == cols - 1, 0.0, later)
        out = out - (later - earlier)
        if y < rows - 1:
            out = out - f_ref[:, pl.ds((rows + y) * cols, cols)]
        if y > 0:
            out = out + f_ref[:, pl.ds((rows + y - 1) * cols, cols)]
        g_ref[y] = out


def inner_fluxes(rows, field, logs, basis_cat, weight_cat, germ_cat, mass_cat):
    p, cols = field.shape[0] // rows, field.shape[1]
    q = basis_cat.shape[0]
    faces = (2 * rows - 1) * cols
    return pl.pallas_call(
        functools.partial(inner_kernel, rows),
        out_shape=jax.ShapeDtypeStruct((rows, p, cols), jnp.float32),
        scratch_shapes=[
            pltpu.VMEM((3 * p, rows * cols), jnp.bfloat16),
            pltpu.VMEM((3 * p, faces), jnp.bfloat16),
            pltpu.VMEM((q, rows * cols), jnp.float32),
            pltpu.VMEM((p, faces), jnp.float32),
        ],
        compiler_params=pltpu.CompilerParams(vmem_limit_bytes=50 << 20),
        cost_estimate=pl.CostEstimate(
            flops=2 * q * faces * p * 6, bytes_accessed=8 << 20, transcendentals=q * rows * cols
        ),
        name="inner_fluxes",
    )(field, logs, basis_cat, germ_cat, weight_cat, mass_cat)


def outer_kernel(
    rows, open_ref, g_ref, first_ref, last_ref, near_ref, up_ref, down_ref,
    left_ref, right_ref, basis_ref, germ_ref, w_ref, out_ref, du_ref, le_ref, ll_ref,
):
    p = w_ref.shape[0] // 2
    q = basis_ref.shape[0]
    cols = LANES
    near = near_ref[...]
    left = pltpu.roll(left_ref[...], cols - rows, axis=1)
    right = pltpu.roll(right_ref[...], rows, axis=1)
    lane = lax.broadcasted_iota(jnp.int32, near.shape, 1)
    earlier = jnp.where(lane < rows, left, near)
    later = jnp.where(lane < rows, near, right)
    pairs = ((up_ref[...], first_ref[...]), (last_ref[...], down_ref[...]), (earlier, later))
    for k, (e, l) in enumerate(pairs):
        span = pl.ds(k * cols, cols)
        diff = l[0:p] - e[0:p]
        if k < 2:
            diff = diff * open_ref[k]
        else:
            low = lane[0:p] < rows
            diff = jnp.where(low, diff * open_ref[2], diff * open_ref[3])
            diff = jnp.where(lane[0:p] < 2 * rows, diff, 0.0)
        put_cat(du_ref, span, diff)
        put_cat(le_ref, span, e[p : p + SLOT])
        put_cat(ll_ref, span, l[p : p + SLOT])

    def values(i):
        return jnp.dot(
            basis_ref[pl.ds(i * PIECE, PIECE), :], du_ref[...], preferred_element_type=jnp.float32
        )

    def total(i):
        germ = germ_ref[pl.ds(i * PIECE, PIECE), :]
        e = jnp.exp2(jnp.dot(germ, le_ref[...], preferred_element_type=jnp.float32))
        return e + jnp.exp2(jnp.dot(germ, ll_ref[...], preferred_element_type=jnp.float32))

    def project(i, parts):
        top, low = parts
        at = pl.ds(i * PIECE, PIECE)
        both = jnp.dot(w_ref[:, at], top, preferred_element_type=jnp.float32)
        rest = jnp.dot(w_ref[0:p, at], low, preferred_element_type=jnp.float32)
        return both[0:p] + both[p : 2 * p] + rest

    steps = q // PIECE
    value, sums = values(0), total(0)
    flux, waiting = None, None
    for i in range(steps):
        later = (values(i + 1), total(i + 1)) if i + 1 < steps else (None, None)
        parts = split(value / sums)
        if waiting is not None:
            term = project(*waiting)
            flux = term if flux is None else flux + term
        waiting = (i, parts)
        value, sums = later
    flux = flux + project(*waiting)

    lane = lax.broadcasted_iota(jnp.int32, (p, cols), 1)
    for y in range(rows):
        out = g_ref[y]
        if y == 0:
            out = out + flux[:, 0:cols]
        if y == rows - 1:
            out = out - flux[:, cols : 2 * cols]
        out = out + jnp.where(lane == 0, flux[:, 2 * cols + y : 2 * cols + y + 1], 0.0)
        at = 2 * cols + rows + y
        out = out - jnp.where(lane == cols - 1, flux[:, at : at + 1], 0.0)
        out_ref[pl.ds(y, p, stride=rows), :] = out


def outer_fluxes(rows, opened, inner, rims, halos, basis_cat, weight_cat, germ_cat):
    p, cols = inner.shape[1:]
    q = basis_cat.shape[0]
    vmem = pl.BlockSpec(memory_space=pltpu.VMEM)
    return pl.pallas_call(
        functools.partial(outer_kernel, rows),
        in_specs=[pl.BlockSpec(memory_space=pltpu.SMEM)] + [vmem] * 11,
        out_shape=jax.ShapeDtypeStruct((p * rows, cols), jnp.float32),
        scratch_shapes=[
            pltpu.VMEM((3 * p, 3 * cols), jnp.bfloat16),
            pltpu.VMEM((3 * SLOT, 3 * cols), jnp.bfloat16),
            pltpu.VMEM((3 * SLOT, 3 * cols), jnp.bfloat16),
        ],
        compiler_params=pltpu.CompilerParams(vmem_limit_bytes=50 << 20),
        cost_estimate=pl.CostEstimate(
            flops=2 * q * 3 * cols * p * 6, bytes_accessed=8 << 20, transcendentals=q * 6 * cols
        ),
        name="outer_fluxes",
    )(opened, inner, *rims, *halos, basis_cat, germ_cat, weight_cat)


def local_kernel(
    nsa, place_ref, part_ref, s0_ref, s1_ref, s2_ref, s3_ref, cy_ref, cxt_ref, ends_of_ref,
    recip_ref, coef_ref, scaled_ref, jump_ref, res_ref,
):
    modes, length, cols = s0_ref.shape
    rows = part_ref.shape[2]
    ngy = 4
    ny = ngy * length
    for d, src_ref in enumerate((s0_ref, s1_ref, s2_ref, s3_ref)):
        g = lax.rem(place_ref[0] + ngy - d, ngy)
        for s, block in enumerate(row_order(nsa)):
            span = pl.ds(pl.multiple_of(g * length + block * rows, 8), rows)
            for m in range(modes):
                res_ref[span, pl.ds(m * cols, cols)] = (
                    src_ref[m, pl.ds(block * rows, rows), :] - part_ref[s * ngy + g, m]
                )
    spectral = jnp.dot(cy_ref[...], res_ref[...], precision=HIGHEST, preferred_element_type=jnp.float32)
    spectral = jnp.concatenate([spectral[:, m * cols : (m + 1) * cols] for m in range(modes)], axis=0)
    spectral = jnp.dot(spectral, cxt_ref[...], precision=HIGHEST, preferred_element_type=jnp.float32)
    recip = recip_ref[...]
    scaled = jnp.concatenate(
        [recip * spectral[m * ny : (m + 1) * ny] for m in range(modes)], axis=0
    )
    both = lax.dot_general(
        ends_of_ref[...], scaled, (((1,), (1,)), ((), ())),
        precision=HIGHEST, preferred_element_type=jnp.float32,
    )
    pad = [jnp.zeros((8 - modes, ny), jnp.float32)]
    first = jnp.concatenate([both[0:1, m * ny : (m + 1) * ny] for m in range(modes)] + pad, axis=0)
    last = jnp.concatenate([both[1:2, m * ny : (m + 1) * ny] for m in range(modes)] + pad, axis=0)
    blocks = jump_ref.shape[0]
    for i in range(blocks + 1):
        term = coef_ref[0, i : i + 1, :] * first + coef_ref[1, i : i + 1, :] * last
        if i < blocks:
            jump_ref[i, 0:8, :] = term
        if i > 0:
            jump_ref[i - 1, 8:16, :] = term
    scaled_ref[...] = scaled


def back_kernel(place_ref, scaled_ref, cx_ref, cyt_ref, p0_ref, p1_ref, p2_ref, p3_ref, rows_ref):
    modes, length, cols = p0_ref.shape
    ny = cyt_ref.shape[0]
    ngy = ny // length
    z = jnp.dot(scaled_ref[...], cx_ref[...], precision=HIGHEST, preferred_element_type=jnp.float32)
    z = jnp.concatenate([z[m * ny : (m + 1) * ny] for m in range(modes)], axis=1)
    rows_ref[...] = jnp.dot(cyt_ref[...], z, precision=HIGHEST, preferred_element_type=jnp.float32)
    for d, out_ref in enumerate((p0_ref, p1_ref, p2_ref, p3_ref)):
        g = lax.rem(place_ref[0] + d, ngy)
        span = pl.ds(pl.multiple_of(g * length, 8), length)
        for m in range(modes):
            out_ref[m] = rows_ref[span, pl.ds(m * cols, cols)]


def final_kernel(
    place_ref, p0_ref, p1_ref, p2_ref, p3_ref, t0_ref, t1_ref, t2_ref, t3_ref, g_first_ref, g_last_ref,
    cyt_ref, now_hbm, before_hbm, fresh_ref, update_ref, now_ref, before_ref, sems,
):
    modes, length, cols = p0_ref.shape
    ngy = fresh_ref.shape[0] // modes
    copies = [
        pltpu.make_async_copy(now_hbm, now_ref, sems.at[0]),
        pltpu.make_async_copy(before_hbm, before_ref, sems.at[1]),
    ]
    for copy in copies:
        copy.start()
    place = place_ref[0]
    back = cyt_ref[pl.ds(pl.multiple_of(place * length, 8), length), :]
    right = split(jnp.concatenate([g_first_ref[...], -g_last_ref[...]], axis=0))
    left = []
    for t_ref in (t0_ref, t1_ref, t2_ref, t3_ref):
        for m in range(modes):
            left.append(
                jnp.concatenate([back * t_ref[m : m + 1, :], back * t_ref[8 + m : 9 + m, :]], axis=1)
            )
    left = split(jnp.concatenate(left, axis=0))
    jump = jnp.dot(left[0], right[0], preferred_element_type=jnp.float32)
    jump = jump + jnp.dot(left[1], right[0], preferred_element_type=jnp.float32)
    jump = jump + jnp.dot(left[0], right[1], preferred_element_type=jnp.float32)
    for copy in copies:
        copy.wait()
    for d, p_ref in enumerate((p0_ref, p1_ref, p2_ref, p3_ref)):
        g = lax.rem(place + ngy - d, ngy)
        for m in range(modes):
            at = (d * modes + m) * length
            update = p_ref[m] + jump[at : at + length]
            mode = g * modes + m
            before = before_ref[mode]
            fresh_ref[mode] = before + relax_weight * (now_ref[mode] - before + step_length * update)
            update_ref[mode] = update


def solve_tables(mean_perm, ny, cols, blocks, position):
    cx = cosine_matrix(cols)
    lam_y = jnp.asarray(eigen_values(ny, ny), jnp.float32)
    lam_x = jnp.asarray(eigen_values(cols, cols), jnp.float32)
    recip = 1.0 / (storage_rate + mean_perm * (lam_y[:, None] + lam_x[None, :]))
    first = jnp.asarray(cx[:, 0][:, None] * cx, jnp.float32)
    last = jnp.asarray(cx[:, -1][:, None] * cx, jnp.float32)
    g_first = jnp.dot(recip, first, precision=HIGHEST)
    g_last = jnp.dot(recip, last, precision=HIGHEST)
    k = np.arange(1, blocks)
    sine = math.sqrt(2.0 / blocks) * np.sin(np.pi * np.outer(np.arange(0, blocks + 1), k) / blocks)
    sine[0] = 0.0
    sine[blocks] = 0.0
    theta = jnp.asarray(2.0 * np.cos(np.pi * k / blocks), jnp.float32)
    spread = 1.0 / (
        1.0 / mean_perm + g_first[:, 0:1] + g_last[:, cols - 1 : cols] - g_first[:, cols - 1 : cols] * theta
    )
    table = jnp.asarray(sine, jnp.float32)
    coef = []
    for end, sign in ((0, -1.0), (1, 1.0)):
        mine = sign * lax.dynamic_slice_in_dim(table, position + end, 1, axis=0)
        coef.append(jnp.einsum("ik,jk->ij", table, spread * mine, precision=HIGHEST))
    return recip, g_first, g_last, jnp.stack(coef)


def row_order(count):
    half = count // 2
    return list(range(half)) + list(range(count - 1, half - 1, -1))


def rotated(x, axis, by):
    count = lax.axis_size(axis)
    return lax.ppermute(x, axis, [(i, (i + by) % count) for i in range(count)])


def dealt_kernel(order, x_ref, out_ref):
    rows = out_ref.shape[2]
    for k, block in enumerate(order):
        out_ref[k] = x_ref[:, block * rows : (block + 1) * rows, :]


def dealt(x, order):
    modes, length, cols = x.shape
    return pl.pallas_call(
        functools.partial(dealt_kernel, order),
        out_shape=jax.ShapeDtypeStruct((len(order), modes, length // len(order), cols), x.dtype),
        name="dealt",
    )(x)


def on_device(
    field_now, field_before, source, log_fields, weights, mean_perm, node_index, mode_index
):
    nsa, ngy, ngx = (lax.axis_size(a) for a in ("sa", "gy", "gx"))
    modes, length, cols = field_now.shape
    rows = length // nsa
    p = modes * nsa
    ny = length * ngy
    sub = modes // ngy
    fields = log_fields.shape[0]

    order = row_order(nsa)
    outgoing = dealt(field_now, order)
    field = lax.all_to_all(outgoing, "sa", 0, 0, tiled=True).reshape(p * rows, cols)

    place = lax.axis_index("gy")
    blocks = source.reshape(ngy, sub, length, cols)
    pieces = [lax.dynamic_index_in_dim(blocks, (place + d) % ngy, 0, keepdims=False) for d in range(ngy)]
    pieces = pieces[:1] + [rotated(pieces[d], "gy", d) for d in range(1, ngy)]

    basis_cat, weight_cat, germ_cat, mass_cat = node_tables(node_index, mode_index, weights)
    recip, g_first, g_last, coef = solve_tables(mean_perm, ny, cols, ngx, lax.axis_index("gx"))

    row_axis = ("gy", "sa")
    member = lax.axis_index("sa")
    row_index = place * nsa + jnp.where(member < nsa // 2, member, nsa - 1 - (member - nsa // 2))
    log_fields = lax.ppermute(
        log_fields, row_axis, [(g * nsa + order[i], g * nsa + i) for g in range(ngy) for i in range(nsa)]
    )
    chain = [g * nsa + order.index(k) for g in range(ngy) for k in range(nsa)]
    ring = [(a, b) for a, b in zip(chain, chain[1:] + chain[:1])]
    col_index = lax.axis_index("gx")
    opened = jnp.stack(
        [row_index > 0, row_index < ngy * nsa - 1, col_index > 0, col_index < ngx - 1]
    ).astype(jnp.float32)
    scaled_logs = jnp.pad(
        log_fields * jnp.float32(-math.log2(math.e)), ((0, SLOT - fields), (0, 0), (0, 0))
    )
    top, low = halves(scaled_logs.reshape(SLOT, rows * cols))
    logs = jnp.concatenate([top, low, top], axis=0)

    field, *pieces = lax.optimization_barrier((field, *pieces))
    rims = rim_of(rows, field, scaled_logs.reshape(SLOT * rows, cols))
    first, last, near = rims
    halos = (
        lax.ppermute(last, row_axis, ring),
        lax.ppermute(first, row_axis, [(b, a) for a, b in ring]),
        rotated(near, "gx", 1),
        rotated(near, "gx", -1),
    )
    inner = inner_fluxes(rows, field, logs, basis_cat, weight_cat, germ_cat, mass_cat)
    galerkin = outer_fluxes(rows, opened, inner, rims, halos, basis_cat, weight_cat, germ_cat)
    part = lax.all_to_all(
        galerkin.reshape(nsa * ngy, sub, rows, cols), ("sa", "gy"), 0, 0, tiled=True
    )

    cy = cosine_matrix(ny)
    cx = cosine_matrix(cols)
    ends_of = np.zeros((8, cols))
    ends_of[0], ends_of[1] = cx[:, 0], cx[:, -1]
    f32 = functools.partial(jnp.asarray, dtype=jnp.float32)
    params = pltpu.CompilerParams(vmem_limit_bytes=40 << 20)
    vmem = pl.BlockSpec(memory_space=pltpu.VMEM)
    scaled, jumps = pl.pallas_call(
        functools.partial(local_kernel, nsa),
        in_specs=[pl.BlockSpec(memory_space=pltpu.SMEM)] + [vmem] * 10,
        out_shape=(
            jax.ShapeDtypeStruct((sub * ny, cols), jnp.float32),
            jax.ShapeDtypeStruct((ngx, 16, ny), jnp.float32),
        ),
        scratch_shapes=[pltpu.VMEM((ny, sub * cols), jnp.float32)],
        compiler_params=params,
        name="local_solve",
    )(place[None], part, *pieces, f32(cy), f32(cx.T), f32(ends_of), recip, coef)
    jumps = lax.all_to_all(jumps, "gx", 0, 0, tiled=True)
    smem = pl.BlockSpec(memory_space=pltpu.SMEM)
    hbm = pl.BlockSpec(memory_space=pl.ANY)
    sent = pl.pallas_call(
        back_kernel,
        in_specs=[smem] + [vmem] * 3,
        out_shape=[jax.ShapeDtypeStruct((sub, length, cols), jnp.float32)] * 4,
        scratch_shapes=[pltpu.VMEM((ny, sub * cols), jnp.float32)],
        compiler_params=params,
        cost_estimate=pl.CostEstimate(
            flops=36 * sub * ny * cols * cols, bytes_accessed=2 << 20, transcendentals=0
        ),
        name="back",
    )(place[None], scaled, f32(cx), f32(cy.T))
    got = [sent[0]] + [rotated(sent[d], "gy", d) for d in range(1, ngy)]
    total = jnp.sum(jumps, axis=0)
    totals = [total] + [rotated(total, "gy", d) for d in range(1, ngy)]
    block = jax.ShapeDtypeStruct(field_now.shape, jnp.float32)
    fresh, update = pl.pallas_call(
        final_kernel,
        in_specs=[smem] + [vmem] * 11 + [hbm] * 2,
        out_shape=[block] * 2,
        scratch_shapes=[
            pltpu.VMEM(field_now.shape, jnp.float32),
            pltpu.VMEM(field_now.shape, jnp.float32),
            pltpu.SemaphoreType.DMA((2,)),
        ],
        compiler_params=params,
        name="final",
    )(place[None], *got, *totals, g_first, g_last, f32(cy.T), field_now, field_before)
    return (fresh, update)


def solution(mesh):
    block = P("sa", "gy", "gx")
    in_specs = (block, block, block, P(None, ("gy", "sa"), "gx"), P(), P(), P(), P())
    return jax.shard_map(
        on_device, mesh=mesh, in_specs=in_specs, out_specs=(block, block), check_vma=False
    )
```

```python
import functools
import math

import jax
import jax.numpy as jnp
import numpy as np
from jax import lax
from jax.experimental import pallas as pl
from jax.experimental.pallas import tpu as pltpu
from jax.sharding import PartitionSpec as P

HIGHEST = lax.Precision.HIGHEST
hermite_points = (
    0.0,
    -1.7320508075688772,
    1.7320508075688772,
    -1.355626179974266,
    1.355626179974266,
    -2.8569700138728056,
    2.8569700138728056,
)
storage_rate = 0.0004
relax_weight = 1.6
step_length = 0.3
QB = 256
LANES = 128


def halves(x):
    top = lax.reduce_precision(x, 8, 7)
    return top.astype(jnp.bfloat16), (x - top).astype(jnp.bfloat16)


def split(x):
    top = x.astype(jnp.bfloat16)
    return top, (x - top.astype(jnp.float32)).astype(jnp.bfloat16)


def cosine_matrix(length):
    k = np.arange(length)[:, None]
    m = np.arange(length)[None, :]
    phase = (k * (2 * m + 1)) % (4 * length)
    factor = np.where(k == 0, math.sqrt(1.0 / length), math.sqrt(2.0 / length))
    return factor * np.cos(phase * (math.pi / (2 * length)))


def eigen_values(count, length):
    return 4.0 * np.sin(np.arange(count) * (math.pi / (2 * length))) ** 2


SLOT = 16
PIECE = 384


def tables_kernel(index_ref, mode_ref, weight_ref, basis_ref, w_ref, germ_ref, mass_ref, sum_ref):
    germs, q = index_ref.shape
    p = mode_ref.shape[0]
    step = pl.program_id(0)
    index = index_ref[...]
    germ = jnp.zeros((germs, q), jnp.float32)
    for level, point in enumerate(hermite_points):
        germ = jnp.where(index == level, jnp.float32(point), germ)
    square = germ * germ
    h2 = (square - 1.0) / math.sqrt(2.0)
    h3 = (square * germ - 3.0 * germ) / math.sqrt(6.0)
    basis = jnp.ones((p, q), jnp.float32)
    for i in range(germs):
        degree = mode_ref[:, i : i + 1]
        factor = jnp.where(
            degree == 1,
            germ[i : i + 1],
            jnp.where(degree == 2, h2[i : i + 1], jnp.where(degree == 3, h3[i : i + 1], 1.0)),
        )
        basis = basis * factor
    weighted = basis * weight_ref[...]
    w_ref[0:p, :], w_ref[p : 2 * p, :] = split(2.0 * weighted)
    top, low = split(basis.T)
    basis_ref[:, 0:p] = top
    basis_ref[:, p : 2 * p] = top
    basis_ref[:, 2 * p : 3 * p] = low
    full = jnp.concatenate(
        [jnp.ones((8, q), jnp.float32), germ, jnp.zeros((LANES - 16, q), jnp.float32)], axis=0
    )
    top, low = split(full.T[:, 7 : 7 + SLOT])
    lane = lax.broadcasted_iota(jnp.int32, (q, SLOT), 1)
    keep = lane < germs + 1
    top = jnp.where(keep, top.astype(jnp.float32), 0.0).astype(jnp.bfloat16)
    low = jnp.where(keep, low.astype(jnp.float32), 0.0).astype(jnp.bfloat16)
    germ_ref[:, 0:SLOT] = top
    germ_ref[:, SLOT : 2 * SLOT] = top
    germ_ref[:, 2 * SLOT : 3 * SLOT] = low

    @pl.when(step == 0)
    def _():
        sum_ref[...] = jnp.zeros_like(sum_ref)

    sum_ref[...] += lax.dot_general(
        storage_rate * weighted, basis, (((1,), (1,)), ((), ())),
        precision=HIGHEST, preferred_element_type=jnp.float32,
    )

    @pl.when(step == pl.num_programs(0) - 1)
    def _():
        top, low = split(sum_ref[...])
        mass_ref[:, 0:p] = top
        mass_ref[:, p : 2 * p] = top
        mass_ref[:, 2 * p : 3 * p] = low


def node_tables(node_index, mode_index, weights):
    q, germs = node_index.shape
    p = mode_index.shape[0]
    pad = -q % QB
    index = jnp.pad(node_index.T, ((0, 0), (0, pad)))
    weights = jnp.pad(weights, (0, pad))[None]
    return pl.pallas_call(
        tables_kernel,
        grid=((q + pad) // QB,),
        in_specs=[
            pl.BlockSpec((germs, QB), lambda i: (0, i)),
            whole((p, germs)),
            pl.BlockSpec((1, QB), lambda i: (0, i)),
        ],
        out_specs=[
            pl.BlockSpec((QB, 3 * p), lambda i: (i, 0)),
            pl.BlockSpec((2 * p, QB), lambda i: (0, i)),
            pl.BlockSpec((QB, 3 * SLOT), lambda i: (i, 0)),
            whole((p, 3 * p)),
        ],
        out_shape=[
            jax.ShapeDtypeStruct((q + pad, 3 * p), jnp.bfloat16),
            jax.ShapeDtypeStruct((2 * p, q + pad), jnp.bfloat16),
            jax.ShapeDtypeStruct((q + pad, 3 * SLOT), jnp.bfloat16),
            jax.ShapeDtypeStruct((p, 3 * p), jnp.bfloat16),
        ],
        scratch_shapes=[pltpu.VMEM((p, p), jnp.float32)],
        compiler_params=pltpu.CompilerParams(vmem_limit_bytes=20 << 20),
        name="node_tables",
    )(index, mode_index, weights)


def whole(shape):
    return pl.BlockSpec(shape, lambda *_: (0,) * len(shape))


def rim_kernel(rows, u_ref, log_ref, first_ref, last_ref, near_ref):
    start = 0
    for ref in (u_ref, log_ref):
        n = ref.shape[0] // rows
        span = slice(start, start + n)
        lane = lax.broadcasted_iota(jnp.int32, (n, LANES), 1)
        near = jnp.zeros((n, LANES), jnp.float32)
        for y in range(rows):
            here = ref[pl.ds(y, n, stride=rows), :]
            if y == 0:
                first_ref[span] = here
            if y == rows - 1:
                last_ref[span] = here
            near = jnp.where(lane == y, here[:, 0:1], near)
            near = jnp.where(lane == rows + y, here[:, LANES - 1 : LANES], near)
        near_ref[span] = near
        start += n


def rim_of(rows, field, logs):
    n = (field.shape[0] + logs.shape[0]) // rows
    return pl.pallas_call(
        functools.partial(rim_kernel, rows),
        out_shape=[jax.ShapeDtypeStruct((n, LANES), jnp.float32)] * 3,
        compiler_params=pltpu.CompilerParams(vmem_limit_bytes=20 << 20),
        name="rim_of",
    )(field, logs)


def put_cat(ref, lanes, x):
    p = x.shape[0]
    top, low = split(x)
    ref[0:p, lanes] = top
    ref[p : 2 * p, lanes] = low
    ref[2 * p : 3 * p, lanes] = top


def projected(w_ref, parts):
    p = w_ref.shape[0] // 2
    top, low = parts
    both = jnp.dot(w_ref[...], top, preferred_element_type=jnp.float32)
    rest = jnp.dot(w_ref[0:p, :], low, preferred_element_type=jnp.float32)
    return both[0:p] + both[p : 2 * p] + rest


def resistance(germ_ref, log):
    return jnp.exp2(jnp.dot(germ_ref[...], log, preferred_element_type=jnp.float32))


def inner_kernel(rows, u_ref, log_ref, basis_ref, germ_ref, w_ref, mass_ref, g_ref, u_cat_ref, du_ref, r_ref, f_ref):
    p = mass_ref.shape[0]
    cols = LANES
    lane = lax.broadcasted_iota(jnp.int32, (p, cols), 1)
    above = None
    for y in range(rows):
        here = u_ref[pl.ds(y, p, stride=rows), :]
        put_cat(u_cat_ref, pl.ds(y * cols, cols), here)
        ahead = pltpu.roll(here, cols - 1, axis=1)
        put_cat(du_ref, pl.ds(y * cols, cols), jnp.where(lane == cols - 1, 0.0, ahead - here))
        if y > 0:
            put_cat(du_ref, pl.ds((rows + y - 1) * cols, cols), here - above)
        above = here

    chunks = [("x", y, 2) for y in range(0, rows, 2)]
    chunks += [("y", y, min(2, rows - 1 - y)) for y in range(0, rows - 1, 2)]

    def lanes(chunk):
        kind, y, n = chunk
        return pl.ds((y if kind == "x" else rows + y) * cols, n * cols)

    def values(chunk):
        return jnp.dot(basis_ref[...], du_ref[:, lanes(chunk)], preferred_element_type=jnp.float32)

    def total(chunk):
        kind, y, n = chunk
        if kind == "y":
            return r_ref[:, pl.ds(y * cols, n * cols)] + r_ref[:, pl.ds((y + 1) * cols, n * cols)]
        sums = []
        for k in range(n):
            r = r_ref[:, pl.ds((y + k) * cols, cols)]
            sums.append(r + pltpu.roll(r, cols - 1, axis=1))
        return jnp.concatenate(sums, axis=1)

    def fill(y):
        span = pl.ds(y * cols, 2 * cols)
        r_ref[:, span] = resistance(germ_ref, log_ref[:, span])

    fill(0)
    value = values(chunks[0])
    waiting = None
    for i, chunk in enumerate(chunks):
        later = values(chunks[i + 1]) if i + 1 < len(chunks) else None
        if 2 * (i + 1) < rows:
            fill(2 * (i + 1))
        parts = split(value / total(chunk))
        if waiting is not None:
            f_ref[:, lanes(waiting[0])] = projected(w_ref, waiting[1])
        waiting = (chunk, parts)
        value = later
    stored = [
        jnp.dot(mass_ref[...], u_cat_ref[:, pl.ds(y * cols, 2 * cols)], preferred_element_type=jnp.float32)
        for y in range(0, rows, 2)
    ]
    f_ref[:, lanes(waiting[0])] = projected(w_ref, waiting[1])

    for y in range(rows):
        out = stored[y // 2][:, (y % 2) * cols : (y % 2 + 1) * cols]
        later = f_ref[:, pl.ds(y * cols, cols)]
        earlier = jnp.where(lane == 0, 0.0, pltpu.roll(later, 1, axis=1))
        later = jnp.where(lane == cols - 1, 0.0, later)
        out = out - (later - earlier)
        if y < rows - 1:
            out = out - f_ref[:, pl.ds((rows + y) * cols, cols)]
        if y > 0:
            out = out + f_ref[:, pl.ds((rows + y - 1) * cols, cols)]
        g_ref[y] = out


def inner_fluxes(rows, field, logs, basis_cat, weight_cat, germ_cat, mass_cat):
    p, cols = field.shape[0] // rows, field.shape[1]
    q = basis_cat.shape[0]
    faces = (2 * rows - 1) * cols
    return pl.pallas_call(
        functools.partial(inner_kernel, rows),
        out_shape=jax.ShapeDtypeStruct((rows, p, cols), jnp.float32),
        scratch_shapes=[
            pltpu.VMEM((3 * p, rows * cols), jnp.bfloat16),
            pltpu.VMEM((3 * p, faces), jnp.bfloat16),
            pltpu.VMEM((q, rows * cols), jnp.float32),
            pltpu.VMEM((p, faces), jnp.float32),
        ],
        compiler_params=pltpu.CompilerParams(vmem_limit_bytes=50 << 20),
        cost_estimate=pl.CostEstimate(
            flops=2 * q * faces * p * 6, bytes_accessed=8 << 20, transcendentals=q * rows * cols
        ),
        name="inner_fluxes",
    )(field, logs, basis_cat, germ_cat, weight_cat, mass_cat)


def outer_kernel(
    rows, open_ref, g_ref, first_ref, last_ref, near_ref, up_ref, down_ref,
    left_ref, right_ref, basis_ref, germ_ref, w_ref, out_ref, du_ref, le_ref, ll_ref,
):
    p = w_ref.shape[0] // 2
    q = basis_ref.shape[0]
    cols = LANES
    near = near_ref[...]
    left = pltpu.roll(left_ref[...], cols - rows, axis=1)
    right = pltpu.roll(right_ref[...], rows, axis=1)
    lane = lax.broadcasted_iota(jnp.int32, near.shape, 1)
    earlier = jnp.where(lane < rows, left, near)
    later = jnp.where(lane < rows, near, right)
    pairs = ((up_ref[...], first_ref[...]), (last_ref[...], down_ref[...]), (earlier, later))
    for k, (e, l) in enumerate(pairs):
        span = pl.ds(k * cols, cols)
        diff = l[0:p] - e[0:p]
        if k < 2:
            diff = diff * open_ref[k]
        else:
            low = lane[0:p] < rows
            diff = jnp.where(low, diff * open_ref[2], diff * open_ref[3])
            diff = jnp.where(lane[0:p] < 2 * rows, diff, 0.0)
        put_cat(du_ref, span, diff)
        put_cat(le_ref, span, e[p : p + SLOT])
        put_cat(ll_ref, span, l[p : p + SLOT])

    def values(i):
        return jnp.dot(
            basis_ref[pl.ds(i * PIECE, PIECE), :], du_ref[...], preferred_element_type=jnp.float32
        )

    def total(i):
        germ = germ_ref[pl.ds(i * PIECE, PIECE), :]
        e = jnp.exp2(jnp.dot(germ, le_ref[...], preferred_element_type=jnp.float32))
        return e + jnp.exp2(jnp.dot(germ, ll_ref[...], preferred_element_type=jnp.float32))

    def project(i, parts):
        top, low = parts
        at = pl.ds(i * PIECE, PIECE)
        both = jnp.dot(w_ref[:, at], top, preferred_element_type=jnp.float32)
        rest = jnp.dot(w_ref[0:p, at], low, preferred_element_type=jnp.float32)
        return both[0:p] + both[p : 2 * p] + rest

    steps = q // PIECE
    value, sums = values(0), total(0)
    flux, waiting = None, None
    for i in range(steps):
        later = (values(i + 1), total(i + 1)) if i + 1 < steps else (None, None)
        parts = split(value / sums)
        if waiting is not None:
            term = project(*waiting)
            flux = term if flux is None else flux + term
        waiting = (i, parts)
        value, sums = later
    flux = flux + project(*waiting)

    lane = lax.broadcasted_iota(jnp.int32, (p, cols), 1)
    for y in range(rows):
        out = g_ref[y]
        if y == 0:
            out = out + flux[:, 0:cols]
        if y == rows - 1:
            out = out - flux[:, cols : 2 * cols]
        out = out + jnp.where(lane == 0, flux[:, 2 * cols + y : 2 * cols + y + 1], 0.0)
        at = 2 * cols + rows + y
        out = out - jnp.where(lane == cols - 1, flux[:, at : at + 1], 0.0)
        out_ref[pl.ds(y, p, stride=rows), :] = out


def outer_fluxes(rows, opened, inner, rims, halos, basis_cat, weight_cat, germ_cat):
    p, cols = inner.shape[1:]
    q = basis_cat.shape[0]
    vmem = pl.BlockSpec(memory_space=pltpu.VMEM)
    return pl.pallas_call(
        functools.partial(outer_kernel, rows),
        in_specs=[pl.BlockSpec(memory_space=pltpu.SMEM)] + [vmem] * 11,
        out_shape=jax.ShapeDtypeStruct((p * rows, cols), jnp.float32),
        scratch_shapes=[
            pltpu.VMEM((3 * p, 3 * cols), jnp.bfloat16),
            pltpu.VMEM((3 * SLOT, 3 * cols), jnp.bfloat16),
            pltpu.VMEM((3 * SLOT, 3 * cols), jnp.bfloat16),
        ],
        compiler_params=pltpu.CompilerParams(vmem_limit_bytes=50 << 20),
        cost_estimate=pl.CostEstimate(
            flops=2 * q * 3 * cols * p * 6, bytes_accessed=8 << 20, transcendentals=q * 6 * cols
        ),
        name="outer_fluxes",
    )(opened, inner, *rims, *halos, basis_cat, germ_cat, weight_cat)


def local_kernel(
    nsa, place_ref, part_ref, s0_ref, s1_ref, s2_ref, s3_ref, cy_ref, cxt_ref, ends_of_ref,
    recip_ref, coef_ref, scaled_ref, jump_ref, res_ref,
):
    modes, length, cols = s0_ref.shape
    rows = part_ref.shape[2]
    ngy = 4
    ny = ngy * length
    for d, src_ref in enumerate((s0_ref, s1_ref, s2_ref, s3_ref)):
        g = lax.rem(place_ref[0] + ngy - d, ngy)
        for s, block in enumerate(row_order(nsa)):
            span = pl.ds(pl.multiple_of(g * length + block * rows, 8), rows)
            for m in range(modes):
                res_ref[span, pl.ds(m * cols, cols)] = (
                    src_ref[m, pl.ds(block * rows, rows), :] - part_ref[s * ngy + g, m]
                )
    spectral = jnp.dot(cy_ref[...], res_ref[...], precision=HIGHEST, preferred_element_type=jnp.float32)
    spectral = jnp.concatenate([spectral[:, m * cols : (m + 1) * cols] for m in range(modes)], axis=0)
    spectral = jnp.dot(spectral, cxt_ref[...], precision=HIGHEST, preferred_element_type=jnp.float32)
    recip = recip_ref[...]
    scaled = jnp.concatenate(
        [recip * spectral[m * ny : (m + 1) * ny] for m in range(modes)], axis=0
    )
    both = lax.dot_general(
        ends_of_ref[...], scaled, (((1,), (1,)), ((), ())),
        precision=HIGHEST, preferred_element_type=jnp.float32,
    )
    pad = [jnp.zeros((8 - modes, ny), jnp.float32)]
    first = jnp.concatenate([both[0:1, m * ny : (m + 1) * ny] for m in range(modes)] + pad, axis=0)
    last = jnp.concatenate([both[1:2, m * ny : (m + 1) * ny] for m in range(modes)] + pad, axis=0)
    blocks = jump_ref.shape[0]
    for i in range(blocks + 1):
        term = coef_ref[0, i : i + 1, :] * first + coef_ref[1, i : i + 1, :] * last
        if i < blocks:
            jump_ref[i, 0:8, :] = term
        if i > 0:
            jump_ref[i - 1, 8:16, :] = term
    scaled_ref[...] = scaled


def dot_in_halves(a, b):
    a, b = split(a), split(b)
    out = jnp.dot(a[0], b[0], preferred_element_type=jnp.float32)
    out = out + jnp.dot(a[1], b[0], preferred_element_type=jnp.float32)
    return out + jnp.dot(a[0], b[1], preferred_element_type=jnp.float32)


def back_kernel(place_ref, scaled_ref, cx_ref, cyt_ref, p0_ref, p1_ref, p2_ref, p3_ref, rows_ref):
    modes, length, cols = p0_ref.shape
    ny = cyt_ref.shape[0]
    ngy = ny // length
    z = dot_in_halves(scaled_ref[...], cx_ref[...])
    z = jnp.concatenate([z[m * ny : (m + 1) * ny] for m in range(modes)], axis=1)
    rows_ref[...] = dot_in_halves(cyt_ref[...], z)
    for d, out_ref in enumerate((p0_ref, p1_ref, p2_ref, p3_ref)):
        g = lax.rem(place_ref[0] + d, ngy)
        span = pl.ds(pl.multiple_of(g * length, 8), length)
        for m in range(modes):
            out_ref[m] = rows_ref[span, pl.ds(m * cols, cols)]


def final_kernel(
    place_ref, p0_ref, p1_ref, p2_ref, p3_ref, t0_ref, t1_ref, t2_ref, t3_ref, g_first_ref, g_last_ref,
    cyt_ref, now_hbm, before_hbm, fresh_ref, update_ref, now_ref, before_ref, sems,
):
    modes, length, cols = p0_ref.shape
    ngy = fresh_ref.shape[0] // modes
    copies = [
        pltpu.make_async_copy(now_hbm, now_ref, sems.at[0]),
        pltpu.make_async_copy(before_hbm, before_ref, sems.at[1]),
    ]
    for copy in copies:
        copy.start()
    place = place_ref[0]
    back = cyt_ref[pl.ds(pl.multiple_of(place * length, 8), length), :]
    right = split(jnp.concatenate([g_first_ref[...], -g_last_ref[...]], axis=0))
    left = []
    for t_ref in (t0_ref, t1_ref, t2_ref, t3_ref):
        for m in range(modes):
            left.append(
                jnp.concatenate([back * t_ref[m : m + 1, :], back * t_ref[8 + m : 9 + m, :]], axis=1)
            )
    left = split(jnp.concatenate(left, axis=0))
    jump = jnp.dot(left[0], right[0], preferred_element_type=jnp.float32)
    jump = jump + jnp.dot(left[1], right[0], preferred_element_type=jnp.float32)
    jump = jump + jnp.dot(left[0], right[1], preferred_element_type=jnp.float32)
    for copy in copies:
        copy.wait()
    for d, p_ref in enumerate((p0_ref, p1_ref, p2_ref, p3_ref)):
        g = lax.rem(place + ngy - d, ngy)
        for m in range(modes):
            at = (d * modes + m) * length
            update = p_ref[m] + jump[at : at + length]
            mode = g * modes + m
            before = before_ref[mode]
            fresh_ref[mode] = before + relax_weight * (now_ref[mode] - before + step_length * update)
            update_ref[mode] = update


def solve_tables(mean_perm, ny, cols, blocks, position):
    cx = cosine_matrix(cols)
    lam_y = jnp.asarray(eigen_values(ny, ny), jnp.float32)
    lam_x = jnp.asarray(eigen_values(cols, cols), jnp.float32)
    recip = 1.0 / (storage_rate + mean_perm * (lam_y[:, None] + lam_x[None, :]))
    first = jnp.asarray(cx[:, 0][:, None] * cx, jnp.float32)
    last = jnp.asarray(cx[:, -1][:, None] * cx, jnp.float32)
    g_first = jnp.dot(recip, first, precision=HIGHEST)
    g_last = jnp.dot(recip, last, precision=HIGHEST)
    k = np.arange(1, blocks)
    sine = math.sqrt(2.0 / blocks) * np.sin(np.pi * np.outer(np.arange(0, blocks + 1), k) / blocks)
    sine[0] = 0.0
    sine[blocks] = 0.0
    theta = jnp.asarray(2.0 * np.cos(np.pi * k / blocks), jnp.float32)
    spread = 1.0 / (
        1.0 / mean_perm + g_first[:, 0:1] + g_last[:, cols - 1 : cols] - g_first[:, cols - 1 : cols] * theta
    )
    table = jnp.asarray(sine, jnp.float32)
    coef = []
    for end, sign in ((0, -1.0), (1, 1.0)):
        mine = sign * lax.dynamic_slice_in_dim(table, position + end, 1, axis=0)
        coef.append(jnp.einsum("ik,jk->ij", table, spread * mine, precision=HIGHEST))
    return recip, g_first, g_last, jnp.stack(coef)


def row_order(count):
    half = count // 2
    return list(range(half)) + list(range(count - 1, half - 1, -1))


def rotated(x, axis, by):
    count = lax.axis_size(axis)
    return lax.ppermute(x, axis, [(i, (i + by) % count) for i in range(count)])


def pairs(chain, shift):
    chain = list(chain)
    found = [(d, d) for d in chain[:shift]]
    for k in range(shift, len(chain), 2):
        two = chain[k : k + 2]
        found += list(zip(two, two[::-1]))
    return found


def dealt_kernel(order, x_ref, out_ref):
    rows = out_ref.shape[2]
    for k, block in enumerate(order):
        out_ref[k] = x_ref[:, block * rows : (block + 1) * rows, :]


def dealt(x, order):
    modes, length, cols = x.shape
    return pl.pallas_call(
        functools.partial(dealt_kernel, order),
        out_shape=jax.ShapeDtypeStruct((len(order), modes, length // len(order), cols), x.dtype),
        name="dealt",
    )(x)


def on_device(
    field_now, field_before, source, log_fields, weights, mean_perm, node_index, mode_index
):
    nsa, ngy, ngx = (lax.axis_size(a) for a in ("sa", "gy", "gx"))
    modes, length, cols = field_now.shape
    rows = length // nsa
    p = modes * nsa
    ny = length * ngy
    sub = modes // ngy
    fields = log_fields.shape[0]

    order = row_order(nsa)
    outgoing = dealt(field_now, order)
    field = lax.all_to_all(outgoing, "sa", 0, 0, tiled=True).reshape(p * rows, cols)

    place = lax.axis_index("gy")
    blocks = source.reshape(ngy, sub, length, cols)
    pieces = [lax.dynamic_index_in_dim(blocks, (place + d) % ngy, 0, keepdims=False) for d in range(ngy)]
    pieces = pieces[:1] + [rotated(pieces[d], "gy", d) for d in range(1, ngy)]

    basis_cat, weight_cat, germ_cat, mass_cat = node_tables(node_index, mode_index, weights)
    recip, g_first, g_last, coef = solve_tables(mean_perm, ny, cols, ngx, lax.axis_index("gx"))

    row_axis = ("gy", "sa")
    member = lax.axis_index("sa")
    row_index = place * nsa + jnp.where(member < nsa // 2, member, nsa - 1 - (member - nsa // 2))
    log_fields = lax.ppermute(
        log_fields, row_axis, [(g * nsa + order[i], g * nsa + i) for g in range(ngy) for i in range(nsa)]
    )
    chain = [g * nsa + order.index(k) for g in range(ngy) for k in range(nsa)]
    col_index = lax.axis_index("gx")
    opened = jnp.stack(
        [row_index > 0, row_index < ngy * nsa - 1, col_index > 0, col_index < ngx - 1]
    ).astype(jnp.float32)
    scaled_logs = jnp.pad(
        log_fields * jnp.float32(-math.log2(math.e)), ((0, SLOT - fields), (0, 0), (0, 0))
    )
    top, low = halves(scaled_logs.reshape(SLOT, rows * cols))
    logs = jnp.concatenate([top, low, top], axis=0)

    field, *pieces = lax.optimization_barrier((field, *pieces))
    rims = rim_of(rows, field, scaled_logs.reshape(SLOT * rows, cols))
    first, last, near = rims
    even_row, even_col = row_index % 2 == 0, col_index % 2 == 0
    sent = jnp.where(even_row, last, first), jnp.where(even_row, first, last)
    rows_got = [lax.ppermute(x, row_axis, pairs(chain, k)) for k, x in enumerate(sent)]
    cols_got = [lax.ppermute(near, "gx", pairs(range(ngx), k)) for k in range(2)]
    halos = (
        jnp.where(even_row, rows_got[1], rows_got[0]),
        jnp.where(even_row, rows_got[0], rows_got[1]),
        jnp.where(even_col, cols_got[1], cols_got[0]),
        jnp.where(even_col, cols_got[0], cols_got[1]),
    )
    inner = inner_fluxes(rows, field, logs, basis_cat, weight_cat, germ_cat, mass_cat)
    galerkin = outer_fluxes(rows, opened, inner, rims, halos, basis_cat, weight_cat, germ_cat)
    part = lax.all_to_all(
        galerkin.reshape(nsa * ngy, sub, rows, cols), ("sa", "gy"), 0, 0, tiled=True
    )

    cy = cosine_matrix(ny)
    cx = cosine_matrix(cols)
    ends_of = np.zeros((8, cols))
    ends_of[0], ends_of[1] = cx[:, 0], cx[:, -1]
    f32 = functools.partial(jnp.asarray, dtype=jnp.float32)
    params = pltpu.CompilerParams(vmem_limit_bytes=40 << 20)
    vmem = pl.BlockSpec(memory_space=pltpu.VMEM)
    scaled, jumps = pl.pallas_call(
        functools.partial(local_kernel, nsa),
        in_specs=[pl.BlockSpec(memory_space=pltpu.SMEM)] + [vmem] * 10,
        out_shape=(
            jax.ShapeDtypeStruct((sub * ny, cols), jnp.float32),
            jax.ShapeDtypeStruct((ngx, 16, ny), jnp.float32),
        ),
        scratch_shapes=[pltpu.VMEM((ny, sub * cols), jnp.float32)],
        compiler_params=params,
        name="local_solve",
    )(place[None], part, *pieces, f32(cy), f32(cx.T), f32(ends_of), recip, coef)
    jumps = lax.all_to_all(jumps, "gx", 0, 0, tiled=True)
    smem = pl.BlockSpec(memory_space=pltpu.SMEM)
    hbm = pl.BlockSpec(memory_space=pl.ANY)
    sent = pl.pallas_call(
        back_kernel,
        in_specs=[smem] + [vmem] * 3,
        out_shape=[jax.ShapeDtypeStruct((sub, length, cols), jnp.float32)] * 4,
        scratch_shapes=[pltpu.VMEM((ny, sub * cols), jnp.float32)],
        compiler_params=params,
        cost_estimate=pl.CostEstimate(
            flops=36 * sub * ny * cols * cols, bytes_accessed=2 << 20, transcendentals=0
        ),
        name="back",
    )(place[None], scaled, f32(cx), f32(cy.T))
    got = [sent[0]] + [rotated(sent[d], "gy", d) for d in range(1, ngy)]
    total = jnp.sum(jumps, axis=0)
    totals = [total] + [rotated(total, "gy", d) for d in range(1, ngy)]
    block = jax.ShapeDtypeStruct(field_now.shape, jnp.float32)
    fresh, update = pl.pallas_call(
        final_kernel,
        in_specs=[smem] + [vmem] * 11 + [hbm] * 2,
        out_shape=[block] * 2,
        scratch_shapes=[
            pltpu.VMEM(field_now.shape, jnp.float32),
            pltpu.VMEM(field_now.shape, jnp.float32),
            pltpu.SemaphoreType.DMA((2,)),
        ],
        compiler_params=params,
        name="final",
    )(place[None], *got, *totals, g_first, g_last, f32(cy.T), field_now, field_before)
    return (fresh, update)


def solution(mesh):
    block = P("sa", "gy", "gx")
    in_specs = (block, block, block, P(None, ("gy", "sa"), "gx"), P(), P(), P(), P())
    return jax.shard_map(
        on_device, mesh=mesh, in_specs=in_specs, out_specs=(block, block), check_vma=False
    )
```
